32 devices in a mesh: height: 2 (over y), chan: 4 (over x, core), batch: 4 (over z).
Axes of the slice: x: 2, y: 2, z: 4, core: 2. Of those that a mesh axis runs over, the one named last changes fastest.
Arguments:
- block_input: bfloat16 [64, 16, 16, 2048], P('batch', 'height', None, 'chan'), may hold values from -6 to 6
- w_reduce: bfloat16 [2048, 1024], P(None, 'chan'), may hold values from -0.125 to 0.125
- w_group: bfloat16 [3, 3, 32, 1024], P(None, None, None, 'chan'), may hold values from -0.375 to 0.375
- w_expand: bfloat16 [1024, 2048], P('chan'), may hold values from -0.1875 to 0.1875
- gain_one: bfloat16 [1024], P('chan'), may hold values from 0.5 to 1.5
- bias_one: bfloat16 [1024], P('chan'), may hold values from -3 to 3
- gain_two: bfloat16 [1024], P('chan'), may hold values from 0.5 to 1.5
- bias_two: bfloat16 [1024], P('chan'), may hold values from -3 to 3
- gain_three: bfloat16 [2048], P('chan'), may hold values from 0.5 to 1.5
- bias_three: bfloat16 [2048], P('chan'), may hold values from -3 to 3
- image_counts: int32 [4], replicated, may hold values from 1 to 16, as said below
- grad_output: bfloat16 [64, 16, 16, 2048], P('batch', 'height', None, 'chan'), may hold values from -6 to 6
Outputs:
- output: bfloat16 [64, 16, 16, 2048], P('batch', 'height', None, 'chan')
- grad_input: bfloat16 [64, 16, 16, 2048], P('batch', 'height', None, 'chan')
- grad_reduce: float32 [2048, 1024], P(None, 'chan')
- grad_group: float32 [3, 3, 32, 1024], P(None, None, None, 'chan')
- grad_expand: float32 [1024, 2048], P('chan')
- grad_gain_one: float32 [1024], P('chan')
- grad_bias_one: float32 [1024], P('chan')
- grad_gain_two: float32 [1024], P('chan')
- grad_bias_two: float32 [1024], P('chan')
- grad_gain_three: float32 [2048], P('chan')
- grad_bias_three: float32 [2048], P('chan')
The draws below stay inside these ranges and needn't reach their ends.
Inputs may be any that keep to these rules, and one draw needn't show every extreme that they name: image_counts[s] real images fill the first slots of batch shard s of 16 slots; the other slots are padding; some shard is full.
All inputs are finite; a program needn't handle non-finite values.
Results may differ from the reference program's by a relative error of at most 0.018.
Values may be sent and summed in bfloat16 or wider, within the bound.
No kernel may reach another device: no remote copies, remote signals or barrier semaphores. Data moves between devices by JAX's collectives and lax.ppermute only.
A program may use at most 192 MiB of HBM per device.

```python
import jax
import jax.numpy as jnp
from jax import lax

CHANNELS = 2048
GROUPS = 32
GROUP_WIDTH = 32
MID = 1024
IMG_H = 16
IMG_W = 16
IMG_CAP = 16
SHARDS = 4
IMAGES = 64


def draw_image_counts(key, part):
    drop_key, split_key, full_key = jax.random.split(key, 3)
    dropped = jax.random.randint(drop_key, (SHARDS,), 0, IMG_CAP)
    divisor = jax.random.randint(split_key, (SHARDS,), 1, 3)
    counted = jnp.maximum(IMG_CAP - dropped // divisor, 1)
    fullest = jax.random.randint(full_key, (), 0, SHARDS)
    return jnp.where(jnp.arange(SHARDS) == fullest, IMG_CAP, counted).astype(jnp.int32)


def level_of(stream_key, dims, pieces, least, high):
    level, own = 1.0, jax.random.fold_in(stream_key, 6)
    for position, parts in pieces:
        heights = jnp.exp(jax.random.uniform(jax.random.fold_in(own, position), (parts,), jnp.float32, least / len(pieces), high / len(pieces)))
        level = level * jnp.repeat(heights, dims[position] // parts).reshape([-1 if axis == position else 1 for axis in range(len(dims))])
    return level


def normal_values(own_key, extent, spread, limit, cuts=(), kind=jnp.bfloat16):
    values = jax.random.normal(own_key, extent, jnp.float32) * spread
    if len(cuts) > 0:
        values = level_of(own_key, extent, cuts, -0.22, 0.18) * values
    return jnp.clip(values, min=-limit, max=limit).astype(kind)


def setup_inputs(seed: int = 0) -> dict:
    keys = jax.random.split(jax.random.key(seed), 13)
    block_input = normal_values(keys[0], (IMAGES, IMG_H, IMG_W, CHANNELS), 1.0, 6.0, ((0, 4), (1, 2), (3, 4)))
    w_reduce = normal_values(keys[1], (CHANNELS, MID), CHANNELS ** -0.5, 0.125, ((1, 4),))
    w_group = normal_values(keys[2], (3, 3, GROUP_WIDTH, MID), (9 * GROUP_WIDTH) ** -0.5, 0.375, ((3, 4),))
    w_expand = normal_values(keys[3], (MID, CHANNELS), MID ** -0.5, 0.1875, ((0, 4),))
    gain_one = jnp.clip(1.0 + 0.1 * jax.random.normal(keys[4], (MID,), jnp.float32), 0.5, 1.5).astype(jnp.bfloat16)
    bias_one = normal_values(keys[5], (MID,), 0.5, 3.0, ((0, 4),))
    gain_two = jnp.clip(1.0 + 0.1 * jax.random.normal(keys[6], (MID,), jnp.float32), 0.5, 1.5).astype(jnp.bfloat16)
    bias_two = normal_values(keys[7], (MID,), 0.5, 3.0, ((0, 4),))
    gain_three = jnp.clip(1.0 + 0.1 * jax.random.normal(keys[8], (CHANNELS,), jnp.float32), 0.5, 1.5).astype(jnp.bfloat16)
    bias_three = normal_values(keys[9], (CHANNELS,), 0.5, 3.0, ((0, 4),))
    image_counts = draw_image_counts(jax.random.fold_in(keys[12], 71), 0)
    grad_output = normal_values(keys[11], (IMAGES, IMG_H, IMG_W, CHANNELS), 1.0, 6.0, ((0, 4), (1, 2), (3, 4)))
    return dict(block_input=block_input, w_reduce=w_reduce, w_group=w_group, w_expand=w_expand, gain_one=gain_one, bias_one=bias_one, gain_two=gain_two, bias_two=bias_two, gain_three=gain_three, bias_three=bias_three, image_counts=image_counts, grad_output=grad_output)


EPSILON = 1e-05

@jax.custom_vjp
def low(v):
    return lax.optimization_barrier(v.astype(jnp.bfloat16)).astype(jnp.float32)

@jax.custom_vjp
def low_back(v):
    return v

def low_keep(v):
    return (low(v), None)

def low_pass(kept, grad):
    return (grad,)

def back_keep(v):
    return (v, None)

def back_low(kept, grad):
    return (low(grad),)
low.defvjp(low_keep, low_pass)
low_back.defvjp(back_keep, back_low)

def image_mask(image_counts):
    per_image = jnp.repeat(image_counts, IMG_CAP, total_repeat_length=IMAGES)
    return (jnp.arange(IMAGES) % IMG_CAP < per_image).astype(jnp.float32)

def batch_norm(values, gain_vec, bias_vec, image_weight, valid_total):
    first_sum = lax.optimization_barrier(jnp.sum(image_weight * values, axis=(0, 1, 2)))
    second_sum = lax.optimization_barrier(jnp.sum(image_weight * values * values, axis=(0, 1, 2)))
    average = first_sum / valid_total
    inv_std = lax.rsqrt(second_sum / valid_total - average * average + EPSILON)
    return (values - average) * inv_std * gain_vec + bias_vec

def forward(block_input, w_reduce, w_group, w_expand, gain_one, bias_one, gain_two, bias_two, gain_three, bias_three, image_weight, valid_total):
    highest = lax.Precision.HIGHEST
    reduced = low_back(jnp.einsum('bhwc,cd->bhwd', block_input, w_reduce, precision=highest))
    act_one = low(image_weight * jax.nn.silu(batch_norm(reduced, gain_one, bias_one, image_weight, valid_total)))
    grouped = low_back(lax.conv_general_dilated(act_one, w_group, (1, 1), ((1, 1), (1, 1)), dimension_numbers=('NHWC', 'HWIO', 'NHWC'), feature_group_count=GROUPS, precision=highest))
    act_two = low(image_weight * jax.nn.silu(batch_norm(grouped, gain_two, bias_two, image_weight, valid_total)))
    expanded = low_back(jnp.einsum('bhwd,dc->bhwc', act_two, w_expand, precision=highest))
    summed = batch_norm(expanded, gain_three, bias_three, image_weight, valid_total) + block_input
    return image_weight * jax.nn.silu(summed)

def reference(block_input, w_reduce, w_group, w_expand, gain_one, bias_one, gain_two, bias_two, gain_three, bias_three, image_counts, grad_output):
    mask = image_mask(image_counts)
    image_weight = mask[:, None, None, None]
    valid_total = jnp.sum(mask) * (IMG_H * IMG_W)
    primals = tuple((array.astype(jnp.float32) for array in (block_input, w_reduce, w_group, w_expand, gain_one, bias_one, gain_two, bias_two, gain_three, bias_three)))

    def run_block(*arrays):
        return forward(*arrays, image_weight, valid_total)
    output, pullback = jax.vjp(run_block, *primals)
    grads = pullback(grad_output.astype(jnp.float32))
    return (output.astype(jnp.bfloat16), grads[0].astype(jnp.bfloat16), grads[1], grads[2], grads[3], grads[4], grads[5], grads[6], grads[7], grads[8], grads[9])
```

```python
import functools

import jax
import jax.numpy as jnp
from jax import lax
from jax.experimental import pallas as pl
from jax.experimental.pallas import tpu as pltpu
from jax.sharding import PartitionSpec as P

EPSILON = 1e-05
F32, BF16 = jnp.float32, jnp.bfloat16
REDUCE_AXES = ("height", "batch")
STEP_IMAGES = 4


def dot(a, b, contract):
    return lax.dot_general(a, b, (contract, ((), ())), preferred_element_type=F32)


def swap(value, distance):
    count = lax.axis_size("chan")
    return lax.ppermute(value, "chan", [(i, i ^ distance) for i in range(count)])


def gather_pieces(value):
    count = lax.axis_size("chan")
    pieces = [None] * count
    pieces[0] = value
    pieces[1] = swap(value, 1)
    for k in range(2, count, 2):
        pieces[k] = swap(value, k)
    for k in range(2, count, 2):
        pieces[k + 1] = swap(pieces[k], 1)
    return pieces


def scatter_pieces(parts):
    count = len(parts)
    low = [swap(parts[k + 1].astype(BF16), 1) for k in range(0, count, 2)]
    sums = [parts[k] + low[k // 2].astype(F32) for k in range(0, count, 2)]
    total = sums[0]
    arrived = [swap(sums[k // 2].astype(BF16), k) for k in range(2, count, 2)]
    for value in arrived:
        total = total + value.astype(F32)
    return total


def total_sums(*vectors):
    stacked = jnp.stack(vectors)
    count = lax.axis_size(REDUCE_AXES)
    sent = jnp.broadcast_to(stacked[None], (count,) + stacked.shape)
    return jnp.sum(lax.all_to_all(sent, REDUCE_AXES, 0, 0), 0)


def smooth_slope(values):
    logistic = jax.nn.sigmoid(values)
    return logistic * (1.0 + values * (1.0 - logistic))


def edge_rows(field):
    count = lax.axis_size("height")
    first, last = field[:, 0], field[:, -1]
    if count == 2:
        mine = jnp.where(lax.axis_index("height") == 0, last, first)
        other = lax.ppermute(mine, "height", [(0, 1), (1, 0)])
        return other, other
    above = lax.ppermute(last, "height", [(i, i + 1) for i in range(count - 1)])
    below = lax.ppermute(first, "height", [(i + 1, i) for i in range(count - 1)])
    return above, below


def fold_rows(values):
    rows, chans = values.shape
    return jnp.sum(values.reshape(rows // 8, 8, chans), 0)


def shifted(value, cols):
    rows = value.shape[0]
    place = lax.broadcasted_iota(jnp.int32, value.shape, 0) % cols
    left = jnp.where(place == 0, 0.0, pltpu.roll(value, 1, 0))
    right = jnp.where(place == cols - 1, 0.0, pltpu.roll(value, rows - 1, 0))
    return left, right


def fill_windows(window_ref, slot, value, cols):
    left, right = shifted(value, cols)
    window_ref[0, slot] = left.astype(BF16)
    window_ref[1, slot] = value.astype(BF16)
    window_ref[2, slot] = right.astype(BF16)


def conv_forward_kernel(
    images, rows, cols, flags_ref, red_ref, above_ref, below_ref, vec_ref, mat_ref,
    act_ref, out_ref, sums_ref, window_ref,
):
    step = pl.program_id(0)
    count = flags_ref[0]
    average, scale, bias = vec_ref[0:1, :], vec_ref[1:2, :], vec_ref[2:3, :]
    pixels = rows * cols
    chans = red_ref.shape[2]

    def activate(v, keep):
        pre = (v - average) * scale + bias
        return jnp.where(keep, pre / (1.0 + jnp.exp(-pre)), 0.0)

    for image in range(images):
        real = step * images + image < count
        own = activate(red_ref[image], real)
        above = activate(above_ref[image], jnp.logical_and(real, flags_ref[1] > 0))
        below = activate(below_ref[image], jnp.logical_and(real, flags_ref[2] > 0))
        act_ref[image] = own.astype(BF16)
        fill_windows(window_ref, image, jnp.concatenate([above, own, below], 0), cols)
    total = jnp.zeros((images * pixels, chans), F32)
    for i in range(3):
        for j in range(3):
            piece = window_ref[j, :, i * cols : i * cols + pixels, :].reshape(images * pixels, chans)
            total = total + dot(piece, mat_ref[3 * i + j], ((1,), (0,)))
    out_ref[...] = total.reshape(images, pixels, chans)

    @pl.when(step == 0)
    def _():
        sums_ref[...] = jnp.zeros_like(sums_ref)

    sums_ref[0] += fold_rows(total)
    sums_ref[1] += fold_rows(total * total)


def conv_forward(reduced, above, below, vectors, matrices, flags, rows, cols):
    image_count, pixels, chans = reduced.shape
    images = STEP_IMAGES
    block = lambda shape: pl.BlockSpec((images,) + shape, lambda s: (s, 0, 0))
    whole = lambda shape: pl.BlockSpec(shape, lambda s: (0,) * len(shape))
    return pl.pallas_call(
        functools.partial(conv_forward_kernel, images, rows, cols),
        grid=(image_count // images,),
        in_specs=[
            pl.BlockSpec(memory_space=pltpu.SMEM),
            block((pixels, chans)),
            block((cols, chans)),
            block((cols, chans)),
            whole((8, chans)),
            whole((9, chans, chans)),
        ],
        out_specs=[block((pixels, chans)), block((pixels, chans)), whole((2, 8, chans))],
        out_shape=[
            jax.ShapeDtypeStruct((image_count, pixels, chans), BF16),
            jax.ShapeDtypeStruct((image_count, pixels, chans), F32),
            jax.ShapeDtypeStruct((2, 8, chans), F32),
        ],
        scratch_shapes=[pltpu.VMEM((3, images, pixels + 2 * cols, chans), BF16)],
        compiler_params=pltpu.CompilerParams(
            dimension_semantics=("arbitrary",), vmem_limit_bytes=40 << 20
        ),
        cost_estimate=pl.CostEstimate(
            flops=18 * image_count * pixels * chans * chans,
            bytes_accessed=image_count * pixels * chans * 10,
            transcendentals=image_count * pixels * chans,
        ),
        name="conv_forward",
    )(flags, reduced, above, below, vectors, matrices)


def conv_backward_kernel(
    images, rows, cols, group, flags_ref, d_ref, d_above_ref, d_below_ref, grp_ref, g_above_ref, g_below_ref,
    red_ref, act_ref, vec_ref, mat_ref, out_ref, sums_ref, kernel_ref, window_ref, total_ref,
):
    step = pl.program_id(0)
    count = flags_ref[0]
    pixels = rows * cols
    chans = d_ref.shape[2]
    avg_two, inv_two, scale_two = vec_ref[0:1, :], vec_ref[1:2, :], vec_ref[2:3, :]
    bias_part, gain_part = vec_ref[3:4, :], vec_ref[4:5, :]
    avg_one, inv_one, gain_one, bias_one = (
        vec_ref[5:6, :], vec_ref[6:7, :], vec_ref[7:8, :], vec_ref[8:9, :],
    )

    def input_grad(d, grouped, keep):
        normalized = (grouped - avg_two) * inv_two
        return jnp.where(keep, scale_two * (d - (bias_part + normalized * gain_part)), 0.0)

    @pl.when(step == 0)
    def _():
        sums_ref[...] = jnp.zeros_like(sums_ref)
        total_ref[...] = jnp.zeros_like(total_ref)

    for image in range(images):
        real = step * images + image < count
        own = input_grad(d_ref[image], grp_ref[image], real)
        above = input_grad(d_above_ref[image], g_above_ref[image], jnp.logical_and(real, flags_ref[1] > 0))
        below = input_grad(d_below_ref[image], g_below_ref[image], jnp.logical_and(real, flags_ref[2] > 0))
        fill_windows(window_ref, image, jnp.concatenate([above, own, below], 0), cols)
    grad = jnp.zeros((images * pixels, chans), F32)
    acts = act_ref[...].reshape(images * pixels, chans)
    for i in range(3):
        for j in range(3):
            piece = window_ref[2 - j, :, (2 - i) * cols : (2 - i) * cols + pixels, :].reshape(images * pixels, chans)
            grad = grad + dot(piece, mat_ref[3 * i + j], ((1,), (0,)))
            total_ref[3 * i + j] += dot(acts, piece, ((0,), (0,)))
    for image in range(images):
        real = step * images + image < count
        normalized = (red_ref[image] - avg_one) * inv_one
        pre = normalized * gain_one + bias_one
        logistic = 1.0 / (1.0 + jnp.exp(-pre))
        slope = logistic * (1.0 + pre * (1.0 - logistic))
        d_one = jnp.where(real, grad[image * pixels : (image + 1) * pixels] * slope, 0.0)
        out_ref[image] = d_one
        sums_ref[0] += fold_rows(d_one)
        sums_ref[1] += fold_rows(d_one * normalized)

    @pl.when(step == pl.num_programs(0) - 1)
    def _():
        row_group = lax.broadcasted_iota(jnp.int32, (chans, chans), 0) // group
        col_group = lax.broadcasted_iota(jnp.int32, (chans, chans), 1) // group
        for tap in range(9):
            own = jnp.where(row_group == col_group, total_ref[tap], 0.0)
            kernel_ref[tap] = jnp.sum(own.reshape(chans // group, group, chans), 0)


def conv_backward(d_two, d_edges, grouped, g_edges, reduced, acts, vectors, matrices, flags, rows, cols, group):
    image_count, pixels, chans = reduced.shape
    images = STEP_IMAGES
    block = lambda shape: pl.BlockSpec((images,) + shape, lambda s: (s, 0, 0))
    whole = lambda shape: pl.BlockSpec(shape, lambda s: (0,) * len(shape))
    field, edge = block((pixels, chans)), block((cols, chans))
    return pl.pallas_call(
        functools.partial(conv_backward_kernel, images, rows, cols, group),
        grid=(image_count // images,),
        in_specs=[
            pl.BlockSpec(memory_space=pltpu.SMEM),
            field, edge, edge, field, edge, edge, field, field,
            whole((16, chans)),
            whole((9, chans, chans)),
        ],
        out_specs=[field, whole((2, 8, chans)), whole((9, group, chans))],
        out_shape=[
            jax.ShapeDtypeStruct((image_count, pixels, chans), F32),
            jax.ShapeDtypeStruct((2, 8, chans), F32),
            jax.ShapeDtypeStruct((9, group, chans), F32),
        ],
        scratch_shapes=[
            pltpu.VMEM((3, images, pixels + 2 * cols, chans), BF16),
            pltpu.VMEM((9, chans, chans), F32),
        ],
        compiler_params=pltpu.CompilerParams(
            dimension_semantics=("arbitrary",), vmem_limit_bytes=40 << 20
        ),
        cost_estimate=pl.CostEstimate(
            flops=36 * image_count * pixels * chans * chans,
            bytes_accessed=image_count * pixels * chans * 18,
            transcendentals=image_count * pixels * chans,
        ),
        name="conv_backward",
    )(flags, d_two, *d_edges, grouped, *g_edges, reduced, acts, vectors, matrices)


def norm_vectors(sums, valid_total):
    average = sums[0] / valid_total
    inv_std = lax.rsqrt(sums[1] / valid_total - average * average + EPSILON)
    return average, inv_std


def block_matrices(kernel):
    group, chans = kernel.shape[2], kernel.shape[3]
    taps = kernel.reshape(9, group, chans)
    same = jnp.arange(chans)[:, None] // group == jnp.arange(chans)[None, :] // group
    spread = jnp.where(same[None], jnp.tile(taps, (1, chans // group, 1)), jnp.zeros((), kernel.dtype))
    return spread, jnp.transpose(spread, (0, 2, 1))


def padded_rows(vectors, count):
    stacked = jnp.stack(vectors)
    return jnp.pad(stacked, ((0, count - stacked.shape[0]), (0, 0)))


def shards(
    block_input, w_reduce, w_group, w_expand, gain_one, bias_one, gain_two, bias_two,
    gain_three, bias_three, image_counts, grad_output,
):
    chan_size = lax.axis_size("chan")
    me = lax.axis_index("chan")
    images, rows, cols, out_part = block_input.shape
    mid_part = w_group.shape[3]
    group = w_group.shape[2]
    out_width = out_part * chan_size
    pixels = images * rows * cols
    own_count = jnp.sum(
        jnp.where(jnp.arange(image_counts.shape[0]) == lax.axis_index("batch"), image_counts, 0)
    )
    valid_total = jnp.sum(image_counts).astype(F32) * (rows * lax.axis_size("height") * cols)
    mask = jnp.repeat((jnp.arange(images) < own_count).astype(F32), rows * cols)[:, None]
    height_at = lax.axis_index("height")
    flags = jnp.stack(
        [own_count, (height_at > 0).astype(jnp.int32), (height_at < lax.axis_size("height") - 1).astype(jnp.int32)]
    ).astype(jnp.int32)
    params = [v.astype(F32) for v in (gain_one, bias_one, gain_two, bias_two, gain_three, bias_three)]
    gain_one, bias_one, gain_two, bias_two, gain_three, bias_three = params
    matrices, matrices_back = block_matrices(w_group)

    reduce_rows = [
        lax.dynamic_slice_in_dim(w_reduce, (me ^ k) * out_part, out_part, 0) for k in range(chan_size)
    ]
    reduce_back = [reduce_rows[0]] + [swap(reduce_rows[k], k) for k in range(1, chan_size)]
    expand_cols = [
        lax.dynamic_slice_in_dim(w_expand, (me ^ k) * out_part, out_part, 1) for k in range(chan_size)
    ]
    expand_here = [expand_cols[0]] + [swap(expand_cols[k], k) for k in range(1, chan_size)]

    field = block_input.reshape(pixels, out_part)
    inputs = gather_pieces(field)
    reduced = dot(inputs[0], reduce_rows[0], ((1,), (0,)))
    for k in range(1, chan_size):
        reduced = reduced + dot(inputs[k], reduce_rows[k], ((1,), (0,)))
    masked = reduced * mask
    sums_one = total_sums(jnp.sum(masked, 0), jnp.sum(masked * reduced, 0))
    reduced = reduced.reshape(images, rows * cols, mid_part)
    red_edges = edge_rows(reduced.reshape(images, rows, cols, mid_part))
    avg_one, inv_one = norm_vectors(sums_one, valid_total)

    acts_one, grouped, part = conv_forward(
        reduced, *red_edges, padded_rows([avg_one, inv_one * gain_one, bias_one], 8), matrices, flags, rows, cols
    )
    part = jnp.sum(part, 1)
    sums_two = total_sums(part[0], part[1])
    grp_edges = edge_rows(grouped.reshape(images, rows, cols, mid_part))
    avg_two, inv_two = norm_vectors(sums_two, valid_total)
    normal_two = (grouped.reshape(pixels, mid_part) - avg_two) * inv_two
    pre_two = normal_two * gain_two + bias_two
    act_two = (mask * jax.nn.silu(pre_two)).astype(BF16)

    acts_two = gather_pieces(act_two)
    expanded = dot(acts_two[0], expand_here[0], ((1,), (0,)))
    for k in range(1, chan_size):
        expanded = expanded + dot(acts_two[k], expand_here[k], ((1,), (0,)))
    masked = expanded * mask
    sums_three = total_sums(jnp.sum(masked, 0), jnp.sum(masked * expanded, 0))
    avg_three, inv_three = norm_vectors(sums_three, valid_total)
    normal_three = (expanded - avg_three) * inv_three
    summed = normal_three * gain_three + bias_three + field.astype(F32)
    output = (mask * jax.nn.silu(summed)).astype(BF16).reshape(block_input.shape)
    grad_summed = mask * grad_output.reshape(pixels, out_part).astype(F32) * smooth_slope(summed)
    grads_three = total_sums(jnp.sum(grad_summed, 0), jnp.sum(grad_summed * normal_three, 0))
    grad_expanded = (
        mask * inv_three * gain_three
        * (grad_summed - (grads_three[0] + normal_three * grads_three[1]) / valid_total)
    ).astype(BF16)

    grad_mid = scatter_pieces([dot(grad_expanded, expand_here[k], ((1,), (1,))) for k in range(chan_size)])
    expand_grads = [
        dot(acts_two[k], grad_expanded, ((0,), (0,))).astype(BF16) for k in range(chan_size)
    ]
    expand_grads = [expand_grads[0]] + [swap(expand_grads[k], k) for k in range(1, chan_size)]
    d_two = mask * grad_mid * smooth_slope(pre_two)
    grads_two = total_sums(jnp.sum(d_two, 0), jnp.sum(d_two * normal_two, 0))
    d_two = d_two.reshape(images, rows * cols, mid_part)
    d_edges = edge_rows(d_two.reshape(images, rows, cols, mid_part))
    vectors = padded_rows(
        [avg_two, inv_two, inv_two * gain_two, grads_two[0] / valid_total, grads_two[1] / valid_total,
         avg_one, inv_one, gain_one, bias_one],
        16,
    )
    d_one, part, grad_group = conv_backward(
        d_two, d_edges, grouped, grp_edges, reduced, acts_one, vectors, matrices_back, flags, rows, cols, group
    )
    part = jnp.sum(part, 1)
    grads_one = total_sums(part[0], part[1])
    normal_one = (reduced.reshape(pixels, mid_part) - avg_one) * inv_one
    grad_reduced = (
        mask * inv_one * gain_one
        * (d_one.reshape(pixels, mid_part) - (grads_one[0] + normal_one * grads_one[1]) / valid_total)
    ).astype(BF16)

    reduce_grads = [dot(inputs[k], grad_reduced, ((0,), (0,))).astype(BF16) for k in range(chan_size)]
    pieces = gather_pieces(grad_reduced)
    back = dot(pieces[0], reduce_back[0], ((1,), (1,)))
    for k in range(1, chan_size):
        back = back + dot(pieces[k], reduce_back[k], ((1,), (1,)))
    grad_input = (grad_summed + back).astype(BF16).reshape(block_input.shape)

    grad_reduce = jnp.zeros((out_width, mid_part), BF16)
    grad_expand = jnp.zeros((mid_part, out_width), BF16)
    for k in range(chan_size):
        grad_reduce = lax.dynamic_update_slice(grad_reduce, reduce_grads[k], ((me ^ k) * out_part, 0))
        grad_expand = lax.dynamic_update_slice(grad_expand, expand_grads[k], (0, (me ^ k) * out_part))
    grad_reduce, grad_group, grad_expand = (
        lax.psum(value, REDUCE_AXES).astype(F32)
        for value in (grad_reduce, grad_group.astype(BF16).reshape(w_group.shape), grad_expand)
    )
    return (
        output, grad_input, grad_reduce, grad_group, grad_expand,
        grads_one[1], grads_one[0], grads_two[1], grads_two[0], grads_three[1], grads_three[0],
    )


def solution(mesh):
    split = P("batch", "height", None, "chan")
    vector = P("chan")
    return jax.shard_map(
        shards,
        mesh=mesh,
        in_specs=(
            split, P(None, "chan"), P(None, None, None, "chan"), P("chan", None),
            vector, vector, vector, vector, vector, vector, P(), split,
        ),
        out_specs=(
            split, split, P(None, "chan"), P(None, None, None, "chan"), P("chan", None),
            vector, vector, vector, vector, vector, vector,
        ),
        check_vma=False,
    )
```

```python
import functools

import jax
import jax.numpy as jnp
from jax import lax
from jax.experimental import pallas as pl
from jax.experimental.pallas import tpu as pltpu
from jax.sharding import PartitionSpec as P

EPSILON = 1e-05
F32, BF16 = jnp.float32, jnp.bfloat16
REDUCE_AXES = ("height", "batch")
CHUNKS = 4
OWN_COUNT, TOTAL_COUNT, HEIGHT_AT, CHAN_AT, EDGE_ROW = range(5)


def dot(a, b, left, right):
    return lax.dot_general(a, b, (((left,), (right,)), ((), ())), preferred_element_type=F32)


def whole(shape):
    return pl.BlockSpec(shape, lambda s: (0,) * len(shape))


def rows_at(shape, offset=0):
    return pl.BlockSpec(shape, lambda s: (s + offset,) + (0,) * (len(shape) - 1))


SCALARS = pl.BlockSpec(memory_space=pltpu.SMEM)
KEPT = pl.BlockSpec(memory_space=pl.ANY)


def kernel_call(body, name, steps, ins, outs, scratch=(), alias=None, flops=0, heavy=0):
    arrays = [a for a, _ in ins]
    moved = sum(a.size * a.dtype.itemsize for a, s in ins if s is not KEPT)
    return pl.pallas_call(
        body,
        grid=(steps,),
        in_specs=[s for _, s in ins],
        out_specs=[s for _, _, s in outs],
        out_shape=[jax.ShapeDtypeStruct(shape, dtype) for shape, dtype, _ in outs],
        scratch_shapes=list(scratch),
        input_output_aliases=alias or {},
        compiler_params=pltpu.CompilerParams(
            dimension_semantics=("arbitrary",), vmem_limit_bytes=48 << 20
        ),
        cost_estimate=pl.CostEstimate(flops=flops, bytes_accessed=moved, transcendentals=heavy),
        name=name,
    )(*arrays)


def permute(value, axis, distance):
    count = lax.axis_size(axis)
    return lax.ppermute(value, axis, [(i, i ^ distance) for i in range(count)])


def swap(value, distance):
    return permute(value, "chan", distance)


def spread_sums(sent):
    return lax.all_to_all(sent, REDUCE_AXES, 0, 0)


def part_of(value, index, count):
    size = value.shape[0] // count
    return lax.dynamic_slice_in_dim(value, index * size, size, 0)


def scatter_over(value, axis):
    count, at = lax.axis_size(axis), lax.axis_index(axis)
    arrived = [permute(part_of(value, at ^ k, count), axis, k) for k in range(1, count)]
    total = part_of(value, at, count).astype(F32)
    for piece in arrived:
        total = total + piece.astype(F32)
    return total.astype(value.dtype)


def gather_over(value, axis):
    count, at = lax.axis_size(axis), lax.axis_index(axis)
    size = value.shape[0]
    pieces = [value] + [permute(value, axis, k) for k in range(1, count)]
    out = jnp.zeros((count * size,) + value.shape[1:], value.dtype)
    for k, piece in enumerate(pieces):
        out = lax.dynamic_update_slice_in_dim(out, piece, (at ^ k) * size, 0)
    return out


def norm_of(sums_ref, total):
    sums = jnp.sum(sums_ref[...], 0)
    average = sums[0:1] / total
    return average, lax.rsqrt(sums[1:2] / total - average * average + EPSILON)


def silu(v):
    return v / (1.0 + jnp.exp(-v))


def silu_slope(v):
    logistic = 1.0 / (1.0 + jnp.exp(-v))
    return logistic * (1.0 + v * (1.0 - logistic))


def fold(values):
    rows, chans = values.shape
    return jnp.sum(values.reshape(rows // 8, 8, chans), 0)


def share(out_ref, acc):
    both = jnp.concatenate([jnp.sum(acc[0], 0, keepdims=True), jnp.sum(acc[1], 0, keepdims=True)], 0)
    out_ref[...] = jnp.broadcast_to(both[None], out_ref.shape)


def start_sums(acc_ref, before_ref):
    @pl.when(pl.program_id(0) == 0)
    def _():
        acc_ref[...] = jnp.zeros_like(acc_ref) if before_ref is None else before_ref[...]


def end_sums(acc_ref, out_ref, last):
    @pl.when(pl.program_id(0) == pl.num_programs(0) - 1)
    def _():
        if last:
            share(out_ref, acc_ref[...])
        else:
            out_ref[...] = acc_ref[...]


def sums_out(last, chans):
    if last:
        shape = (lax.axis_size(REDUCE_AXES), 2, chans)
    else:
        shape = (2, 8, chans)
    return (shape, F32, whole(shape))


def block_matrices_kernel(group, taps_ref, fwd_ref, back_ref):
    chans = taps_ref.shape[2]
    same = (
        lax.broadcasted_iota(jnp.int32, (chans, chans), 0) // group
        == lax.broadcasted_iota(jnp.int32, (chans, chans), 1) // group
    )
    for tap in range(9):
        wide = jnp.concatenate([taps_ref[tap].astype(F32)] * (chans // group), 0)
        wide = jnp.where(same, wide, 0.0)
        fwd_ref[tap] = wide.astype(BF16)
        back_ref[tap] = wide.T.astype(BF16)


def block_matrices(kernel):
    group, chans = kernel.shape[2], kernel.shape[3]
    taps = kernel.reshape(9, group, chans)
    shape = (9, chans, chans)
    return kernel_call(
        functools.partial(block_matrices_kernel, group), "block_matrices", 1,
        [(taps, whole(taps.shape))], [(shape, BF16, whole(shape))] * 2,
    )


def reduce_kernel(offset, images, count, last, chained, info_ref, *refs):
    pieces, w_ref, refs = refs[:count], refs[count], refs[count + 1 :]
    before_ref = None
    if chained:
        before_ref, refs = refs[0], refs[3:]
    red_ref, edge_ref, sums_ref, acc_ref = refs
    start_sums(acc_ref, before_ref)
    me = info_ref[CHAN_AT]
    part = pieces[0].shape[1]
    total = None
    for k in range(count):
        rows = w_ref[pl.ds(pl.multiple_of((me ^ k) * part, part), part), :]
        term = dot(pieces[k][...], rows, 1, 0)
        total = term if total is None else total + term
    red_ref[...] = total.reshape(red_ref.shape)
    keep_edges(info_ref, red_ref, edge_ref, images)
    add_images(info_ref, acc_ref, offset, images, total, None)
    end_sums(acc_ref, sums_ref, last)


def keep_edges(info_ref, field_ref, edge_ref, images):
    rows = pl.ds(pl.multiple_of(info_ref[EDGE_ROW], 16), edge_ref.shape[1])
    for image in range(images):
        edge_ref[image] = field_ref[image, rows, :]


def add_images(info_ref, acc_ref, offset, images, values, others):
    pixels = values.shape[0] // images
    for image in range(images):
        real = offset + pl.program_id(0) * images + image < info_ref[OWN_COUNT]
        at = slice(image * pixels, (image + 1) * pixels)
        value = jnp.where(real, values[at], 0.0)
        other = value if others is None else others[at]
        acc_ref[0] += fold(value)
        acc_ref[1] += fold(value * other)


def reduce_chunk(info, inputs, chunk, w_reduce, state, plan):
    images, pixels, cols, step_images, per_chunk = plan
    count = len(inputs)
    part, mid = inputs[0].shape[1], w_reduce.shape[1]
    steps = per_chunk // step_images
    block = step_images * pixels
    ins = [(info, SCALARS)]
    for k, piece in enumerate(inputs):
        if k < 2:
            ins.append((piece, rows_at((block, part), chunk * steps)))
        else:
            ins.append((piece[chunk], rows_at((block, part))))
    ins.append((w_reduce, whole(w_reduce.shape)))
    alias = {}
    if state is not None:
        red, edge, acc = state
        ins += [(acc, whole(acc.shape)), (red, KEPT), (edge, KEPT)]
        alias = {len(ins) - 2: 0, len(ins) - 1: 1}
    last = (chunk + 1) * per_chunk == images
    return kernel_call(
        functools.partial(reduce_kernel, chunk * per_chunk, step_images, count, last, state is not None),
        "reduce", steps, ins,
        [
            ((images, pixels, mid), F32, rows_at((step_images, pixels, mid), chunk * steps)),
            ((images, cols, mid), F32, rows_at((step_images, cols, mid), chunk * steps)),
            sums_out(last, mid),
        ],
        [pltpu.VMEM((2, 8, mid), F32)], alias, 2 * per_chunk * pixels * part * count * mid,
    )


def fill_windows(window_ref, slot, value, cols):
    rows = value.shape[0]
    place = lax.broadcasted_iota(jnp.int32, value.shape, 0) % cols
    left = jnp.where(place == 0, 0.0, pltpu.roll(value, 1, 0))
    right = jnp.where(place == cols - 1, 0.0, pltpu.roll(value, rows - 1, 0))
    window_ref[0, slot] = left.astype(BF16)
    window_ref[1, slot] = value.astype(BF16)
    window_ref[2, slot] = right.astype(BF16)


def with_edges(info_ref, own, edge):
    above = jnp.where(info_ref[HEIGHT_AT] > 0, edge, 0.0)
    below = jnp.where(info_ref[HEIGHT_AT] > 0, 0.0, edge)
    return jnp.concatenate([above, own, below], 0)


def conv_forward_kernel(
    images, per_image, info_ref, red_ref, edge_ref, sums_one_ref, par_ref, mat_ref,
    act_ref, out_ref, out_edge_ref, sums_ref, window_ref, acc_ref,
):
    step = pl.program_id(0)
    pixels, chans = red_ref.shape[1:]
    cols = edge_ref.shape[1]
    start_sums(acc_ref, None)
    average, inv_std = norm_of(sums_one_ref, info_ref[TOTAL_COUNT].astype(F32) * per_image)
    scale, bias = inv_std * par_ref[0:1, :], par_ref[1:2, :]
    for image in range(images):
        real = step * images + image < info_ref[OWN_COUNT]
        own = jnp.where(real, silu((red_ref[image] - average) * scale + bias), 0.0)
        edge = jnp.where(real, silu((edge_ref[image] - average) * scale + bias), 0.0)
        act_ref[image] = own.astype(BF16)
        fill_windows(window_ref, image, with_edges(info_ref, own, edge), cols)
    total = jnp.zeros((images * pixels, chans), F32)
    for i in range(3):
        for j in range(3):
            piece = window_ref[j, :, i * cols : i * cols + pixels, :].reshape(images * pixels, chans)
            total = total + dot(piece, mat_ref[3 * i + j], 1, 0)
    out_ref[...] = total.reshape(images, pixels, chans)
    keep_edges(info_ref, out_ref, out_edge_ref, images)
    add_images(info_ref, acc_ref, 0, images, total, None)
    end_sums(acc_ref, sums_ref, True)


def conv_forward(info, reduced, edge, sums_one, params, matrices, per_image):
    image_count, pixels, chans = reduced.shape
    cols = edge.shape[1]
    images = 4
    field, edges = rows_at((images, pixels, chans)), rows_at((images, cols, chans))
    return kernel_call(
        functools.partial(conv_forward_kernel, images, per_image), "conv_forward", image_count // images,
        [
            (info, SCALARS), (reduced, field), (edge, edges), (sums_one, whole(sums_one.shape)),
            (params, whole(params.shape)), (matrices, whole(matrices.shape)),
        ],
        [
            (reduced.shape, BF16, field), (reduced.shape, F32, field), (edge.shape, F32, edges),
            sums_out(True, chans),
        ],
        [pltpu.VMEM((3, images, pixels + 2 * cols, chans), BF16), pltpu.VMEM((2, 8, chans), F32)],
        flops=18 * image_count * pixels * chans * chans, heavy=image_count * pixels * chans,
    )


def act_two_kernel(offset, images, per_image, info_ref, grp_ref, sums_ref, par_ref, out_ref):
    pixels = grp_ref.shape[1]
    average, inv_std = norm_of(sums_ref, info_ref[TOTAL_COUNT].astype(F32) * per_image)
    scale, bias = inv_std * par_ref[2:3, :], par_ref[3:4, :]
    for image in range(images):
        real = offset + pl.program_id(0) * images + image < info_ref[OWN_COUNT]
        act = jnp.where(real, silu((grp_ref[image] - average) * scale + bias), 0.0)
        out_ref[image * pixels : (image + 1) * pixels] = act.astype(BF16)


def act_two_chunk(info, grouped, sums_two, params, chunk, plan, per_image):
    images, pixels, cols, step_images, per_chunk = plan
    mid = grouped.shape[2]
    steps = per_chunk // step_images
    return kernel_call(
        functools.partial(act_two_kernel, chunk * per_chunk, step_images, per_image), "act_two", steps,
        [
            (info, SCALARS), (grouped, rows_at((step_images, pixels, mid), chunk * steps)),
            (sums_two, whole(sums_two.shape)), (params, whole(params.shape)),
        ],
        [((per_chunk * pixels, mid), BF16, rows_at((step_images * pixels, mid)))],
        heavy=per_chunk * pixels * mid,
    )[0]


def expand_kernel(offset, images, count, last, chained, info_ref, *refs):
    acts, weights, refs = refs[:count], refs[count : 2 * count], refs[2 * count :]
    before_ref = None
    if chained:
        before_ref, refs = refs[0], refs[2:]
    out_ref, sums_ref, acc_ref = refs
    start_sums(acc_ref, before_ref)
    total = None
    for a_ref, w_ref in zip(acts, weights):
        term = dot(a_ref[...], w_ref[...], 1, 0)
        total = term if total is None else total + term
    out_ref[...] = total
    add_images(info_ref, acc_ref, offset, images, total, None)
    end_sums(acc_ref, sums_ref, last)


def expand_chunk(info, acts, weights, chunk, state, plan):
    images, pixels, cols, step_images, per_chunk = plan
    count, mid, out = len(acts), acts[0].shape[1], weights[0].shape[1]
    steps = per_chunk // step_images
    block = step_images * pixels
    ins = [(info, SCALARS)]
    ins += [(a, rows_at((block, mid))) for a in acts]
    ins += [(w, whole(w.shape)) for w in weights]
    alias = {}
    if state is not None:
        buffer, acc = state
        ins += [(acc, whole(acc.shape)), (buffer, KEPT)]
        alias = {len(ins) - 1: 0}
    last = (chunk + 1) * per_chunk == images
    return kernel_call(
        functools.partial(expand_kernel, chunk * per_chunk, step_images, count, last, state is not None),
        "expand", steps, ins,
        [((images * pixels, out), F32, rows_at((block, out), chunk * steps)), sums_out(last, out)],
        [pltpu.VMEM((2, 8, out), F32)], alias, 2 * per_chunk * pixels * mid * count * out,
    )


def output_kernel(images, per_image, info_ref, exp_ref, in_ref, go_ref, sums_three_ref, par_ref,
                  out_ref, grad_ref, sums_ref, acc_ref):
    start_sums(acc_ref, None)
    average, inv_std = norm_of(sums_three_ref, info_ref[TOTAL_COUNT].astype(F32) * per_image)
    pixels = exp_ref.shape[0] // images
    for image in range(images):
        real = pl.program_id(0) * images + image < info_ref[OWN_COUNT]
        at = slice(image * pixels, (image + 1) * pixels)
        normalized = (exp_ref[at] - average) * inv_std
        summed = normalized * par_ref[0:1, :] + par_ref[1:2, :] + in_ref[at].astype(F32)
        logistic = 1.0 / (1.0 + jnp.exp(-summed))
        out_ref[at] = jnp.where(real, summed * logistic, 0.0).astype(BF16)
        slope = logistic * (1.0 + summed * (1.0 - logistic))
        grad = jnp.where(real, go_ref[at].astype(F32) * slope, 0.0)
        grad_ref[at] = grad
        acc_ref[0] += fold(grad)
        acc_ref[1] += fold(grad * normalized)
    end_sums(acc_ref, sums_ref, True)


def output_pass(info, expanded, field, grad_output, sums_three, params, plan, per_image):
    images, pixels, cols, step_images, per_chunk = plan
    out = expanded.shape[1]
    spec = rows_at((step_images * pixels, out))
    return kernel_call(
        functools.partial(output_kernel, step_images, per_image), "output", images // step_images,
        [
            (info, SCALARS), (expanded, spec), (field, spec), (grad_output, spec),
            (sums_three, whole(sums_three.shape)), (params, whole(params.shape)),
        ],
        [(expanded.shape, BF16, spec), (expanded.shape, F32, spec), sums_out(True, out)],
        [pltpu.VMEM((2, 8, out), F32)], heavy=expanded.size,
    )


def back_expand_kernel(offset, images, count, per_image, chained, info_ref, grad_ref, exp_ref, sums_three_ref,
                       grads_ref, par_ref, *refs):
    weights, refs = refs[:count], refs[count:]
    if chained:
        refs = refs[1:]
    out_ref, near_ref, far_ref = refs
    total = info_ref[TOTAL_COUNT].astype(F32) * per_image
    average, inv_std = norm_of(sums_three_ref, total)
    grads = jnp.sum(grads_ref[...], 0)
    bias_part, gain_part = grads[0:1] / total, grads[1:2] / total
    scale = inv_std * par_ref[0:1, :]
    pixels = grad_ref.shape[0] // images
    for image in range(images):
        real = offset + pl.program_id(0) * images + image < info_ref[OWN_COUNT]
        at = slice(image * pixels, (image + 1) * pixels)
        normalized = (exp_ref[at] - average) * inv_std
        value = scale * (grad_ref[at] - (bias_part + normalized * gain_part))
        out_ref[at] = jnp.where(real, value, 0.0).astype(BF16)
    grad = out_ref[...]
    mid = weights[0].shape[0]
    for k in range(count):
        term = dot(grad, weights[k][...], 1, 1)
        to = slice((k // 2) * mid, (k // 2 + 1) * mid)
        if k % 2 == 0:
            near_ref[:, to] = term
        else:
            far_ref[:, to] = term.astype(BF16)


def back_expand_chunk(info, grad_summed, expanded, sums_three, grads_three, params, weights, chunk, state, plan, per_image):
    images, pixels, cols, step_images, per_chunk = plan
    count, mid, out = len(weights), weights[0].shape[0], expanded.shape[1]
    steps = per_chunk // step_images
    block = step_images * pixels
    spec = rows_at((block, out), chunk * steps)
    ins = [
        (info, SCALARS), (grad_summed, spec), (expanded, spec), (sums_three, whole(sums_three.shape)),
        (grads_three, whole(grads_three.shape)), (params, whole(params.shape)),
    ]
    ins += [(w, whole(w.shape)) for w in weights]
    alias = {}
    if state is not None:
        ins.append((state, KEPT))
        alias = {len(ins) - 1: 0}
    half = count // 2 * mid
    return kernel_call(
        functools.partial(back_expand_kernel, chunk * per_chunk, step_images, count, per_image, state is not None),
        "back_expand", steps, ins,
        [
            (expanded.shape, BF16, spec),
            ((per_chunk * pixels, half), F32, rows_at((block, half))),
            ((per_chunk * pixels, half), BF16, rows_at((block, half))),
        ],
        alias=alias, flops=2 * per_chunk * pixels * mid * count * out,
    )


def pair_sum_kernel(near_ref, far_ref, own_ref, *send_refs):
    mid = own_ref.shape[1]
    for k, ref in enumerate((own_ref,) + send_refs):
        at = slice(k * mid, (k + 1) * mid)
        ref[...] = (near_ref[:, at] + far_ref[:, at].astype(F32)).astype(ref.dtype)


def pair_sum(near, far, mid):
    rows, half = near.shape
    spec = whole((rows, half))
    return kernel_call(
        pair_sum_kernel, "pair_sum", 1, [(near, spec), (far, spec)],
        [((rows, mid), F32 if k == 0 else BF16, whole((rows, mid))) for k in range(half // mid)],
    )


def slope_two_kernel(offset, images, count, per_image, last, chained, info_ref, own_ref, *refs):
    arrived, refs = refs[:count], refs[count:]
    grp_ref, sums_two_ref, par_ref, refs = refs[0], refs[1], refs[2], refs[3:]
    before_ref = None
    if chained:
        before_ref, refs = refs[0], refs[3:]
    out_ref, edge_ref, sums_ref, acc_ref = refs
    start_sums(acc_ref, before_ref)
    average, inv_std = norm_of(sums_two_ref, info_ref[TOTAL_COUNT].astype(F32) * per_image)
    gain, bias = par_ref[2:3, :], par_ref[3:4, :]
    pixels = grp_ref.shape[1]
    for image in range(images):
        real = offset + pl.program_id(0) * images + image < info_ref[OWN_COUNT]
        at = slice(image * pixels, (image + 1) * pixels)
        grad = own_ref[at]
        for ref in arrived:
            grad = grad + ref[at].astype(F32)
        normalized = (grp_ref[image] - average) * inv_std
        grad = jnp.where(real, grad * silu_slope(normalized * gain + bias), 0.0)
        out_ref[image] = grad
        acc_ref[0] += fold(grad)
        acc_ref[1] += fold(grad * normalized)
    keep_edges(info_ref, out_ref, edge_ref, images)
    end_sums(acc_ref, sums_ref, last)


def slope_two_chunk(info, own, arrived, grouped, sums_two, params, chunk, state, plan, per_image):
    images, pixels, cols, step_images, per_chunk = plan
    mid = grouped.shape[2]
    steps = per_chunk // step_images
    local = rows_at((step_images * pixels, mid))
    field = rows_at((step_images, pixels, mid), chunk * steps)
    ins = [(info, SCALARS), (own, local)] + [(a, local) for a in arrived]
    ins += [(grouped, field), (sums_two, whole(sums_two.shape)), (params, whole(params.shape))]
    alias = {}
    if state is not None:
        buffer, edge, acc = state
        ins += [(acc, whole(acc.shape)), (buffer, KEPT), (edge, KEPT)]
        alias = {len(ins) - 2: 0, len(ins) - 1: 1}
    last = (chunk + 1) * per_chunk == images
    return kernel_call(
        functools.partial(
            slope_two_kernel, chunk * per_chunk, step_images, len(arrived), per_image, last, state is not None
        ),
        "slope_two", steps, ins,
        [
            (grouped.shape, F32, field),
            ((images, cols, mid), F32, rows_at((step_images, cols, mid), chunk * steps)),
            sums_out(last, mid),
        ],
        [pltpu.VMEM((2, 8, mid), F32)], alias, heavy=per_chunk * pixels * mid,
    )


def expand_grad_kernel(count, chunks, parts, *refs):
    acts, grad_ref, out_ref = refs[: count * chunks], refs[-2], refs[-1]
    rows = grad_ref.shape[0] // chunks
    mid = acts[0].shape[1]
    size = mid // parts
    for k in range(count):
        total = None
        for c in range(chunks):
            term = dot(acts[k * chunks + c][...], grad_ref[c * rows : (c + 1) * rows, :], 0, 0)
            total = term if total is None else total + term
        out_ref[:, k] = total.reshape(parts, size, total.shape[1]).astype(BF16)


def expand_grad(acts, grad_expanded, parts):
    count, chunks = len(acts), len(acts[0])
    mid, out = acts[0][0].shape[1], grad_expanded.shape[1]
    shape = (parts, count, mid // parts, out)
    return kernel_call(
        functools.partial(expand_grad_kernel, count, chunks, parts), "expand_grad", 1,
        [(a, whole(a.shape)) for piece in acts for a in piece] + [(grad_expanded, whole(grad_expanded.shape))],
        [(shape, BF16, whole(shape))],
        flops=2 * grad_expanded.shape[0] * mid * count * out,
    )[0]


def conv_backward_kernel(
    images, per_image, group, info_ref, d_ref, d_edge_ref, grp_ref, g_edge_ref, red_ref, act_ref,
    sums_two_ref, grads_two_ref, sums_one_ref, par_ref, mat_ref,
    out_ref, sums_ref, kernel_ref, window_ref, total_ref, acc_ref,
):
    step = pl.program_id(0)
    pixels, chans = d_ref.shape[1:]
    cols = d_edge_ref.shape[1]
    total_pixels = info_ref[TOTAL_COUNT].astype(F32) * per_image
    avg_two, inv_two = norm_of(sums_two_ref, total_pixels)
    grads = jnp.sum(grads_two_ref[...], 0)
    bias_part, gain_part = grads[0:1] / total_pixels, grads[1:2] / total_pixels
    scale_two = inv_two * par_ref[2:3, :]
    avg_one, inv_one = norm_of(sums_one_ref, total_pixels)
    gain_one, bias_one = par_ref[0:1, :], par_ref[1:2, :]

    def input_grad(d, grouped, keep):
        normalized = (grouped - avg_two) * inv_two
        return jnp.where(keep, scale_two * (d - (bias_part + normalized * gain_part)), 0.0)

    start_sums(acc_ref, None)

    @pl.when(step == 0)
    def _():
        total_ref[...] = jnp.zeros_like(total_ref)

    for image in range(images):
        real = step * images + image < info_ref[OWN_COUNT]
        own = input_grad(d_ref[image], grp_ref[image], real)
        edge = input_grad(d_edge_ref[image], g_edge_ref[image], real)
        fill_windows(window_ref, image, with_edges(info_ref, own, edge), cols)
    grad = jnp.zeros((images * pixels, chans), F32)
    acts = act_ref[...].reshape(images * pixels, chans)
    for i in range(3):
        for j in range(3):
            at = (2 - i) * cols
            piece = window_ref[2 - j, :, at : at + pixels, :].reshape(images * pixels, chans)
            grad = grad + dot(piece, mat_ref[3 * i + j], 1, 0)
            total_ref[3 * i + j] += dot(acts, piece, 0, 0)
    for image in range(images):
        real = step * images + image < info_ref[OWN_COUNT]
        normalized = (red_ref[image] - avg_one) * inv_one
        slope = silu_slope(normalized * gain_one + bias_one)
        d_one = jnp.where(real, grad[image * pixels : (image + 1) * pixels] * slope, 0.0)
        out_ref[image] = d_one
        acc_ref[0] += fold(d_one)
        acc_ref[1] += fold(d_one * normalized)
    end_sums(acc_ref, sums_ref, True)

    @pl.when(step == pl.num_programs(0) - 1)
    def _():
        same = (
            lax.broadcasted_iota(jnp.int32, (chans, chans), 0) // group
            == lax.broadcasted_iota(jnp.int32, (chans, chans), 1) // group
        )
        for tap in range(9):
            own = jnp.where(same, total_ref[tap], 0.0)
            kernel_ref[tap] = jnp.sum(own.reshape(chans // group, group, chans), 0).astype(kernel_ref.dtype)


def conv_backward(info, d_two, d_edge, grouped, g_edge, reduced, acts, sums_two, grads_two, sums_one, params, matrices,
                  group, per_image):
    image_count, pixels, chans = reduced.shape
    cols = d_edge.shape[1]
    images = 4
    field, edges = rows_at((images, pixels, chans)), rows_at((images, cols, chans))
    small = [(v, whole(v.shape)) for v in (sums_two, grads_two, sums_one, params, matrices)]
    return kernel_call(
        functools.partial(conv_backward_kernel, images, per_image, group), "conv_backward", image_count // images,
        [
            (info, SCALARS), (d_two, field), (d_edge, edges), (grouped, field), (g_edge, edges),
            (reduced, field), (acts, field),
        ] + small,
        [
            (reduced.shape, F32, field), sums_out(True, chans),
            ((9, group, chans), BF16, whole((9, group, chans))),
        ],
        [
            pltpu.VMEM((3, images, pixels + 2 * cols, chans), BF16),
            pltpu.VMEM((9, chans, chans), F32),
            pltpu.VMEM((2, 8, chans), F32),
        ],
        flops=36 * image_count * pixels * chans * chans, heavy=image_count * pixels * chans,
    )


def grad_reduced_kernel(offset, images, per_image, info_ref, d_ref, red_ref, sums_one_ref, grads_ref, par_ref, out_ref):
    total = info_ref[TOTAL_COUNT].astype(F32) * per_image
    average, inv_std = norm_of(sums_one_ref, total)
    grads = jnp.sum(grads_ref[...], 0)
    bias_part, gain_part = grads[0:1] / total, grads[1:2] / total
    scale = inv_std * par_ref[0:1, :]
    pixels = d_ref.shape[1]
    for image in range(images):
        real = offset + pl.program_id(0) * images + image < info_ref[OWN_COUNT]
        normalized = (red_ref[image] - average) * inv_std
        value = scale * (d_ref[image] - (bias_part + normalized * gain_part))
        out_ref[image * pixels : (image + 1) * pixels] = jnp.where(real, value, 0.0).astype(BF16)


def grad_reduced_chunk(info, d_one, reduced, sums_one, grads_one, params, chunk, plan, per_image):
    images, pixels, cols, step_images, per_chunk = plan
    mid = reduced.shape[2]
    steps = per_chunk // step_images
    field = rows_at((step_images, pixels, mid), chunk * steps)
    return kernel_call(
        functools.partial(grad_reduced_kernel, chunk * per_chunk, step_images, per_image), "grad_reduced", steps,
        [
            (info, SCALARS), (d_one, field), (reduced, field), (sums_one, whole(sums_one.shape)),
            (grads_one, whole(grads_one.shape)), (params, whole(params.shape)),
        ],
        [((per_chunk * pixels, mid), BF16, rows_at((step_images * pixels, mid)))],
    )[0]


def reduce_grad_kernel(counts, chunks, *refs):
    grads, out_ref = refs[-1 - chunks : -1], refs[-1]
    rows = grads[0].shape[0]
    at = 0
    for k, pieces in enumerate(counts):
        total = None
        for c in range(chunks):
            ref = refs[at] if pieces == 1 else refs[at + c]
            value = ref[c * rows : (c + 1) * rows, :] if pieces == 1 else ref[...]
            term = dot(value, grads[c][...], 0, 0)
            total = term if total is None else total + term
        at += pieces
        part = total.shape[0]
        out_ref[k * part : (k + 1) * part, :] = total.astype(BF16)


def reduce_grad(inputs, grads):
    flat, counts = [], []
    for piece in inputs:
        piece = piece if isinstance(piece, (list, tuple)) else [piece]
        flat += piece
        counts.append(len(piece))
    part, mid = flat[0].shape[1], grads[0].shape[1]
    shape = (len(inputs) * part, mid)
    return kernel_call(
        functools.partial(reduce_grad_kernel, tuple(counts), len(grads)), "reduce_grad", 1,
        [(v, whole(v.shape)) for v in flat + list(grads)],
        [(shape, BF16, whole(shape))],
        flops=2 * len(grads) * grads[0].shape[0] * shape[0] * mid,
    )[0]


def input_grad_kernel(count, chained, grad_ref, *refs):
    pieces, weights, out_ref = refs[:count], refs[count : 2 * count], refs[-1]
    total = grad_ref[...]
    for p_ref, w_ref in zip(pieces, weights):
        total = total + dot(p_ref[...], w_ref[...], 1, 1)
    out_ref[...] = total.astype(BF16)


def input_grad_chunk(grad_summed, pieces, weights, chunk, state, plan):
    images, pixels, cols, step_images, per_chunk = plan
    count, mid, out = len(pieces), pieces[0].shape[1], grad_summed.shape[1]
    steps = per_chunk // step_images
    block = step_images * pixels
    spec = rows_at((block, out), chunk * steps)
    ins = [(grad_summed, spec)] + [(p, rows_at((block, mid))) for p in pieces]
    ins += [(w, whole(w.shape)) for w in weights]
    alias = {}
    if state is not None:
        ins.append((state, KEPT))
        alias = {len(ins) - 1: 0}
    return kernel_call(
        functools.partial(input_grad_kernel, count, state is not None), "input_grad", steps, ins,
        [(grad_summed.shape, BF16, spec)], alias=alias, flops=2 * per_chunk * pixels * mid * count * out,
    )[0]


def widen_kernel(at_ref, in_ref, out_ref):
    out_ref[...] = in_ref[...].reshape(out_ref.shape).astype(F32)


def place(at, value, block, out_shape, out_block, in_map, out_map, grid):
    return pl.pallas_call(
        widen_kernel,
        grid_spec=pltpu.PrefetchScalarGridSpec(
            num_scalar_prefetch=1, grid=grid,
            in_specs=[pl.BlockSpec(block, in_map)], out_specs=pl.BlockSpec(out_block, out_map),
        ),
        out_shape=jax.ShapeDtypeStruct(out_shape, F32),
        compiler_params=pltpu.CompilerParams(vmem_limit_bytes=48 << 20),
        name="place",
    )(at, value)


def shards(
    block_input, w_reduce, w_group, w_expand, gain_one, bias_one, gain_two, bias_two,
    gain_three, bias_three, image_counts, grad_output,
):
    chan_size = lax.axis_size("chan")
    me = lax.axis_index("chan")
    height_at = lax.axis_index("height")
    images, rows, cols, out_part = block_input.shape
    mid_part, group = w_group.shape[3], w_group.shape[2]
    pixels = rows * cols
    per_image = float(pixels * lax.axis_size("height"))
    per_chunk = images // CHUNKS
    plan = (images, pixels, cols, 2, per_chunk)
    chunk_rows = per_chunk * pixels
    own_count = jnp.sum(
        jnp.where(jnp.arange(image_counts.shape[0]) == lax.axis_index("batch"), image_counts, 0)
    )
    info = jnp.stack(
        [own_count, jnp.sum(image_counts), height_at, me, jnp.where(height_at == 0, pixels - cols, 0)]
    ).astype(jnp.int32)
    mid_params = jnp.stack([gain_one, bias_one, gain_two, bias_two]).astype(F32)
    out_params = jnp.stack([gain_three, bias_three]).astype(F32)
    chunks = range(CHUNKS)
    distances = range(2, chan_size, 2)

    def edge_swap(edge):
        return permute(edge, "height", 1)

    field = block_input.reshape(images * pixels, out_part)
    grad_field = grad_output.reshape(images * pixels, out_part)
    pieces = [lax.slice_in_dim(field, c * chunk_rows, (c + 1) * chunk_rows) for c in chunks]
    inputs = [field, swap(field, 1)] + [[] for _ in range(2, chan_size)]
    for c in chunks:
        for k in distances:
            inputs[k].append(swap(pieces[c], k))
    matrices, matrices_back = block_matrices(w_group)
    state = None
    for c in chunks:
        for k in distances:
            inputs[k + 1].append(swap(inputs[k][c], 1))
        state = reduce_chunk(info, inputs, c, w_reduce, state, plan)
    reduced, red_edge, sums = state
    sums_one = spread_sums(sums)
    red_edge = edge_swap(red_edge)

    reduced, w_expand, w_reduce = lax.optimization_barrier((reduced, w_expand, w_reduce))
    expand_here = [lax.dynamic_slice_in_dim(w_expand, (me ^ k) * out_part, out_part, 1) for k in range(chan_size)]
    expand_here = expand_here[:1] + [swap(expand_here[k], k) for k in range(1, chan_size)]
    reduce_back = [lax.dynamic_slice_in_dim(w_reduce, (me ^ k) * out_part, out_part, 0) for k in range(chan_size)]
    reduce_back = reduce_back[:1] + [swap(reduce_back[k], k) for k in range(1, chan_size)]

    acts_one, grouped, grp_edge, sums = conv_forward(
        info, reduced, red_edge, sums_one, mid_params, matrices, per_image
    )
    sums_two = spread_sums(sums)
    grp_edge = edge_swap(grp_edge)

    acts = [[] for _ in range(chan_size)]
    for c in chunks:
        acts[0].append(act_two_chunk(info, grouped, sums_two, mid_params, c, plan, per_image))
        for k in distances:
            acts[k].append(swap(acts[0][c], k))
        acts[1].append(swap(acts[0][c], 1))
    state = None
    for c in chunks:
        for k in distances:
            acts[k + 1].append(swap(acts[k][c], 1))
        state = expand_chunk(info, [piece[c] for piece in acts], expand_here, c, state, plan)
    expanded, sums = state
    sums_three = spread_sums(sums)
    output, grad_summed, sums = output_pass(
        info, expanded, field, grad_field, sums_three, out_params, plan, per_image
    )
    grads_three = spread_sums(sums)

    own, sent = [], []
    grad_expanded = None
    for c in chunks:
        grad_expanded, near, far = back_expand_chunk(
            info, grad_summed, expanded, sums_three, grads_three, out_params, expand_here, c, grad_expanded, plan, per_image
        )
        summed = pair_sum(near, swap(far, 1), mid_part)
        own.append(summed[0])
        sent.append([swap(value, k) for value, k in zip(summed[1:], distances)])
    state = None
    for c in chunks:
        state = slope_two_chunk(
            info, own[c], sent[c], grouped, sums_two, mid_params, c, state, plan, per_image
        )
    d_two, d_edge, sums = state
    grads_two = spread_sums(sums)
    d_edge = edge_swap(d_edge)

    parts = lax.axis_size(REDUCE_AXES)
    expand_part = expand_grad(acts, grad_expanded, parts)
    expand_part = scatter_over(scatter_over(expand_part, "height"), "batch")

    d_one, sums, grad_group = conv_backward(
        info, d_two, d_edge, grouped, grp_edge, reduced, acts_one, sums_two, grads_two, sums_one, mid_params,
        matrices_back, group, per_image,
    )
    grads_one = spread_sums(sums)
    grad_group = lax.psum(grad_group, REDUCE_AXES).astype(F32).reshape(w_group.shape)

    grads = [[] for _ in range(chan_size)]
    for c in chunks:
        grads[0].append(grad_reduced_chunk(info, d_one, reduced, sums_one, grads_one, mid_params, c, plan, per_image))
        for k in distances:
            grads[k].append(swap(grads[0][c], k))
        grads[1].append(swap(grads[0][c], 1))
    half = chan_size // 2
    reduce_parts = [reduce_grad(inputs[i * half : (i + 1) * half], grads[0]) for i in range(2)]
    reduce_parts = [scatter_over(v, "height") for v in reduce_parts]
    reduce_parts = [scatter_over(v, "batch") for v in reduce_parts]
    reduce_parts = [gather_over(v, "batch") for v in reduce_parts]
    reduce_parts = [gather_over(v, "height") for v in reduce_parts]
    grad_input = None
    for c in chunks:
        for k in distances:
            grads[k + 1].append(swap(grads[k][c], 1))
        grad_input = input_grad_chunk(
            grad_summed, [piece[c] for piece in grads], reduce_back, c, grad_input, plan
        )

    expand_part = [expand_part[:, k] for k in range(chan_size)]
    expand_part = expand_part[:1] + [swap(expand_part[k], k) for k in range(1, chan_size)]
    expand_all = gather_over(gather_over(jnp.stack(expand_part, 1), "batch"), "height")
    at = info[CHAN_AT : CHAN_AT + 1]
    size = mid_part // parts
    grad_expand = place(
        at, expand_all, (parts, None, size, out_part), (mid_part, out_part * chan_size), (mid_part, out_part),
        lambda k, at: (0, k, 0, 0), lambda k, at: (0, at[0] ^ k), (chan_size,),
    )
    grad_reduce = place(
        at, jnp.concatenate(reduce_parts, 0), (out_part, mid_part), (out_part * chan_size, mid_part), (out_part, mid_part),
        lambda k, at: (k, 0), lambda k, at: (at[0] ^ k, 0), (chan_size,),
    )
    vectors = [jnp.sum(v, 0) for v in (grads_one, grads_two, grads_three)]
    return (
        output.reshape(block_input.shape), grad_input.reshape(block_input.shape), grad_reduce, grad_group, grad_expand,
        vectors[0][1], vectors[0][0], vectors[1][1], vectors[1][0], vectors[2][1], vectors[2][0],
    )


def solution(mesh):
    split = P("batch", "height", None, "chan")
    vector = P("chan")
    return jax.shard_map(
        shards,
        mesh=mesh,
        in_specs=(
            split, P(None, "chan"), P(None, None, None, "chan"), P("chan", None),
            vector, vector, vector, vector, vector, vector, P(), split,
        ),
        out_specs=(
            split, split, P(None, "chan"), P(None, None, None, "chan"), P("chan", None),
            vector, vector, vector, vector, vector, vector,
        ),
        check_vma=False,
    )
```

```python
import functools

import jax
import jax.numpy as jnp
from jax import lax
from jax.experimental import pallas as pl
from jax.experimental.pallas import tpu as pltpu
from jax.sharding import PartitionSpec as P

EPSILON = 1e-05
F32, BF16 = jnp.float32, jnp.bfloat16
REDUCE_AXES = ("height", "batch")
REDUCE_CHUNKS, EXPAND_CHUNKS, BACK_CHUNKS = (12, 4), (8, 8), (4, 8, 4)
OWN_COUNT, TOTAL_COUNT, HEIGHT_AT, CHAN_AT, EDGE_ROW, BATCH_AT = range(6)
VMEM = pl.BlockSpec(memory_space=pltpu.VMEM)
SMEM = pl.BlockSpec(memory_space=pltpu.SMEM)


def dot(a, b, left, right):
    return lax.dot_general(a, b, (((left,), (right,)), ((), ())), preferred_element_type=F32)


def kernel_call(body, name, ins, outs, scratch=(), alias=None, flops=0, heavy=0, room=16):
    moved = sum(a.size * a.dtype.itemsize for a in ins)
    return pl.pallas_call(
        body,
        in_specs=[SMEM if a.dtype == jnp.int32 else VMEM for a in ins],
        out_specs=[VMEM] * len(outs),
        out_shape=[jax.ShapeDtypeStruct(shape, dtype) for shape, dtype in outs],
        scratch_shapes=list(scratch),
        input_output_aliases=alias or {},
        compiler_params=pltpu.CompilerParams(vmem_limit_bytes=room << 20),
        cost_estimate=pl.CostEstimate(flops=flops, bytes_accessed=moved, transcendentals=heavy),
        name=name,
    )(*ins)


def after(value, *others):
    return lax.optimization_barrier((value,) + others)[0]


def permute(value, axis, distance):
    count = lax.axis_size(axis)
    return lax.ppermute(value, axis, [(i, i ^ distance) for i in range(count)])


def swap(value, distance):
    return permute(value, "chan", distance)


def spread_sums(sent):
    return lax.all_to_all(sent, REDUCE_AXES, 0, 0)


def norm_of(sums_ref, total):
    sums = jnp.sum(sums_ref[...], 0)
    average = sums[0:1] / total
    return average, lax.rsqrt(sums[1:2] / total - average * average + EPSILON)


def pixel_count(info_ref, per_image):
    return info_ref[TOTAL_COUNT].astype(F32) * per_image


def sigmoid(v):
    return 0.5 * jnp.tanh(0.5 * v) + 0.5


def silu_slope(v):
    logistic = sigmoid(v)
    return logistic * (1.0 + v * (1.0 - logistic))


def fold(values):
    rows, chans = values.shape
    return jnp.sum(values.reshape(rows // 8, 8, chans), 0)


def put_sums(out_ref, one, two):
    if out_ref.shape[1] == 8:
        out_ref[0] = one
        out_ref[1] = two
    else:
        both = jnp.concatenate([jnp.sum(one, 0, keepdims=True), jnp.sum(two, 0, keepdims=True)], 0)
        out_ref[...] = jnp.broadcast_to(both[None], out_ref.shape)


def sums_out(last, chans):
    return ((lax.axis_size(REDUCE_AXES), 2, chans) if last else (2, 8, chans), F32)


def before_sums(before_ref, chans):
    if before_ref is None:
        zero = jnp.zeros((8, chans), F32)
        return zero, zero
    return before_ref[0], before_ref[1]


def edge_rows(info_ref, ref, image, cols):
    return ref[image, pl.ds(pl.multiple_of(info_ref[EDGE_ROW], 16), cols), :]


def prepare_kernel(group, info_ref, taps_ref, mid_a, mid_b, mid_c, mid_d, out_a, out_b, fwd_ref, back_ref, mid_ref, out_ref):
    chans = taps_ref.shape[2]
    same = (
        lax.broadcasted_iota(jnp.int32, (chans, chans), 0) // group
        == lax.broadcasted_iota(jnp.int32, (chans, chans), 1) // group
    )
    for i in range(3):
        for j in range(3):
            wide = jnp.concatenate([taps_ref[3 * i + j].astype(F32)] * (chans // group), 0)
            wide = jnp.where(same, wide, 0.0)
            fwd_ref[i, j * chans : (j + 1) * chans, :] = wide.astype(BF16)
            back_ref[2 - i, (2 - j) * chans : (3 - j) * chans, :] = wide.T.astype(BF16)
    for row, ref in enumerate((mid_a, mid_b, mid_c, mid_d)):
        mid_ref[row : row + 1, :] = ref[...].astype(F32)
    for row, ref in enumerate((out_a, out_b)):
        out_ref[row : row + 1, :] = ref[...].astype(F32)


def prepare(info, kernel, mid_vectors, out_vectors):
    group, chans = kernel.shape[2], kernel.shape[3]
    wide = (3, 3 * chans, chans)
    rows = [v.reshape(1, -1) for v in list(mid_vectors) + list(out_vectors)]
    return kernel_call(
        functools.partial(prepare_kernel, group), "prepare", [info, kernel.reshape(9, group, chans)] + rows,
        [(wide, BF16), (wide, BF16), ((4, chans), F32), ((2, rows[-1].shape[1]), F32)],
    )


def cut_images(shares):
    return [(sum(shares[:i]), share) for i, share in enumerate(shares)]


def reduce_kernel(first, plan, count, info_ref, *refs):
    pixels, cols = plan
    pieces, w_ref, before_ref = refs[:count], refs[count], None if len(refs) == count + 4 else refs[count + 1]
    red_ref, edge_ref, sums_ref = refs[-3:]
    me = info_ref[CHAN_AT]
    part, images = pieces[0].shape[1], red_ref.shape[0]
    one, two = before_sums(before_ref, w_ref.shape[1])
    step = min(4, images)
    for start in range(0, images, step):
        total = None
        for k in range(count):
            rows = w_ref[pl.ds(pl.multiple_of((me ^ k) * part, part), part), :]
            term = dot(pieces[k][start * pixels : (start + step) * pixels, :], rows, 1, 0)
            total = term if total is None else total + term
        for i in range(start, start + step):
            value = total[(i - start) * pixels : (i - start + 1) * pixels]
            red_ref[i] = value
            edge_ref[i] = edge_rows(info_ref, red_ref, i, cols).astype(BF16)
            value = value * (first + i < info_ref[OWN_COUNT]).astype(F32)
            one, two = one + fold(value), two + fold(value * value)
    put_sums(sums_ref, one, two)


def reduce_chunk(info, pieces, chunk, w_reduce, before, images, plan):
    pixels, cols = plan
    first, share = chunk
    count, mid = len(pieces), w_reduce.shape[1]
    ins = [info] + list(pieces) + [w_reduce] + ([] if before is None else [before])
    return kernel_call(
        functools.partial(reduce_kernel, first, plan, count), "reduce", ins,
        [((share, pixels, mid), F32), ((share, cols, mid), BF16), sums_out(first + share == images, mid)],
        flops=2 * pieces[0].size * count * mid,
    )


def each_image(chunks, body, carry, step=1):
    first = 0
    for refs in chunks:
        count = refs[0].shape[0]
        start = first
        carry = lax.fori_loop(
            0, count // step, lambda i, c, refs=refs, start=start: body(refs, i * step, start + i * step, c), carry
        )
        first += count
    return carry


def fill_windows(window_ref, slot, value, cols):
    rows, chans = value.shape
    place = lax.broadcasted_iota(jnp.int32, value.shape, 0) % cols
    left = jnp.where(place == 0, 0.0, pltpu.roll(value, 1, 0))
    right = jnp.where(place == cols - 1, 0.0, pltpu.roll(value, rows - 1, 0))
    window_ref[slot, :, 0:chans] = left.astype(BF16)
    window_ref[slot, :, chans : 2 * chans] = value.astype(BF16)
    window_ref[slot, :, 2 * chans : 3 * chans] = right.astype(BF16)


def with_edges(info_ref, own, edge):
    low = (info_ref[HEIGHT_AT] > 0).astype(F32)
    return jnp.concatenate([edge * low, own, edge * (1.0 - low)], 0)


def conv_forward_kernel(
    per_image, group_images, count, info_ref, *refs
):
    fields = list(zip(refs[:count], refs[count : 2 * count]))
    sums_one_ref, par_ref, mat_ref, act_ref, out_ref, out_edge_ref, sums_ref, window_ref = refs[2 * count :]
    images, pixels, chans = act_ref.shape
    cols = out_edge_ref.shape[1]
    average, inv_std = norm_of(sums_one_ref, pixel_count(info_ref, per_image))
    scale, bias = inv_std * par_ref[0:1, :], par_ref[1:2, :]

    def activate(v, keep):
        pre = (v - average) * scale + bias
        return pre * sigmoid(pre) * keep

    def fill(refs, at, image, nothing):
        keep = (image < info_ref[OWN_COUNT]).astype(F32)
        own = activate(refs[0][at], keep)
        edge = activate(refs[1][at].astype(F32), keep)
        act_ref[image] = own.astype(BF16)
        fill_windows(window_ref, image, with_edges(info_ref, own, edge), cols)
        return nothing

    def convolve(step, sums):
        first = step * group_images
        total = None
        for i in range(3):
            piece = window_ref[pl.ds(first, group_images), i * cols : i * cols + pixels, :]
            term = dot(piece.reshape(group_images * pixels, 3 * chans), mat_ref[i], 1, 0)
            total = term if total is None else total + term
        out_ref[pl.ds(first, group_images)] = total.reshape(group_images, pixels, chans)
        for i in range(group_images):
            out_edge_ref[first + i] = edge_rows(info_ref, out_ref, first + i, cols).astype(BF16)
        return sums[0] + fold(total), sums[1] + fold(total * total)

    each_image(fields, fill, 0)
    zero = jnp.zeros((8, chans), F32)
    put_sums(sums_ref, *lax.fori_loop(0, images // group_images, convolve, (zero, zero)))


def conv_forward(info, reduced, edges, sums_one, params, matrices, per_image):
    images = sum(v.shape[0] for v in reduced)
    pixels, chans = reduced[0].shape[1:]
    cols = edges[0].shape[1]
    shape = (images, pixels, chans)
    return kernel_call(
        functools.partial(conv_forward_kernel, per_image, 4, len(reduced)), "conv_forward",
        [info, *reduced, *edges, sums_one, params, matrices],
        [(shape, BF16), (shape, F32), ((images, cols, chans), BF16), sums_out(True, chans)],
        [pltpu.VMEM((images, pixels + 2 * cols, 3 * chans), BF16)],
        flops=18 * images * pixels * chans * chans, heavy=images * pixels * chans,
    )


def act_two_kernel(chunk, plan, per_image, info_ref, grp_ref, sums_ref, par_ref, out_ref):
    pixels, cols = plan
    first, images = chunk
    average, inv_std = norm_of(sums_ref, pixel_count(info_ref, per_image))
    scale, bias = inv_std * par_ref[2:3, :], par_ref[3:4, :]
    for i in range(images):
        image = first + i
        pre = (grp_ref[image] - average) * scale + bias
        act = pre * sigmoid(pre) * (image < info_ref[OWN_COUNT]).astype(F32)
        out_ref[i * pixels : (i + 1) * pixels] = act.astype(BF16)


def act_two_chunk(info, grouped, sums_two, params, chunk, plan, per_image):
    pixels, cols = plan
    shape = (chunk[1] * pixels, grouped.shape[2])
    return kernel_call(
        functools.partial(act_two_kernel, chunk, plan, per_image), "act_two",
        [info, grouped, sums_two, params], [(shape, BF16)], heavy=shape[0] * shape[1],
    )[0]


def expand_kernel(first, plan, count, mid, info_ref, *refs):
    pixels, cols = plan
    acts, weights = refs[:count], refs[count : 2 * count]
    before_ref = None if len(refs) == 2 * count + 2 else refs[2 * count]
    out_ref, sums_ref = refs[-2:]
    images = out_ref.shape[0]
    one, two = before_sums(before_ref, out_ref.shape[2])
    step = min(4, images)
    for start in range(0, images, step):
        total = None
        for a_ref, w_ref in zip(acts, weights):
            term = dot(a_ref[start * pixels : (start + step) * pixels, :], w_ref[0:mid, :], 1, 0)
            total = term if total is None else total + term
        out_ref[start : start + step] = total.reshape(step, pixels, total.shape[1])
        for i in range(step):
            keep = (first + start + i < info_ref[OWN_COUNT]).astype(F32)
            value = total[i * pixels : (i + 1) * pixels] * keep
            one, two = one + fold(value), two + fold(value * value)
    put_sums(sums_ref, one, two)


def expand_chunk(info, acts, weights, chunk, before, images, plan):
    pixels, cols = plan
    first, share = chunk
    count, mid, out = len(acts), acts[0].shape[1], weights[0].shape[1]
    ins = [info] + list(acts) + list(weights) + ([] if before is None else [before])
    return kernel_call(
        functools.partial(expand_kernel, first, plan, count, mid), "expand", ins,
        [((share, pixels, out), F32), sums_out(first + share == images, out)],
        flops=2 * acts[0].size * count * out,
    )


def output_kernel(per_image, count, info_ref, *refs):
    expanded = [[v] for v in refs[:count]]
    in_ref, go_ref, sums_three_ref, par_ref, out_ref, grad_ref, sums_ref = refs[count:]
    average, inv_std = norm_of(sums_three_ref, pixel_count(info_ref, per_image))
    gain, bias = par_ref[0:1, :], par_ref[1:2, :]
    chans = out_ref.shape[2]

    def body(refs, at, image, sums):
        keep = (image < info_ref[OWN_COUNT]).astype(F32)
        normalized = (refs[0][at] - average) * inv_std
        summed = normalized * gain + bias + in_ref[image].astype(F32)
        logistic = sigmoid(summed)
        out_ref[image] = (summed * logistic * keep).astype(BF16)
        slope = logistic * (1.0 + summed * (1.0 - logistic))
        grad = go_ref[image].astype(F32) * (slope * keep)
        grad_ref[image] = grad
        return sums[0] + fold(grad), sums[1] + fold(grad * normalized)

    zero = jnp.zeros((8, chans), F32)
    put_sums(sums_ref, *each_image(expanded, body, (zero, zero)))


def output_pass(info, expanded, field, grad_output, sums_three, params, per_image):
    return kernel_call(
        functools.partial(output_kernel, per_image, len(expanded)), "output",
        [info, *expanded, field, grad_output, sums_three, params],
        [(field.shape, BF16), (field.shape, F32), sums_out(True, field.shape[2])],
        heavy=field.size,
    )


def at_image(refs, image):
    for ref in refs:
        if image < ref.shape[0]:
            return ref[image]
        image -= ref.shape[0]


def back_expand_kernel(first, plan, count, mid, fields, per_image, info_ref, *refs):
    pixels, cols = plan
    expanded, refs = refs[:fields], refs[fields:]
    grad_ref, sums_three_ref, grads_ref, par_ref = refs[:4]
    weights = refs[4 : 4 + count]
    out_ref, near_ref, far_ref = refs[-3:]
    total = pixel_count(info_ref, per_image)
    average, inv_std = norm_of(sums_three_ref, total)
    grads = jnp.sum(grads_ref[...], 0)
    scale = inv_std * par_ref[0:1, :]
    bias_part, gain_part = grads[0:1] / total, grads[1:2] / total * inv_std
    for i in range(out_ref.shape[0] // pixels):
        image = first + i
        value = grad_ref[image] - (bias_part + (at_image(expanded, image) - average) * gain_part)
        value = value * (scale * (image < info_ref[OWN_COUNT]).astype(F32))
        out_ref[i * pixels : (i + 1) * pixels, :] = value.astype(BF16)
    for k in range(count):
        term = dot(out_ref[...], weights[k][0:mid, :], 1, 1)
        to = slice((k // 2) * mid, (k // 2 + 1) * mid)
        if k % 2 == 0:
            near_ref[:, to] = term
        else:
            far_ref[:, to] = term.astype(BF16)


def back_expand_chunk(info, grad_summed, expanded, sums_three, grads_three, params, weights, chunk, mid, plan, per_image):
    pixels, cols = plan
    count, out = len(weights), grad_summed.shape[2]
    block, half = chunk[1] * pixels, count // 2 * mid
    return kernel_call(
        functools.partial(back_expand_kernel, chunk[0], plan, count, mid, len(expanded), per_image), "back_expand",
        [info, *expanded, grad_summed, sums_three, grads_three, params, *weights],
        [((block, out), BF16), ((block, half), F32), ((block, half), BF16)],
        flops=2 * block * mid * count * out,
    )


def pair_sum_kernel(near_ref, far_ref, own_ref, *send_refs):
    mid = own_ref.shape[1]
    for k, ref in enumerate((own_ref,) + send_refs):
        at = slice(k * mid, (k + 1) * mid)
        ref[...] = (near_ref[:, at] + far_ref[:, at].astype(F32)).astype(ref.dtype)


def pair_sum(near, far, mid):
    rows, half = near.shape
    return kernel_call(
        pair_sum_kernel, "pair_sum", [near, far],
        [((rows, mid), F32 if k == 0 else BF16) for k in range(half // mid)],
    )


def slope_two_kernel(first, plan, count, per_image, info_ref, own_ref, *refs):
    pixels, cols = plan
    arrived, refs = refs[:count], refs[count:]
    grp_ref, sums_two_ref, par_ref = refs[:3]
    before_ref = None if len(refs) == 6 else refs[3]
    out_ref, edge_ref, sums_ref = refs[-3:]
    average, inv_std = norm_of(sums_two_ref, pixel_count(info_ref, per_image))
    gain, bias = par_ref[2:3, :], par_ref[3:4, :]
    one, two = before_sums(before_ref, grp_ref.shape[2])
    for i in range(out_ref.shape[0]):
        image = first + i
        at = slice(i * pixels, (i + 1) * pixels)
        grad = own_ref[at, :]
        for ref in arrived:
            grad = grad + ref[at, :].astype(F32)
        normalized = (grp_ref[image] - average) * inv_std
        keep = (image < info_ref[OWN_COUNT]).astype(F32)
        grad = grad * (silu_slope(normalized * gain + bias) * keep)
        out_ref[i] = grad
        edge_ref[i] = edge_rows(info_ref, out_ref, i, cols).astype(BF16)
        one, two = one + fold(grad), two + fold(grad * normalized)
    put_sums(sums_ref, one, two)


def slope_two_chunk(info, own, arrived, grouped, sums_two, params, chunk, before, plan, per_image):
    pixels, cols = plan
    first, share = chunk
    images, mid = grouped.shape[0], grouped.shape[2]
    ins = [info, own] + list(arrived) + [grouped, sums_two, params] + ([] if before is None else [before])
    return kernel_call(
        functools.partial(slope_two_kernel, first, plan, len(arrived), per_image), "slope_two", ins,
        [((share, pixels, mid), F32), ((share, cols, mid), BF16), sums_out(first + share == images, mid)],
        heavy=own.size,
    )


def conv_backward_kernel(
    per_image, group_images, group, d_count, red_count, info_ref, *refs
):
    d_fields, refs = list(zip(refs[:d_count], refs[d_count : 2 * d_count])), refs[2 * d_count :]
    reduced, refs = [[v] for v in refs[:red_count]], refs[red_count:]
    grp_ref, g_edge_ref, act_ref, sums_two_ref, grads_two_ref, sums_one_ref, par_ref, mat_ref = refs[:8]
    out_ref, sums_ref, kernel_ref, window_ref, turned_ref = refs[8:]
    images, pixels, chans = act_ref.shape
    cols = g_edge_ref.shape[1]
    total_pixels = pixel_count(info_ref, per_image)
    avg_two, inv_two = norm_of(sums_two_ref, total_pixels)
    grads = jnp.sum(grads_two_ref[...], 0)
    bias_part, gain_part = grads[0:1] / total_pixels, grads[1:2] / total_pixels * inv_two
    scale_two = inv_two * par_ref[2:3, :]
    avg_one, inv_one = norm_of(sums_one_ref, total_pixels)
    gain_one, bias_one = par_ref[0:1, :], par_ref[1:2, :]

    def input_grad(d, grouped, keep):
        return (d - (bias_part + (grouped - avg_two) * gain_part)) * (scale_two * keep)

    def fill(refs, at, image, nothing):
        keep = (image < info_ref[OWN_COUNT]).astype(F32)
        own = input_grad(refs[0][at], grp_ref[image], keep)
        edge = input_grad(refs[1][at].astype(F32), g_edge_ref[image].astype(F32), keep)
        fill_windows(window_ref, image, with_edges(info_ref, own, edge), cols)
        turned_ref[:, pl.ds(pl.multiple_of(image * pixels, pixels), pixels)] = act_ref[image].T
        return nothing

    def convolve(refs, at, first, sums):
        grad = None
        for i in range(3):
            piece = window_ref[pl.ds(first, group_images), i * cols : i * cols + pixels, :]
            term = dot(piece.reshape(group_images * pixels, 3 * chans), mat_ref[i], 1, 0)
            grad = term if grad is None else grad + term
        one, two = sums
        for i in range(group_images):
            image = first + i
            keep = (image < info_ref[OWN_COUNT]).astype(F32)
            normalized = (refs[0][at + i] - avg_one) * inv_one
            slope = silu_slope(normalized * gain_one + bias_one)
            d_one = grad[i * pixels : (i + 1) * pixels] * (slope * keep)
            out_ref[image] = d_one
            one, two = one + fold(d_one), two + fold(d_one * normalized)
        return one, two

    each_image(d_fields, fill, 0)
    zero = jnp.zeros((8, chans), F32)
    put_sums(sums_ref, *each_image(reduced, convolve, (zero, zero), group_images))
    same = (
        lax.broadcasted_iota(jnp.int32, (chans, 3 * chans), 0) // group
        == lax.broadcasted_iota(jnp.int32, (chans, 3 * chans), 1) % chans // group
    )
    for i in range(3):
        total = None
        for first in range(0, images, group_images):
            piece = window_ref[first : first + group_images, i * cols : i * cols + pixels, :]
            turned = turned_ref[:, first * pixels : (first + group_images) * pixels]
            term = dot(turned, piece.reshape(group_images * pixels, 3 * chans), 1, 0)
            total = term if total is None else total + term
        total = jnp.sum(jnp.where(same, total, 0.0).reshape(chans // group, group, 3 * chans), 0)
        for j in range(3):
            kernel_ref[3 * (2 - i) + 2 - j] = total[:, j * chans : (j + 1) * chans].astype(kernel_ref.dtype)


def conv_backward(info, d_two, d_edges, grouped, g_edge, reduced, acts, sums_two, grads_two, sums_one, params, matrices,
                  group, per_image):
    images, pixels, chans = grouped.shape
    cols = g_edge.shape[1]
    return kernel_call(
        functools.partial(conv_backward_kernel, per_image, 4, group, len(d_two), len(reduced)), "conv_backward",
        [info, *d_two, *d_edges, *reduced, grouped, g_edge, acts, sums_two, grads_two, sums_one, params, matrices],
        [(grouped.shape, F32), sums_out(True, chans), ((9, group, chans), F32)],
        [
            pltpu.VMEM((images, pixels + 2 * cols, 3 * chans), BF16),
            pltpu.VMEM((chans, images * pixels), BF16),
        ],
        flops=36 * images * pixels * chans * chans, heavy=images * pixels * chans,
    )


def grad_reduced_kernel(per_image, count, info_ref, *refs):
    reduced = [[v] for v in refs[:count]]
    d_ref, sums_one_ref, grads_ref, par_ref, out_ref = refs[count:]
    pixels = d_ref.shape[1]
    total = pixel_count(info_ref, per_image)
    average, inv_std = norm_of(sums_one_ref, total)
    grads = jnp.sum(grads_ref[...], 0)
    bias_part, gain_part = grads[0:1] / total, grads[1:2] / total * inv_std
    scale = inv_std * par_ref[0:1, :]

    def body(refs, at, image, nothing):
        value = d_ref[image] - (bias_part + (refs[0][at] - average) * gain_part)
        value = value * (scale * (image < info_ref[OWN_COUNT]).astype(F32))
        out_ref[pl.ds(pl.multiple_of(image * pixels, pixels), pixels), :] = value.astype(BF16)
        return nothing

    each_image(reduced, body, 0)


def grad_reduced(info, d_one, reduced, sums_one, grads_one, params, per_image):
    images, pixels, mid = d_one.shape
    return kernel_call(
        functools.partial(grad_reduced_kernel, per_image, len(reduced)), "grad_reduced",
        [info, *reduced, d_one, sums_one, grads_one, params], [((images * pixels, mid), BF16)],
    )[0]


def input_grad_kernel(count, mid, grad_ref, *refs):
    pieces, weights, out_ref = refs[:count], refs[count : 2 * count], refs[-1]
    rows = 512

    def body(step, nothing):
        at = pl.ds(pl.multiple_of(step * rows, rows), rows)
        total = grad_ref[at, :]
        for p_ref, w_ref in zip(pieces, weights):
            total = total + dot(p_ref[at, :], w_ref[mid : 2 * mid, :], 1, 0)
        out_ref[at, :] = total.astype(BF16)
        return nothing

    lax.fori_loop(0, grad_ref.shape[0] // rows, body, 0)


def input_grad(grad_summed, pieces, weights):
    count, mid = len(pieces), pieces[0].shape[1]
    return kernel_call(
        functools.partial(input_grad_kernel, count, mid), "input_grad", [grad_summed] + list(pieces) + list(weights),
        [(grad_summed.shape, BF16)], flops=2 * pieces[0].size * count * grad_summed.shape[1],
    )[0]


def cut_weights_kernel(count, info_ref, reduce_ref, expand_ref, *refs):
    me = info_ref[CHAN_AT]
    mid = expand_ref.shape[0]
    for k, ref in enumerate(refs):
        part = ref.shape[1]
        at = pl.ds(pl.multiple_of((me ^ k) * part, part), part)
        ref[0:mid, :] = expand_ref[:, at]
        ref[mid : 2 * mid, :] = reduce_ref[at, :].T


def cut_weights(info, w_reduce, w_expand, count):
    part, mid = w_reduce.shape[0] // count, w_reduce.shape[1]
    return kernel_call(
        functools.partial(cut_weights_kernel, count), "cut_weights", [info, w_reduce, w_expand],
        [((2 * mid, part), BF16)] * count,
    )


def sum_vectors_kernel(*refs):
    half = len(refs) // 3
    for ref, out_one, out_two in zip(refs[:half], refs[half::2], refs[half + 1 :: 2]):
        sums = jnp.sum(ref[...], 0)
        out_one[...] = sums[0:1]
        out_two[...] = sums[1:2]


def sum_vectors(values):
    outs = [((1, v.shape[2]), F32) for v in values for _ in range(2)]
    return [v.reshape(-1) for v in kernel_call(sum_vectors_kernel, "sum_vectors", list(values), outs)]


def split(at, keep_ref, send_ref, all_ref, arrived_ref):
    half = keep_ref.shape[0]
    for to, ref in ((at, keep_ref), (1 - at, send_ref)):
        value = all_ref[pl.ds(to * half, half)]
        if arrived_ref is not None:
            value = value + arrived_ref[pl.ds(to * half, half)].astype(F32)
        ref[...] = value.astype(ref.dtype)


def split_first_kernel(make, info_ref, *refs):
    keep_ref, send_ref, all_ref = refs[-3:]
    make(refs[:-3], all_ref)
    split(info_ref[HEIGHT_AT], keep_ref, send_ref, all_ref, None)


def split_first(info, make, name, ins, shape, flops):
    half = (shape[0] // 2,) + shape[1:]
    return kernel_call(
        functools.partial(split_first_kernel, make), name, [info] + ins, [(half, F32), (half, BF16)],
        [pltpu.VMEM(shape, F32)], flops=flops,
    )


def split_next_kernel(bit, info_ref, keep_ref, arrived_ref, out_ref, send_ref):
    split((info_ref[BATCH_AT] >> bit) & 1, out_ref, send_ref, keep_ref, arrived_ref)


def split_next(info, bit, keep, arrived):
    half = (keep.shape[0] // 2,) + keep.shape[1:]
    return kernel_call(
        functools.partial(split_next_kernel, bit), "split_next", [info, keep, arrived], [(half, F32), (half, BF16)]
    )


def add_kernel(first_ref, second_ref, out_ref):
    out_ref[...] = (first_ref[...] + second_ref[...].astype(F32)).astype(BF16)


def add_last(keep, arrived):
    return kernel_call(add_kernel, "add_last", [keep, arrived], [(keep.shape, BF16)])[0]


def join_kernel(*refs):
    size = refs[0].shape[0]
    for k, ref in enumerate(refs[:-1]):
        refs[-1][k * size : (k + 1) * size] = ref[...]


def join(*values):
    shape = (values[0].shape[0] * len(values),) + values[0].shape[1:]
    return kernel_call(join_kernel, "join", list(values), [(shape, BF16)])[0]


def batch_distance(bit):
    return lax.axis_size("batch") >> (bit + 1)


def scatter_height(pair):
    return pair[0], permute(pair[1], "height", 1)


def scatter_batch(info, pair):
    for bit in reversed(range(lax.axis_size("batch").bit_length() - 1)):
        keep, send = split_next(info, bit, *pair)
        pair = keep, permute(send, "batch", batch_distance(bit))
    return add_last(*pair)


def gather_batch(value):
    for bit in range(lax.axis_size("batch").bit_length() - 1):
        value = join(value, permute(value, "batch", batch_distance(bit)))
    return value


def gather_height(value):
    return value, permute(value, "height", 1)


def reduce_grad_make(places, spans, extra, refs, all_ref):
    grad_ref = refs[places * len(spans)]
    parts = all_ref.shape[0]
    per = parts // places
    for k in range(places):
        total = None
        for c, (first, end) in enumerate(spans):
            term = dot(refs[k * len(spans) + c][...], grad_ref[first:end, :], 0, 0)
            total = term if total is None else total + term
        size = total.shape[0] // per
        all_ref[k * per : (k + 1) * per, 0:size, :] = total.reshape(per, size, total.shape[1])
    if extra:
        more = refs[-1][...]
        more = more.reshape(-1, more.shape[2])
        room = parts * extra - more.shape[0]
        more = jnp.concatenate([more, jnp.zeros((room, more.shape[1]), F32)], 0)
        all_ref[:, size : size + extra, :] = more.reshape(parts, extra, more.shape[1])


def reduce_grad(info, inputs, grad, parts, more):
    spans = spans_of(inputs[0])
    rows, mid = len(inputs) * inputs[0][0].shape[1], grad.shape[1]
    extra = 0 if more is None else -(-more.shape[0] * more.shape[1] // (8 * parts)) * 8
    ins = [v for piece in inputs for v in piece] + [grad] + ([] if more is None else [more])
    return split_first(
        info, functools.partial(reduce_grad_make, len(inputs), tuple(spans), extra), "reduce_grad", ins,
        (parts, rows // parts + extra, mid), 2 * grad.size * rows,
    )


def spans_of(values):
    spans, at = [], 0
    for value in values:
        spans.append((at, at + value.shape[0]))
        at += value.shape[0]
    return spans


def expand_grad_make(count, chunks, refs, all_ref):
    acts, grads = refs[: count * chunks], refs[count * chunks :]
    parts, wide, out = all_ref.shape
    size = wide // count
    for k in range(count):
        total = None
        own = acts[k * chunks : (k + 1) * chunks]
        for a_ref, (a_first, a_end) in zip(own, spans_of(own)):
            for g_ref, (g_first, g_end) in zip(grads, spans_of(grads)):
                first, end = max(a_first, g_first), min(a_end, g_end)
                if first < end:
                    term = dot(a_ref[first - a_first : end - a_first, :], g_ref[first - g_first : end - g_first, :], 0, 0)
                    total = term if total is None else total + term
        all_ref[:, k * size : (k + 1) * size, :] = total.reshape(parts, size, out)


def expand_grad(info, acts, grads, parts):
    count, mid, out = len(acts), acts[0][0].shape[1], grads[0].shape[1]
    return split_first(
        info, functools.partial(expand_grad_make, count, len(acts[0])), "expand_grad",
        [a for piece in acts for a in piece] + list(grads),
        (parts, count * mid // parts, out), 2 * sum(g.size for g in grads) * mid * count,
    )


def cut_places_kernel(in_ref, *refs):
    size = refs[0].shape[0]
    for k, ref in enumerate(refs):
        ref[...] = in_ref[0, k * size : (k + 1) * size, :]


def cut_places(value, count):
    rows, out = value.shape[1:]
    return kernel_call(cut_places_kernel, "cut_places", [value], [((rows // count, out), BF16)] * count)


def part_rows(info_ref, other, k, batches):
    return (info_ref[HEIGHT_AT] ^ other) * batches + (info_ref[BATCH_AT] ^ k)


def place_reduce_kernel(count, info_ref, *refs):
    out_ref, more_ref = refs[4:]
    me = info_ref[CHAN_AT]
    part = out_ref.shape[0] // count
    batches = refs[0].shape[0]
    size = refs[2].shape[1]
    extra = refs[0].shape[1] - size
    for half in range(2):
        for other in range(2):
            ref = refs[2 * half + other]
            for k in range(batches):
                at = part_rows(info_ref, other, k, batches)
                row = at * size
                to = (me ^ (half * (count // 2) + row // part)) * part + row % part
                out_ref[pl.ds(pl.multiple_of(to, size), size), :] = ref[k, 0:size, :].astype(F32)
                if half == 0:
                    more_ref[pl.ds(pl.multiple_of(at * extra, 8), extra), :] = ref[k, size:, :].astype(F32)


def place_reduce(info, halves, count, part):
    batches, rows, mid = halves[0][0].shape
    extra = rows - halves[1][0].shape[1]
    return kernel_call(
        functools.partial(place_reduce_kernel, count), "place_reduce", [info] + [v for pair in halves for v in pair],
        [((part * count, mid), F32), ((2 * batches * extra, mid), F32)],
    )


def place_expand_kernel(count, info_ref, own_ref, arrived_ref, out_ref):
    me = info_ref[CHAN_AT]
    batches, rows, out = own_ref.shape
    size = rows // count
    for other, ref in enumerate((own_ref, arrived_ref)):
        for k in range(batches):
            row = part_rows(info_ref, other, k, batches) * size
            for place in range(count):
                to = pl.ds(pl.multiple_of((me ^ place) * out, out), out)
                out_ref[pl.ds(pl.multiple_of(row, size), size), to] = ref[k, place * size : (place + 1) * size, :].astype(F32)


def place_expand(info, pair, count, mid):
    out = pair[0].shape[2]
    return kernel_call(
        functools.partial(place_expand_kernel, count), "place_expand", [info] + list(pair), [((mid, out * count), F32)]
    )[0]


def plain_weight_grads(inputs, grad, acts, grad_expanded, grad_group):
    count, me = len(inputs), lax.axis_index("chan")
    part, mid = inputs[0][0].shape[1], grad.shape[1]
    grad_reduce = jnp.zeros((part * count, mid), BF16)
    grad_expand = jnp.zeros((mid, part * count), BF16)
    for k in range(count):
        block = dot(jnp.concatenate(inputs[k], 0), grad, 0, 0).astype(BF16)
        grad_reduce = lax.dynamic_update_slice(grad_reduce, block, ((me ^ k) * part, 0))
        block = dot(jnp.concatenate(acts[k], 0), jnp.concatenate(grad_expanded, 0), 0, 0).astype(BF16)
        block = swap(block, k) if k else block
        grad_expand = lax.dynamic_update_slice(grad_expand, block, (0, (me ^ k) * part))
    return [lax.psum(v, REDUCE_AXES).astype(F32) for v in (grad_reduce, grad_expand, grad_group.astype(BF16))]


def shards(
    block_input, w_reduce, w_group, w_expand, gain_one, bias_one, gain_two, bias_two,
    gain_three, bias_three, image_counts, grad_output,
):
    chan_size = lax.axis_size("chan")
    me = lax.axis_index("chan")
    height_at = lax.axis_index("height")
    images, rows, cols, out_part = block_input.shape
    mid_part, group = w_group.shape[3], w_group.shape[2]
    pixels = rows * cols
    per_image = float(pixels * lax.axis_size("height"))
    plan = (pixels, cols)
    distances = range(2, chan_size, 2)
    own_count = jnp.sum(
        jnp.where(jnp.arange(image_counts.shape[0]) == lax.axis_index("batch"), image_counts, 0)
    )
    batch_at, bits = lax.axis_index("batch"), lax.axis_size("batch").bit_length() - 1
    turned = sum(((batch_at >> bit) & 1) << (bits - 1 - bit) for bit in range(bits))
    info = jnp.stack(
        [own_count, jnp.sum(image_counts), height_at, me, jnp.where(height_at == 0, pixels - cols, 0), turned]
    ).astype(jnp.int32)
    parts = lax.axis_size(REDUCE_AXES)
    staged = lax.axis_size("batch") == 4

    def edge_swap(edge):
        return permute(edge, "height", 1)

    def far_swaps(value, pieces):
        for k in distances:
            pieces[k].append(swap(value, k))

    def core_swaps(pieces, *waits):
        for k in distances:
            pieces[k + 1].append(swap(after(pieces[k][-1], *waits) if waits else pieces[k][-1], 1))

    field = block_input.reshape(images * pixels, out_part)
    matrices, matrices_back, mid_params, out_params = prepare(
        info, w_group, (gain_one, bias_one, gain_two, bias_two), (gain_three, bias_three)
    )
    inputs = [[] for _ in range(chan_size)]
    reduced, red_edges, sums = [], [], None
    for first, share in cut_images(REDUCE_CHUNKS):
        source = after(field, inputs[0][0]) if first else field
        piece = lax.slice_in_dim(source, first * pixels, (first + share) * pixels)
        inputs[0].append(piece)
        far_swaps(piece, inputs)
        inputs[1].append(swap(piece, 1))
        core_swaps(inputs, *(() if sums is None else (sums,)))
        red, edge, sums = reduce_chunk(info, [p[-1] for p in inputs], (first, share), w_reduce, sums, images, plan)
        reduced.append(red)
        red_edges.append(edge_swap(edge))
    sums_one = spread_sums(sums)

    w_expand, w_reduce = after((w_expand, w_reduce), sums)
    weights = cut_weights(info, w_reduce, w_expand, chan_size)
    weights = [v if k == 0 else swap(v, k) for k, v in enumerate(weights)]

    acts_one, grouped, grp_edge, sums = conv_forward(
        info, reduced, red_edges, sums_one, mid_params, matrices, per_image
    )
    sums_two = spread_sums(sums)

    acts = [[] for _ in range(chan_size)]
    for chunk in cut_images(EXPAND_CHUNKS):
        acts[0].append(act_two_chunk(info, grouped, sums_two, mid_params, chunk, plan, per_image))
        far_swaps(acts[0][-1], acts)
    expanded, sums = [], None
    for c, chunk in enumerate(cut_images(EXPAND_CHUNKS)):
        acts[1].append(swap(acts[0][c], 1))
        for k in distances:
            acts[k + 1].append(swap(acts[k][c] if sums is None else after(acts[k][c], sums), 1))
        out, sums = expand_chunk(info, [piece[c] for piece in acts], weights, chunk, sums, images, plan)
        expanded.append(out)
    sums_three = spread_sums(sums)
    grp_edge = edge_swap(after(grp_edge, sums_three))
    output, grad_summed, sums = output_pass(
        info, expanded, field.reshape(images, pixels, out_part), grad_output.reshape(images, pixels, out_part), sums_three,
        out_params, per_image,
    )
    grads_three = spread_sums(sums)

    own, sent = [], [[] for _ in range(chan_size)]
    grad_expanded = []
    for chunk in cut_images(BACK_CHUNKS):
        grad_here = after(grad_summed, own[-2]) if len(own) > 1 else grad_summed
        grad, near, far = back_expand_chunk(
            info, grad_here, expanded, sums_three, grads_three, out_params, weights, chunk, mid_part, plan, per_image
        )
        grad_expanded.append(grad)
        summed = pair_sum(near, swap(far, 1), mid_part)
        own.append(summed[0])
        for value, k in zip(summed[1:], distances):
            sent[k].append(swap(value, k))
    if staged:
        expand_part = scatter_height(expand_grad(info, acts, after(grad_expanded, own[-1]), parts))
    d_two, d_edges, sums = [], [], None
    for c, chunk in enumerate(cut_images(BACK_CHUNKS)):
        grad, edge, sums = slope_two_chunk(
            info, own[c], [sent[k][c] for k in distances], grouped, sums_two, mid_params, chunk, sums, plan, per_image
        )
        d_two.append(grad)
        d_edges.append(edge)
    if staged:
        sums = after(sums, expand_part[1])
    grads_two = spread_sums(sums)
    d_edges = [edge_swap(edge) for edge in d_edges]
    if staged:
        expand_part = scatter_batch(info, (expand_part[0], after(expand_part[1], grads_two)))

    d_one, sums, grad_group = conv_backward(
        info, d_two, d_edges, grouped, grp_edge, reduced, acts_one, sums_two, grads_two, sums_one, mid_params,
        matrices_back, group, per_image,
    )
    grads_one = spread_sums(sums)

    grads = [[] for _ in range(chan_size)]
    grads[0].append(grad_reduced(info, d_one, reduced, sums_one, grads_one, mid_params, per_image))
    far_swaps(grads[0][0], grads)
    grads[1].append(swap(grads[0][0], 1))
    core_swaps(grads)
    half = chan_size // 2
    if staged:
        halves = [
            scatter_height(reduce_grad(info, inputs[i * half : (i + 1) * half], grads[0][0], parts, None if i else grad_group))
            for i in range(2)
        ]
        halves = [gather_height(gather_batch(scatter_batch(info, pair))) for pair in halves]
        grad_reduce, grad_group = place_reduce(info, halves, chan_size, out_part)
        grad_group = grad_group[: 9 * group]
        places = cut_places(expand_part, chan_size)
        places = [v if k == 0 else swap(v, k) for k, v in enumerate(places)]
        expand_part = after(join(*places), grads_one)
        expand_part = gather_height(gather_batch(expand_part.reshape((1,) + expand_part.shape)))
        grad_expand = place_expand(info, expand_part, chan_size, mid_part)
    else:
        grad_reduce, grad_expand, grad_group = plain_weight_grads(inputs, grads[0][0], acts, grad_expanded, grad_group)
    grad_input = input_grad(grad_summed.reshape(images * pixels, out_part), [piece[0] for piece in grads], weights)
    vectors = sum_vectors([grads_one, grads_two, grads_three])
    return (
        output.reshape(block_input.shape), grad_input.reshape(block_input.shape), grad_reduce,
        grad_group.reshape(w_group.shape), grad_expand,
        vectors[1], vectors[0], vectors[3], vectors[2], vectors[5], vectors[4],
    )


def solution(mesh):
    split = P("batch", "height", None, "chan")
    vector = P("chan")
    return jax.shard_map(
        shards,
        mesh=mesh,
        in_specs=(
            split, P(None, "chan"), P(None, None, None, "chan"), P("chan", None),
            vector, vector, vector, vector, vector, vector, P(), split,
        ),
        out_specs=(
            split, split, P(None, "chan"), P(None, None, None, "chan"), P("chan", None),
            vector, vector, vector, vector, vector, vector,
        ),
        check_vma=False,
    )
```

```python
import functools

import jax
import jax.numpy as jnp
from jax import lax
from jax.experimental import pallas as pl
from jax.experimental.pallas import tpu as pltpu
from jax.sharding import PartitionSpec as P

EPSILON = 1e-05
F32, BF16 = jnp.float32, jnp.bfloat16
REDUCE_AXES = ("height", "batch")
REDUCE_CHUNKS, EXPAND_CHUNKS, BACK_CHUNKS = (8, 8), (8, 8), (8, 8)
OWN_COUNT, TOTAL_COUNT, HEIGHT_AT, CHAN_AT, EDGE_ROW, NEAR_AT, FAR_AT = range(7)
VMEM = pl.BlockSpec(memory_space=pltpu.VMEM)
SMEM = pl.BlockSpec(memory_space=pltpu.SMEM)


def dot(a, b, left, right):
    return lax.dot_general(a, b, (((left,), (right,)), ((), ())), preferred_element_type=F32)


def kernel_call(body, name, ins, outs, scratch=(), alias=None, flops=0, room=16):
    return pl.pallas_call(
        body,
        in_specs=[SMEM if a.dtype == jnp.int32 else VMEM for a in ins],
        out_specs=[VMEM] * len(outs),
        out_shape=[jax.ShapeDtypeStruct(shape, dtype) for shape, dtype in outs],
        scratch_shapes=list(scratch),
        input_output_aliases=alias or {},
        compiler_params=pltpu.CompilerParams(vmem_limit_bytes=room << 20),
        cost_estimate=pl.CostEstimate(flops=flops, bytes_accessed=0, transcendentals=0),
        name=name,
    )(*ins)


def after(value, *others):
    return lax.optimization_barrier((value,) + others)[0]


def permute(value, axis, distance):
    count = lax.axis_size(axis)
    return lax.ppermute(value, axis, [(i, i ^ distance) for i in range(count)])


def swap(value, distance):
    return permute(value, "chan", distance)


def spread_sums(sent):
    return lax.all_to_all(sent, REDUCE_AXES, 0, 0)


def staged_sums(partial, *waits):
    chans = partial.shape[2]
    both = kernel_call(
        add_rows_kernel, "add_rows", [after(partial, *waits), permute(partial, "height", 1)], [((2, chans), F32)]
    )[0]
    others = [permute(both, "batch", k) for k in range(1, lax.axis_size("batch"))]
    return kernel_call(add_sums_kernel, "add_sums", [both] + others, [((1, 2, chans), F32)])[0]


def add_rows_kernel(own_ref, other_ref, out_ref):
    out_ref[...] = jnp.sum(own_ref[...] + other_ref[...], 1)


def add_sums_kernel(*refs):
    total = refs[0][...]
    for ref in refs[1:-1]:
        total = total + ref[...]
    refs[-1][0] = total


def norm_of(sums_ref, total):
    sums = jnp.sum(sums_ref[...], 0)
    average = sums[0:1] / total
    return average, lax.rsqrt(sums[1:2] / total - average * average + EPSILON)


def pixel_count(info_ref, per_image):
    return info_ref[TOTAL_COUNT].astype(F32) * per_image


def sigmoid(v):
    return 0.5 * jnp.tanh(0.5 * v) + 0.5


def silu_slope(v):
    logistic = sigmoid(v)
    return logistic * (1.0 + v * (1.0 - logistic))


def fold(values):
    rows, chans = values.shape
    return jnp.sum(values.reshape(rows // 8, 8, chans), 0)


def put_sums(out_ref, one, two):
    if out_ref.shape[1] == 8:
        out_ref[0] = one
        out_ref[1] = two
    else:
        both = jnp.concatenate([jnp.sum(one, 0, keepdims=True), jnp.sum(two, 0, keepdims=True)], 0)
        out_ref[...] = jnp.broadcast_to(both[None], out_ref.shape)


def sums_out(last, chans):
    return ((lax.axis_size(REDUCE_AXES), 2, chans) if last else (2, 8, chans), F32)


def before_sums(before_ref, chans):
    if before_ref is None:
        zero = jnp.zeros((8, chans), F32)
        return zero, zero
    return before_ref[0], before_ref[1]


def edge_rows(info_ref, ref, image, cols):
    return ref[image, pl.ds(pl.multiple_of(info_ref[EDGE_ROW], 16), cols), :]


def prepare_kernel(group, info_ref, taps_ref, mid_a, mid_b, mid_c, mid_d, out_a, out_b, fwd_ref, back_ref, mid_ref, out_ref):
    chans = taps_ref.shape[2]
    same = (
        lax.broadcasted_iota(jnp.int32, (chans, chans), 0) // group
        == lax.broadcasted_iota(jnp.int32, (chans, chans), 1) // group
    )
    for i in range(3):
        for j in range(3):
            wide = jnp.concatenate([taps_ref[3 * i + j].astype(F32)] * (chans // group), 0)
            wide = jnp.where(same, wide, 0.0)
            fwd_ref[i, j * chans : (j + 1) * chans, :] = wide.astype(BF16)
            back_ref[2 - i, (2 - j) * chans : (3 - j) * chans, :] = wide.T.astype(BF16)
    for row, ref in enumerate((mid_a, mid_b, mid_c, mid_d)):
        mid_ref[row : row + 1, :] = ref[...].astype(F32)
    for row, ref in enumerate((out_a, out_b)):
        out_ref[row : row + 1, :] = ref[...].astype(F32)


def prepare(info, kernel, mid_vectors, out_vectors):
    group, chans = kernel.shape[2], kernel.shape[3]
    wide = (3, 3 * chans, chans)
    rows = [v.reshape(1, -1) for v in list(mid_vectors) + list(out_vectors)]
    return kernel_call(
        functools.partial(prepare_kernel, group), "prepare", [info, kernel.reshape(9, group, chans)] + rows,
        [(wide, BF16), (wide, BF16), ((4, chans), F32), ((2, rows[-1].shape[1]), F32)],
    )


def cut_images(shares):
    return [(sum(shares[:i]), share) for i, share in enumerate(shares)]


def reduce_kernel(first, plan, count, info_ref, *refs):
    pixels, cols = plan
    pieces, w_ref, before_ref = refs[:count], refs[count], None if len(refs) == count + 4 else refs[count + 1]
    red_ref, edge_ref, sums_ref = refs[-3:]
    me = info_ref[CHAN_AT]
    part, images = pieces[0].shape[1], red_ref.shape[0]
    one, two = before_sums(before_ref, w_ref.shape[1])
    step = min(4, images)
    for start in range(0, images, step):
        total = None
        for k in range(count):
            rows = w_ref[pl.ds(pl.multiple_of((me ^ k) * part, part), part), :]
            term = dot(pieces[k][start * pixels : (start + step) * pixels, :], rows, 1, 0)
            total = term if total is None else total + term
        for i in range(start, start + step):
            value = total[(i - start) * pixels : (i - start + 1) * pixels]
            red_ref[i] = value
            edge_ref[i] = edge_rows(info_ref, red_ref, i, cols).astype(BF16)
            value = value * (first + i < info_ref[OWN_COUNT]).astype(F32)
            one, two = one + fold(value), two + fold(value * value)
    put_sums(sums_ref, one, two)


def reduce_chunk(info, pieces, chunk, w_reduce, before, images, plan, staged):
    pixels, cols = plan
    first, share = chunk
    count, mid = len(pieces), w_reduce.shape[1]
    ins = [info] + list(pieces) + [w_reduce] + ([] if before is None else [before])
    return kernel_call(
        functools.partial(reduce_kernel, first, plan, count), "reduce", ins,
        [((share, pixels, mid), F32), ((share, cols, mid), BF16), sums_out(first + share == images and not staged, mid)],
        flops=2 * pieces[0].size * count * mid,
    )


def each_image(chunks, body, carry, step=1):
    first = 0
    for refs in chunks:
        count = refs[0].shape[0]
        start = first
        carry = lax.fori_loop(
            0, count // step, lambda i, c, refs=refs, start=start: body(refs, i * step, start + i * step, c), carry
        )
        first += count
    return carry


def fill_windows(window_ref, slot, value, cols):
    rows, chans = value.shape
    place = lax.broadcasted_iota(jnp.int32, value.shape, 0) % cols
    left = jnp.where(place == 0, 0.0, pltpu.roll(value, 1, 0))
    right = jnp.where(place == cols - 1, 0.0, pltpu.roll(value, rows - 1, 0))
    window_ref[slot, :, 0:chans] = left.astype(BF16)
    window_ref[slot, :, chans : 2 * chans] = value.astype(BF16)
    window_ref[slot, :, 2 * chans : 3 * chans] = right.astype(BF16)


def with_edges(info_ref, own, edge):
    low = (info_ref[HEIGHT_AT] > 0).astype(F32)
    return jnp.concatenate([edge * low, own, edge * (1.0 - low)], 0)


def conv_forward_kernel(
    per_image, group_images, count, info_ref, *refs
):
    fields = list(zip(refs[:count], refs[count : 2 * count]))
    sums_one_ref, par_ref, mat_ref, act_ref, out_ref, out_edge_ref, sums_ref, window_ref = refs[2 * count :]
    images, pixels, chans = act_ref.shape
    cols = out_edge_ref.shape[1]
    average, inv_std = norm_of(sums_one_ref, pixel_count(info_ref, per_image))
    scale, bias = inv_std * par_ref[0:1, :], par_ref[1:2, :]

    def activate(v, keep):
        pre = (v - average) * scale + bias
        return pre * sigmoid(pre) * keep

    def fill(refs, at, image, nothing):
        keep = (image < info_ref[OWN_COUNT]).astype(F32)
        own = activate(refs[0][at], keep)
        edge = activate(refs[1][at].astype(F32), keep)
        act_ref[image] = own.astype(BF16)
        fill_windows(window_ref, image, with_edges(info_ref, own, edge), cols)
        return nothing

    def convolve(step, sums):
        first = step * group_images
        total = None
        for i in range(3):
            piece = window_ref[pl.ds(first, group_images), i * cols : i * cols + pixels, :]
            term = dot(piece.reshape(group_images * pixels, 3 * chans), mat_ref[i], 1, 0)
            total = term if total is None else total + term
        out_ref[pl.ds(first, group_images)] = total.reshape(group_images, pixels, chans)
        for i in range(group_images):
            out_edge_ref[first + i] = edge_rows(info_ref, out_ref, first + i, cols).astype(BF16)
        return sums[0] + fold(total), sums[1] + fold(total * total)

    each_image(fields, fill, 0)
    zero = jnp.zeros((8, chans), F32)
    put_sums(sums_ref, *lax.fori_loop(0, images // group_images, convolve, (zero, zero)))


def conv_forward(info, reduced, edges, sums_one, params, matrices, per_image):
    images = sum(v.shape[0] for v in reduced)
    pixels, chans = reduced[0].shape[1:]
    cols = edges[0].shape[1]
    shape = (images, pixels, chans)
    return kernel_call(
        functools.partial(conv_forward_kernel, per_image, 4, len(reduced)), "conv_forward",
        [info, *reduced, *edges, sums_one, params, matrices],
        [(shape, BF16), (shape, F32), ((images, cols, chans), BF16), sums_out(True, chans)],
        [pltpu.VMEM((images, pixels + 2 * cols, 3 * chans), BF16)],
    )


def act_two_kernel(chunk, plan, per_image, info_ref, grp_ref, sums_ref, par_ref, out_ref):
    pixels, cols = plan
    first, images = chunk
    average, inv_std = norm_of(sums_ref, pixel_count(info_ref, per_image))
    scale, bias = inv_std * par_ref[2:3, :], par_ref[3:4, :]
    for i in range(images):
        image = first + i
        pre = (grp_ref[image] - average) * scale + bias
        act = pre * sigmoid(pre) * (image < info_ref[OWN_COUNT]).astype(F32)
        out_ref[i * pixels : (i + 1) * pixels] = act.astype(BF16)


def act_two_chunk(info, grouped, sums_two, params, chunk, plan, per_image):
    pixels, cols = plan
    shape = (chunk[1] * pixels, grouped.shape[2])
    return kernel_call(
        functools.partial(act_two_kernel, chunk, plan, per_image), "act_two",
        [info, grouped, sums_two, params], [(shape, BF16)],
    )[0]


def expand_kernel(first, plan, count, mid, info_ref, *refs):
    pixels, cols = plan
    acts, weights = refs[:count], refs[count : 2 * count]
    before_ref = None if len(refs) == 2 * count + 2 else refs[2 * count]
    out_ref, sums_ref = refs[-2:]
    images = out_ref.shape[0]
    one, two = before_sums(before_ref, out_ref.shape[2])
    step = min(4, images)
    for start in range(0, images, step):
        total = None
        for a_ref, w_ref in zip(acts, weights):
            term = dot(a_ref[start * pixels : (start + step) * pixels, :], w_ref[...], 1, 0)
            total = term if total is None else total + term
        out_ref[start : start + step] = total.reshape(step, pixels, total.shape[1])
        for i in range(step):
            keep = (first + start + i < info_ref[OWN_COUNT]).astype(F32)
            value = total[i * pixels : (i + 1) * pixels] * keep
            one, two = one + fold(value), two + fold(value * value)
    put_sums(sums_ref, one, two)


def expand_chunk(info, acts, weights, chunk, before, images, plan):
    pixels, cols = plan
    first, share = chunk
    count, mid, out = len(acts), acts[0].shape[1], weights[0].shape[1]
    ins = [info] + list(acts) + list(weights) + ([] if before is None else [before])
    return kernel_call(
        functools.partial(expand_kernel, first, plan, count, mid), "expand", ins,
        [((share, pixels, out), F32), sums_out(first + share == images, out)],
    )


def output_kernel(per_image, count, info_ref, *refs):
    expanded = [[v] for v in refs[:count]]
    in_ref, go_ref, sums_three_ref, par_ref, out_ref, grad_ref, sums_ref = refs[count:]
    average, inv_std = norm_of(sums_three_ref, pixel_count(info_ref, per_image))
    gain, bias = par_ref[0:1, :], par_ref[1:2, :]
    chans = out_ref.shape[2]

    def body(refs, at, image, sums):
        keep = (image < info_ref[OWN_COUNT]).astype(F32)
        normalized = (refs[0][at] - average) * inv_std
        summed = normalized * gain + bias + in_ref[image].astype(F32)
        logistic = sigmoid(summed)
        out_ref[image] = (summed * logistic * keep).astype(BF16)
        slope = logistic * (1.0 + summed * (1.0 - logistic))
        grad = go_ref[image].astype(F32) * (slope * keep)
        grad_ref[image] = grad
        return sums[0] + fold(grad), sums[1] + fold(grad * normalized)

    zero = jnp.zeros((8, chans), F32)
    put_sums(sums_ref, *each_image(expanded, body, (zero, zero)))


def output_pass(info, expanded, field, grad_output, sums_three, params, per_image):
    return kernel_call(
        functools.partial(output_kernel, per_image, len(expanded)), "output",
        [info, *expanded, field, grad_output, sums_three, params],
        [(field.shape, BF16), (field.shape, F32), sums_out(True, field.shape[2])],
    )


def at_image(refs, image):
    for ref in refs:
        if image < ref.shape[0]:
            return ref[image]
        image -= ref.shape[0]


def back_expand_kernel(first, plan, count, mid, fields, per_image, info_ref, *refs):
    pixels, cols = plan
    expanded, refs = refs[:fields], refs[fields:]
    grad_ref, sums_three_ref, grads_ref, par_ref = refs[:4]
    weights = refs[4 : 4 + count]
    out_ref, near_ref, far_ref = refs[-3:]
    total = pixel_count(info_ref, per_image)
    average, inv_std = norm_of(sums_three_ref, total)
    grads = jnp.sum(grads_ref[...], 0)
    scale = inv_std * par_ref[0:1, :]
    bias_part, gain_part = grads[0:1] / total, grads[1:2] / total * inv_std
    for i in range(out_ref.shape[0] // pixels):
        image = first + i
        value = grad_ref[image] - (bias_part + (at_image(expanded, image) - average) * gain_part)
        value = value * (scale * (image < info_ref[OWN_COUNT]).astype(F32))
        out_ref[i * pixels : (i + 1) * pixels, :] = value.astype(BF16)
    for k in range(count):
        term = dot(out_ref[...], weights[k][...], 1, 1)
        to = slice((k // 2) * mid, (k // 2 + 1) * mid)
        if k % 2 == 0:
            near_ref[:, to] = term
        else:
            far_ref[:, to] = term.astype(BF16)


def back_expand_chunk(info, grad_summed, expanded, sums_three, grads_three, params, weights, chunk, mid, plan, per_image):
    pixels, cols = plan
    count, out = len(weights), grad_summed.shape[2]
    block, half = chunk[1] * pixels, count // 2 * mid
    return kernel_call(
        functools.partial(back_expand_kernel, chunk[0], plan, count, mid, len(expanded), per_image), "back_expand",
        [info, *expanded, grad_summed, sums_three, grads_three, params, *weights],
        [((block, out), BF16), ((block, half), F32), ((block, half), BF16)],
        flops=2 * block * mid * count * out,
    )


def pair_sum_kernel(info_ref, near_ref, far_ref, own_ref, *send_refs):
    mid = own_ref.shape[1]
    for k, ref in enumerate((own_ref,) + send_refs):
        at = slice(k * mid, (k + 1) * mid)
        ref[...] = (near_ref[:, at] + far_ref[:, at].astype(F32)).astype(ref.dtype)


def pair_sum(info, near, far, mid):
    rows, half = near.shape
    return kernel_call(
        pair_sum_kernel, "pair_sum", [info, near, far],
        [((rows, mid), F32 if k == 0 else BF16) for k in range(half // mid)],
    )


def slope_two_kernel(first, plan, count, per_image, info_ref, own_ref, *refs):
    pixels, cols = plan
    arrived, refs = refs[:count], refs[count:]
    grp_ref, sums_two_ref, par_ref = refs[:3]
    before_ref = None if len(refs) == 6 else refs[3]
    out_ref, edge_ref, sums_ref = refs[-3:]
    average, inv_std = norm_of(sums_two_ref, pixel_count(info_ref, per_image))
    gain, bias = par_ref[2:3, :], par_ref[3:4, :]
    one, two = before_sums(before_ref, grp_ref.shape[2])
    for i in range(out_ref.shape[0]):
        image = first + i
        at = slice(i * pixels, (i + 1) * pixels)
        grad = own_ref[at, :]
        for ref in arrived:
            grad = grad + ref[at, :].astype(F32)
        normalized = (grp_ref[image] - average) * inv_std
        keep = (image < info_ref[OWN_COUNT]).astype(F32)
        grad = grad * (silu_slope(normalized * gain + bias) * keep)
        out_ref[i] = grad
        edge_ref[i] = edge_rows(info_ref, out_ref, i, cols).astype(BF16)
        one, two = one + fold(grad), two + fold(grad * normalized)
    put_sums(sums_ref, one, two)


def slope_two_chunk(info, own, arrived, grouped, sums_two, params, chunk, before, plan, per_image, staged):
    pixels, cols = plan
    first, share = chunk
    images, mid = grouped.shape[0], grouped.shape[2]
    ins = [info, own] + list(arrived) + [grouped, sums_two, params] + ([] if before is None else [before])
    return kernel_call(
        functools.partial(slope_two_kernel, first, plan, len(arrived), per_image), "slope_two", ins,
        [((share, pixels, mid), F32), ((share, cols, mid), BF16), sums_out(first + share == images and not staged, mid)],
    )


def conv_backward_kernel(
    per_image, group_images, group, d_count, red_count, info_ref, *refs
):
    d_fields, refs = list(zip(refs[:d_count], refs[d_count : 2 * d_count])), refs[2 * d_count :]
    reduced, refs = [[v] for v in refs[:red_count]], refs[red_count:]
    grp_ref, g_edge_ref, act_ref, sums_two_ref, grads_two_ref, sums_one_ref, par_ref, mat_ref = refs[:8]
    out_ref, sums_ref, kernel_ref, window_ref, turned_ref = refs[8:]
    images, pixels, chans = act_ref.shape
    cols = g_edge_ref.shape[1]
    total_pixels = pixel_count(info_ref, per_image)
    avg_two, inv_two = norm_of(sums_two_ref, total_pixels)
    grads = jnp.sum(grads_two_ref[...], 0)
    bias_part, gain_part = grads[0:1] / total_pixels, grads[1:2] / total_pixels * inv_two
    scale_two = inv_two * par_ref[2:3, :]
    avg_one, inv_one = norm_of(sums_one_ref, total_pixels)
    gain_one, bias_one = par_ref[0:1, :], par_ref[1:2, :]

    def input_grad(d, grouped, keep):
        return (d - (bias_part + (grouped - avg_two) * gain_part)) * (scale_two * keep)

    def fill(refs, at, image, nothing):
        keep = (image < info_ref[OWN_COUNT]).astype(F32)
        own = input_grad(refs[0][at], grp_ref[image], keep)
        edge = input_grad(refs[1][at].astype(F32), g_edge_ref[image].astype(F32), keep)
        fill_windows(window_ref, image, with_edges(info_ref, own, edge), cols)
        turned_ref[:, pl.ds(pl.multiple_of(image * pixels, pixels), pixels)] = act_ref[image].T
        return nothing

    def convolve(refs, at, first, sums):
        grad = None
        for i in range(3):
            piece = window_ref[pl.ds(first, group_images), i * cols : i * cols + pixels, :]
            term = dot(piece.reshape(group_images * pixels, 3 * chans), mat_ref[i], 1, 0)
            grad = term if grad is None else grad + term
        one, two = sums
        for i in range(group_images):
            image = first + i
            keep = (image < info_ref[OWN_COUNT]).astype(F32)
            normalized = (refs[0][at + i] - avg_one) * inv_one
            slope = silu_slope(normalized * gain_one + bias_one)
            d_one = grad[i * pixels : (i + 1) * pixels] * (slope * keep)
            out_ref[image] = d_one
            one, two = one + fold(d_one), two + fold(d_one * normalized)
        return one, two

    each_image(d_fields, fill, 0)
    zero = jnp.zeros((8, chans), F32)
    put_sums(sums_ref, *each_image(reduced, convolve, (zero, zero), group_images))
    same = (
        lax.broadcasted_iota(jnp.int32, (chans, 3 * chans), 0) // group
        == lax.broadcasted_iota(jnp.int32, (chans, 3 * chans), 1) % chans // group
    )
    for i in range(3):
        total = None
        for first in range(0, images, group_images):
            piece = window_ref[first : first + group_images, i * cols : i * cols + pixels, :]
            turned = turned_ref[:, first * pixels : (first + group_images) * pixels]
            term = dot(turned, piece.reshape(group_images * pixels, 3 * chans), 1, 0)
            total = term if total is None else total + term
        total = jnp.sum(jnp.where(same, total, 0.0).reshape(chans // group, group, 3 * chans), 0)
        for j in range(3):
            kernel_ref[3 * (2 - i) + 2 - j] = total[:, j * chans : (j + 1) * chans].astype(kernel_ref.dtype)


def conv_backward(info, d_two, d_edges, grouped, g_edge, reduced, acts, sums_two, grads_two, sums_one, params, matrices,
                  group, per_image):
    images, pixels, chans = grouped.shape
    cols = g_edge.shape[1]
    return kernel_call(
        functools.partial(conv_backward_kernel, per_image, 4, group, len(d_two), len(reduced)), "conv_backward",
        [info, *d_two, *d_edges, *reduced, grouped, g_edge, acts, sums_two, grads_two, sums_one, params, matrices],
        [(grouped.shape, F32), sums_out(True, chans), ((9, group, chans), F32)],
        [
            pltpu.VMEM((images, pixels + 2 * cols, 3 * chans), BF16),
            pltpu.VMEM((chans, images * pixels), BF16),
        ],
    )


def grad_reduced_kernel(per_image, count, info_ref, *refs):
    reduced = [[v] for v in refs[:count]]
    d_ref, sums_one_ref, grads_ref, par_ref, out_ref = refs[count:]
    pixels = d_ref.shape[1]
    total = pixel_count(info_ref, per_image)
    average, inv_std = norm_of(sums_one_ref, total)
    grads = jnp.sum(grads_ref[...], 0)
    bias_part, gain_part = grads[0:1] / total, grads[1:2] / total * inv_std
    scale = inv_std * par_ref[0:1, :]

    def body(refs, at, image, nothing):
        value = d_ref[image] - (bias_part + (refs[0][at] - average) * gain_part)
        value = value * (scale * (image < info_ref[OWN_COUNT]).astype(F32))
        out_ref[pl.ds(pl.multiple_of(image * pixels, pixels), pixels), :] = value.astype(BF16)
        return nothing

    each_image(reduced, body, 0)


def grad_reduced(info, d_one, reduced, sums_one, grads_one, params, per_image):
    images, pixels, mid = d_one.shape
    return kernel_call(
        functools.partial(grad_reduced_kernel, per_image, len(reduced)), "grad_reduced",
        [info, *reduced, d_one, sums_one, grads_one, params], [((images * pixels, mid), BF16)],
    )[0]


def input_grad_kernel(count, info_ref, grad_ref, *refs):
    pieces, weights, out_ref = refs[:count], refs[count : 2 * count], refs[-1]
    rows = 512

    def body(step, nothing):
        at = pl.ds(pl.multiple_of(step * rows, rows), rows)
        total = grad_ref[at, :]
        for p_ref, w_ref in zip(pieces, weights):
            total = total + dot(p_ref[at, :], w_ref[...], 1, 1)
        out_ref[at, :] = total.astype(BF16)
        return nothing

    lax.fori_loop(0, grad_ref.shape[0] // rows, body, 0)


def input_grad(info, grad_summed, pieces, weights):
    return kernel_call(
        functools.partial(input_grad_kernel, len(pieces)), "input_grad", [info, grad_summed] + list(pieces) + list(weights),
        [(grad_summed.shape, BF16)],
    )[0]


def cut_columns_kernel(info_ref, in_ref, *refs):
    for k, ref in enumerate(refs):
        part = ref.shape[1]
        ref[...] = in_ref[:, pl.ds(pl.multiple_of((info_ref[CHAN_AT] ^ k) * part, part), part)]


def cut_columns(info, value, count):
    rows, part = value.shape[0], value.shape[1] // count
    return kernel_call(cut_columns_kernel, "cut_columns", [info, value], [((rows, part), BF16)] * count)


def cut_rows_kernel(info_ref, in_ref, *refs):
    for k, ref in enumerate(refs):
        part = ref.shape[0]
        ref[...] = in_ref[pl.ds(pl.multiple_of((info_ref[CHAN_AT] ^ k) * part, part), part), :]


def cut_rows(info, value, count):
    part, cols = value.shape[0] // count, value.shape[1]
    return kernel_call(cut_rows_kernel, "cut_rows", [info, value], [((part, cols), BF16)] * count)


def sum_vectors_kernel(*refs):
    half = len(refs) // 3
    for ref, out_one, out_two in zip(refs[:half], refs[half::2], refs[half + 1 :: 2]):
        sums = jnp.sum(ref[...], 0)
        out_one[...] = sums[0:1]
        out_two[...] = sums[1:2]


def sum_vectors(values):
    outs = [((1, v.shape[2]), F32) for v in values for _ in range(2)]
    return [v.reshape(-1) for v in kernel_call(sum_vectors_kernel, "sum_vectors", list(values), outs)]


REDUCE_STEPS = (("height", 1, HEIGHT_AT), ("batch", 1, NEAR_AT), ("batch", 2, FAR_AT))
EXPAND_STEPS = (("height", 1, HEIGHT_AT), ("batch", 1, NEAR_AT), ("batch", 2, FAR_AT))


def part_of(info_ref, steps):
    number = 0
    for _, _, field in steps:
        number = number * 2 + info_ref[field]
    return number


def send_half(pair, step):
    return pair[0], permute(pair[1], step[0], step[1])


def split(at, keep_ref, send_ref, all_ref, arrived_ref):
    half = keep_ref.shape[0]
    for to, ref in ((at, keep_ref), (1 - at, send_ref)):
        value = all_ref[pl.ds(to * half, half)]
        if arrived_ref is not None:
            value = value + arrived_ref[pl.ds(to * half, half)].astype(F32)
        ref[...] = value.astype(ref.dtype)


def split_first_kernel(make, field, info_ref, *refs):
    keep_ref, send_ref, all_ref = refs[-3:]
    make(refs[:-3], all_ref)
    split(info_ref[field], keep_ref, send_ref, all_ref, None)


def split_first(info, make, step, name, ins, shape):
    half = (shape[0] // 2,) + shape[1:]
    return kernel_call(
        functools.partial(split_first_kernel, make, step[2]), name, [info] + ins, [(half, F32), (half, BF16)],
        [pltpu.VMEM(shape, F32)],
    )


def split_next_kernel(field, info_ref, keep_ref, arrived_ref, out_ref, send_ref):
    split(info_ref[field], out_ref, send_ref, keep_ref, arrived_ref)


def split_next(info, pair, step):
    half = (pair[0].shape[0] // 2,) + pair[0].shape[1:]
    return kernel_call(
        functools.partial(split_next_kernel, step[2]), "split_next", [info, *pair], [(half, F32), (half, BF16)]
    )


def add_kernel(info_ref, first_ref, second_ref, out_ref):
    out_ref[...] = (first_ref[...] + second_ref[...].astype(F32)).astype(BF16)


def add_last(info, pair):
    return kernel_call(add_kernel, "add_last", [info, *pair], [(pair[0].shape, BF16)])[0]


def join_kernel(info_ref, *refs):
    size = refs[0].shape[0]
    for k, ref in enumerate(refs[:-1]):
        refs[-1][k * size : (k + 1) * size] = ref[...]


def join(info, *values):
    shape = (values[0].shape[0] * len(values),) + values[0].shape[1:]
    return kernel_call(join_kernel, "join", [info, *values], [(shape, BF16)])[0]


def send_back(value, step):
    return value, permute(value, step[0], step[1])


def reduce_grad_make(places, spans, extra, refs, all_ref):
    grad_ref = refs[places * len(spans)]
    parts = all_ref.shape[0]
    per = parts // places
    for k in range(places):
        total = None
        for c, (first, end) in enumerate(spans):
            term = dot(refs[k * len(spans) + c][...], grad_ref[first:end, :], 0, 0)
            total = term if total is None else total + term
        size = total.shape[0] // per
        all_ref[k * per : (k + 1) * per, 0:size, :] = total.reshape(per, size, total.shape[1])
    if extra:
        more = refs[-1][...]
        more = more.reshape(-1, more.shape[2])
        room = parts * extra - more.shape[0]
        more = jnp.concatenate([more, jnp.zeros((room, more.shape[1]), F32)], 0)
        all_ref[:, size : size + extra, :] = more.reshape(parts, extra, more.shape[1])


def reduce_grad(info, inputs, grad, parts, more):
    spans = spans_of(inputs[0])
    rows, mid = len(inputs) * inputs[0][0].shape[1], grad.shape[1]
    extra = 0 if more is None else -(-more.shape[0] * more.shape[1] // (8 * parts)) * 8
    ins = [v for piece in inputs for v in piece] + [grad] + ([] if more is None else [more])
    return split_first(
        info, functools.partial(reduce_grad_make, len(inputs), tuple(spans), extra), REDUCE_STEPS[0], "reduce_grad", ins,
        (parts, rows // parts + extra, mid),
    )


def spans_of(values):
    spans, at = [], 0
    for value in values:
        spans.append((at, at + value.shape[0]))
        at += value.shape[0]
    return spans


def expand_grad_make(count, chunks, refs, all_ref):
    acts, grads = refs[: count * chunks], refs[count * chunks :]
    parts, wide, out = all_ref.shape
    size = wide // count
    for k in range(count):
        total = None
        own = acts[k * chunks : (k + 1) * chunks]
        for a_ref, (a_first, a_end) in zip(own, spans_of(own)):
            for g_ref, (g_first, g_end) in zip(grads, spans_of(grads)):
                first, end = max(a_first, g_first), min(a_end, g_end)
                if first < end:
                    term = dot(a_ref[first - a_first : end - a_first, :], g_ref[first - g_first : end - g_first, :], 0, 0)
                    total = term if total is None else total + term
        all_ref[:, k * size : (k + 1) * size, :] = total.reshape(parts, size, out)


def expand_grad(info, acts, grads, parts):
    count, mid, out = len(acts), acts[0][0].shape[1], grads[0].shape[1]
    return split_first(
        info, functools.partial(expand_grad_make, count, len(acts[0])), EXPAND_STEPS[0], "expand_grad",
        [a for piece in acts for a in piece] + list(grads), (parts, count * mid // parts, out),
    )


def cut_places_kernel(info_ref, keep_ref, arrived_ref, *refs):
    size = refs[0].shape[0]
    total = (keep_ref[0] + arrived_ref[0].astype(F32)).astype(BF16)
    for k, ref in enumerate(refs):
        ref[...] = total[k * size : (k + 1) * size, :]


def cut_places(info, pair, count):
    rows, out = pair[0].shape[1:]
    return kernel_call(cut_places_kernel, "cut_places", [info, *pair], [((rows // count, out), BF16)] * count)


def place_reduce_kernel(count, info_ref, *refs):
    out_ref, group_ref, more_ref = refs[4:]
    me, number = info_ref[CHAN_AT], part_of(info_ref, REDUCE_STEPS)
    part = out_ref.shape[0] // count
    batches = refs[0].shape[0]
    size = refs[2].shape[1]
    extra = refs[0].shape[1] - size
    for half in range(2):
        for other in range(2):
            ref = refs[2 * half + other]
            for k in range(batches):
                at = number ^ (other * batches + k)
                row = at * size
                to = (me ^ (half * (count // 2) + row // part)) * part + row % part
                out_ref[pl.ds(pl.multiple_of(to, size), size), :] = ref[k, 0:size, :].astype(F32)
                if half == 0:
                    more_ref[pl.ds(pl.multiple_of(at * extra, 8), extra), :] = ref[k, size:, :].astype(F32)
    group_ref[...] = more_ref[0 : group_ref.shape[0], :]


def place_reduce(info, halves, count, part, group_rows):
    batches, rows, mid = halves[0][0].shape
    extra = rows - halves[1][0].shape[1]
    return kernel_call(
        functools.partial(place_reduce_kernel, count), "place_reduce", [info] + [v for pair in halves for v in pair],
        [((part * count, mid), F32), ((group_rows, mid), F32)], [pltpu.VMEM((2 * batches * extra, mid), F32)],
    )


def place_expand_kernel(count, info_ref, own_ref, arrived_ref, out_ref):
    me, number = info_ref[CHAN_AT], part_of(info_ref, EXPAND_STEPS)
    batches, rows, out = own_ref.shape
    size = rows // count
    for other, ref in enumerate((own_ref, arrived_ref)):
        for k in range(batches):
            row = (number ^ (other * batches + k)) * size
            for place in range(count):
                to = pl.ds(pl.multiple_of((me ^ place) * out, out), out)
                out_ref[pl.ds(pl.multiple_of(row, size), size), to] = ref[k, place * size : (place + 1) * size, :].astype(F32)


def place_expand(info, pair, count, mid):
    out = pair[0].shape[2]
    return kernel_call(
        functools.partial(place_expand_kernel, count), "place_expand", [info] + list(pair), [((mid, out * count), F32)]
    )[0]


def plain_weight_grads(inputs, grad, acts, grad_expanded, grad_group):
    count, me = len(inputs), lax.axis_index("chan")
    part, mid = inputs[0][0].shape[1], grad.shape[1]
    grad_reduce = jnp.zeros((part * count, mid), BF16)
    grad_expand = jnp.zeros((mid, part * count), BF16)
    for k in range(count):
        block = dot(jnp.concatenate(inputs[k], 0), grad, 0, 0).astype(BF16)
        grad_reduce = lax.dynamic_update_slice(grad_reduce, block, ((me ^ k) * part, 0))
        block = dot(jnp.concatenate(acts[k], 0), jnp.concatenate(grad_expanded, 0), 0, 0).astype(BF16)
        block = swap(block, k) if k else block
        grad_expand = lax.dynamic_update_slice(grad_expand, block, (0, (me ^ k) * part))
    return [lax.psum(v, REDUCE_AXES).astype(F32) for v in (grad_reduce, grad_expand, grad_group.astype(BF16))]


def shards(
    block_input, w_reduce, w_group, w_expand, gain_one, bias_one, gain_two, bias_two,
    gain_three, bias_three, image_counts, grad_output,
):
    chan_size = lax.axis_size("chan")
    me = lax.axis_index("chan")
    height_at = lax.axis_index("height")
    images, rows, cols, out_part = block_input.shape
    mid_part, group = w_group.shape[3], w_group.shape[2]
    pixels = rows * cols
    per_image = float(pixels * lax.axis_size("height"))
    plan = (pixels, cols)
    distances = range(2, chan_size, 2)
    own_count = jnp.sum(
        jnp.where(jnp.arange(image_counts.shape[0]) == lax.axis_index("batch"), image_counts, 0)
    )
    batch_at = lax.axis_index("batch")
    info = jnp.stack(
        [
            own_count, jnp.sum(image_counts), height_at, me, jnp.where(height_at == 0, pixels - cols, 0),
            batch_at & 1, (batch_at >> 1) & 1,
        ]
    ).astype(jnp.int32)
    parts = lax.axis_size(REDUCE_AXES)
    staged = (lax.axis_size("height"), lax.axis_size("batch")) == (2, 4)

    def edge_swap(edge):
        return permute(edge, "height", 1)

    def sums_of(sums, *waits):
        return staged_sums(sums, *waits) if staged else spread_sums(sums)

    def gather(value, *waits):
        pieces = [value, swap(value, 1)]
        for k in distances:
            pieces.append(swap(value, k))
            pieces.append(swap(after(pieces[k], *waits) if waits else pieces[k], 1))
        return pieces

    field = block_input.reshape(images * pixels, out_part)
    matrices, matrices_back, mid_params, out_params = prepare(
        info, w_group, (gain_one, bias_one, gain_two, bias_two), (gain_three, bias_three)
    )
    columns = cut_columns(info, w_expand, chan_size)
    rows_back = cut_rows(info, w_reduce, chan_size)
    weights = [columns[0], swap(columns[1], 1)]
    reduce_back = [rows_back[0], swap(rows_back[1], 1)]
    inputs = []
    for first, share in cut_images(REDUCE_CHUNKS):
        source = after(field, inputs[0][0], info) if first else field
        piece = lax.slice_in_dim(source, first * pixels, (first + share) * pixels)
        inputs.append(gather(piece, mid_params, weights[1], reduce_back[1]) if first else gather(piece))
    reduced, red_edges, sums = [], [], None
    for pieces, (first, share) in zip(inputs, cut_images(REDUCE_CHUNKS)):
        red, edge, sums = reduce_chunk(info, pieces, (first, share), w_reduce, sums, images, plan, False)
        reduced.append(red)
        red_edges.append(edge_swap(edge))
    inputs = [list(chunks) for chunks in zip(*inputs)]
    weights += [swap(after(columns[k], inputs[2][-1]), k) for k in range(2, chan_size)]
    sums_one = spread_sums(after(sums, *weights[2:]))

    acts_one, grouped, grp_edge, sums = conv_forward(
        info, reduced, red_edges, sums_one, mid_params, matrices, per_image
    )
    sums_two = spread_sums(sums)

    acts = []
    for chunk in cut_images(EXPAND_CHUNKS):
        acts.append(gather(act_two_chunk(info, grouped, sums_two, mid_params, chunk, plan, per_image)))
    expanded, sums = [], None
    for pieces, chunk in zip(acts, cut_images(EXPAND_CHUNKS)):
        out, sums = expand_chunk(info, pieces, weights, chunk, sums, images, plan)
        expanded.append(out)
    acts = [list(chunks) for chunks in zip(*acts)]
    sums_three = spread_sums(sums)
    output, grad_summed, sums = output_pass(
        info, expanded, field.reshape(images, pixels, out_part), grad_output.reshape(images, pixels, out_part), sums_three,
        out_params, per_image,
    )
    grads_three = spread_sums(sums)

    grad_expanded, halves = [], []
    for chunk in cut_images(BACK_CHUNKS):
        grad, near, far = back_expand_chunk(
            info, grad_summed, expanded, sums_three, grads_three, out_params, weights, chunk, mid_part, plan, per_image
        )
        grad_expanded.append(grad)
        halves.append((near, swap(far, 1)))
    own, sent = [], []
    for near, far in halves:
        summed = pair_sum(info, near, far, mid_part)
        own.append(summed[0])
        sent.append([swap(value, k) for value, k in zip(summed[1:], distances)])
    grp_edge = edge_swap(after(grp_edge, own[0]))
    if staged:
        expand_pair = send_half(expand_grad(info, acts, grad_expanded, parts), EXPAND_STEPS[0])
    d_two, d_edges, sums, turn = [], [], None, info
    for c, chunk in enumerate(cut_images(BACK_CHUNKS)):
        if staged and c == 1:
            pair = split_next(after(info, d_two[0]), expand_pair, EXPAND_STEPS[1])
            turn = after(info, pair[0])
            expand_pair = send_half(pair, EXPAND_STEPS[1])
        grad, edge, sums = slope_two_chunk(
            turn, own[c], sent[c], grouped, sums_two, mid_params, chunk, sums, plan, per_image, staged
        )
        d_two.append(grad)
        d_edges.append(edge_swap(edge))
    grads_two = sums_of(sums, grp_edge, *d_edges)
    turn = info
    if staged:
        pair = split_next(after(info, grads_two), expand_pair, EXPAND_STEPS[2])
        turn = after(info, pair[0])
        expand_pair = send_half(pair, EXPAND_STEPS[2])

    d_one, sums, grad_group = conv_backward(
        turn, d_two, d_edges, grouped, grp_edge, reduced, acts_one, sums_two, grads_two, sums_one, mid_params,
        matrices_back, group, per_image,
    )
    if staged:
        places = cut_places(after(info, d_one), expand_pair, chan_size)
        sums = after(sums, places[0])
    grads_one = spread_sums(sums)

    grad = grad_reduced(info, d_one, reduced, sums_one, grads_one, mid_params, per_image)
    grad_field = grad_summed.reshape(images * pixels, out_part)
    if staged:
        half = chan_size // 2
        pairs, turn = [], after(info, grad)

        def in_turn(call, *args):
            nonlocal turn
            result = call(turn, *args)
            turn = after(info, result[0] if isinstance(result, (list, tuple)) else result)
            return result

        def first_half(i):
            own = inputs[i * half : (i + 1) * half]
            pair = in_turn(reduce_grad, own, grad, parts, None if i else grad_group)
            pairs.append(send_half(pair, REDUCE_STEPS[0]))

        def next_half(i, step):
            pairs[i] = send_half(in_turn(split_next, pairs[i], REDUCE_STEPS[step]), REDUCE_STEPS[step])

        def last_half(i):
            pairs[i] = send_back(in_turn(add_last, pairs[i]), REDUCE_STEPS[2])

        def back_half(i, step):
            pairs[i] = send_back(in_turn(join, *pairs[i]), REDUCE_STEPS[step])

        first_half(0)
        first_half(1)
        places = [v if k == 0 else swap(after(v, turn), k) for k, v in enumerate(places)]
        back = in_turn(join, *places)
        back = send_back(back.reshape((1,) + back.shape), EXPAND_STEPS[2])
        far_grads = [swap(after(grad, turn), k) for k in distances]
        next_half(0, 1)
        next_half(1, 1)
        back = send_back(in_turn(join, *back), EXPAND_STEPS[1])
        next_half(0, 2)
        next_half(1, 2)
        back = send_back(in_turn(join, *back), EXPAND_STEPS[0])
        last_half(0)
        last_half(1)
        grads = [grad, swap(after(grad, turn), 1)]
        for value in far_grads:
            grads += [value, swap(after(value, turn), 1)]
        reduce_back += [swap(after(rows_back[k], turn), k) for k in range(2, chan_size)]
        back_half(0, 1)
        grad_input = in_turn(input_grad, grad_field, grads, reduce_back)
        back_half(1, 1)
        back_half(0, 0)
        grad_expand = in_turn(place_expand, back, chan_size, mid_part)
        back_half(1, 0)
        grad_reduce, grad_group = place_reduce(turn, pairs, chan_size, out_part, 9 * group)
    else:
        reduce_back += [swap(rows_back[k], k) for k in range(2, chan_size)]
        grad_input = input_grad(info, grad_field, gather(grad), reduce_back)
        grad_reduce, grad_expand, grad_group = plain_weight_grads(inputs, grad, acts, grad_expanded, grad_group)
    vectors = sum_vectors([grads_one, grads_two, grads_three])
    return (
        output.reshape(block_input.shape), grad_input.reshape(block_input.shape), grad_reduce,
        grad_group.reshape(w_group.shape), grad_expand,
        vectors[1], vectors[0], vectors[3], vectors[2], vectors[5], vectors[4],
    )


def solution(mesh):
    split = P("batch", "height", None, "chan")
    vector = P("chan")
    return jax.shard_map(
        shards,
        mesh=mesh,
        in_specs=(
            split, P(None, "chan"), P(None, None, None, "chan"), P("chan", None),
            vector, vector, vector, vector, vector, vector, P(), split,
        ),
        out_specs=(
            split, split, P(None, "chan"), P(None, None, None, "chan"), P("chan", None),
            vector, vector, vector, vector, vector, vector,
        ),
        check_vma=False,
    )
```

```python
import functools

import jax
import jax.numpy as jnp
from jax import lax
from jax.experimental import pallas as pl
from jax.experimental.pallas import tpu as pltpu
from jax.sharding import PartitionSpec as P

EPSILON = 1e-05
F32, BF16 = jnp.float32, jnp.bfloat16
REDUCE_AXES = ("height", "batch")
REDUCE_CHUNKS, EXPAND_CHUNKS, BACK_CHUNKS = (8, 8), (8, 8), (8, 8)
OWN_COUNT, TOTAL_COUNT, HEIGHT_AT, CHAN_AT, EDGE_ROW, NEAR_AT, FAR_AT = range(7)
VMEM = pl.BlockSpec(memory_space=pltpu.VMEM)
SMEM = pl.BlockSpec(memory_space=pltpu.SMEM)


def dot(a, b, left, right):
    return lax.dot_general(a, b, (((left,), (right,)), ((), ())), preferred_element_type=F32)


def kernel_call(body, name, ins, outs, scratch=(), alias=None, flops=0, room=16):
    return pl.pallas_call(
        body,
        in_specs=[SMEM if a.dtype == jnp.int32 else VMEM for a in ins],
        out_specs=[VMEM] * len(outs),
        out_shape=[jax.ShapeDtypeStruct(shape, dtype) for shape, dtype in outs],
        scratch_shapes=list(scratch),
        input_output_aliases=alias or {},
        compiler_params=pltpu.CompilerParams(vmem_limit_bytes=room << 20),
        cost_estimate=pl.CostEstimate(flops=flops, bytes_accessed=0, transcendentals=0),
        name=name,
    )(*ins)


def after(value, *others):
    return lax.optimization_barrier((value,) + others)[0]


def permute(value, axis, distance):
    count = lax.axis_size(axis)
    return lax.ppermute(value, axis, [(i, i ^ distance) for i in range(count)])


def swap(value, distance):
    return permute(value, "chan", distance)


def spread_sums(sent):
    return lax.all_to_all(sent, REDUCE_AXES, 0, 0)


def staged_sums(partial, *waits):
    chans = partial.shape[2]
    both = kernel_call(
        add_rows_kernel, "add_rows", [after(partial, *waits), permute(partial, "height", 1)], [((2, chans), F32)]
    )[0]
    others = [permute(both, "batch", k) for k in range(1, lax.axis_size("batch"))]
    return kernel_call(add_sums_kernel, "add_sums", [both] + others, [((1, 2, chans), F32)])[0]


def add_rows_kernel(own_ref, other_ref, out_ref):
    out_ref[...] = jnp.sum(own_ref[...] + other_ref[...], 1)


def add_sums_kernel(*refs):
    total = refs[0][...]
    for ref in refs[1:-1]:
        total = total + ref[...]
    refs[-1][0] = total


def norm_of(sums_ref, total):
    sums = jnp.sum(sums_ref[...], 0)
    average = sums[0:1] / total
    return average, lax.rsqrt(sums[1:2] / total - average * average + EPSILON)


def pixel_count(info_ref, per_image):
    return info_ref[TOTAL_COUNT].astype(F32) * per_image


def sigmoid(v):
    return 0.5 * jnp.tanh(0.5 * v) + 0.5


def silu_slope(v):
    logistic = sigmoid(v)
    return logistic * (1.0 + v * (1.0 - logistic))


def fold(values):
    rows, chans = values.shape
    return jnp.sum(values.reshape(rows // 8, 8, chans), 0)


def put_sums(out_ref, one, two):
    if out_ref.shape[1] == 8:
        out_ref[0] = one
        out_ref[1] = two
    else:
        both = jnp.concatenate([jnp.sum(one, 0, keepdims=True), jnp.sum(two, 0, keepdims=True)], 0)
        out_ref[...] = jnp.broadcast_to(both[None], out_ref.shape)


def sums_out(last, chans):
    return ((lax.axis_size(REDUCE_AXES), 2, chans) if last else (2, 8, chans), F32)


def before_sums(before_ref, chans):
    if before_ref is None:
        zero = jnp.zeros((8, chans), F32)
        return zero, zero
    return before_ref[0], before_ref[1]


def edge_rows(info_ref, ref, image, cols):
    return ref[image, pl.ds(pl.multiple_of(info_ref[EDGE_ROW], 16), cols), :]


def prepare_kernel(group, info_ref, taps_ref, mid_a, mid_b, mid_c, mid_d, out_a, out_b, fwd_ref, back_ref, mid_ref, out_ref):
    chans = taps_ref.shape[2]
    same = (
        lax.broadcasted_iota(jnp.int32, (chans, chans), 0) // group
        == lax.broadcasted_iota(jnp.int32, (chans, chans), 1) // group
    )
    for i in range(3):
        for j in range(3):
            wide = jnp.concatenate([taps_ref[3 * i + j].astype(F32)] * (chans // group), 0)
            wide = jnp.where(same, wide, 0.0)
            fwd_ref[i, j * chans : (j + 1) * chans, :] = wide.astype(BF16)
            back_ref[2 - i, (2 - j) * chans : (3 - j) * chans, :] = wide.T.astype(BF16)
    for row, ref in enumerate((mid_a, mid_b, mid_c, mid_d)):
        mid_ref[row : row + 1, :] = ref[...].astype(F32)
    for row, ref in enumerate((out_a, out_b)):
        out_ref[row : row + 1, :] = ref[...].astype(F32)


def prepare(info, kernel, mid_vectors, out_vectors):
    group, chans = kernel.shape[2], kernel.shape[3]
    wide = (3, 3 * chans, chans)
    rows = [v.reshape(1, -1) for v in list(mid_vectors) + list(out_vectors)]
    return kernel_call(
        functools.partial(prepare_kernel, group), "prepare", [info, kernel.reshape(9, group, chans)] + rows,
        [(wide, BF16), (wide, BF16), ((4, chans), F32), ((2, rows[-1].shape[1]), F32)],
    )


def cut_images(shares):
    return [(sum(shares[:i]), share) for i, share in enumerate(shares)]


def reduce_kernel(first, plan, count, info_ref, *refs):
    pixels, cols = plan
    pieces, w_ref, before_ref = refs[:count], refs[count], None if len(refs) == count + 4 else refs[count + 1]
    red_ref, edge_ref, sums_ref = refs[-3:]
    me = info_ref[CHAN_AT]
    part, images = pieces[0].shape[1], red_ref.shape[0]
    one, two = before_sums(before_ref, w_ref.shape[1])
    step = min(4, images)
    for start in range(0, images, step):
        total = None
        for k in range(count):
            rows = w_ref[pl.ds(pl.multiple_of((me ^ k) * part, part), part), :]
            term = dot(pieces[k][start * pixels : (start + step) * pixels, :], rows, 1, 0)
            total = term if total is None else total + term
        for i in range(start, start + step):
            value = total[(i - start) * pixels : (i - start + 1) * pixels]
            red_ref[i] = value
            edge_ref[i] = edge_rows(info_ref, red_ref, i, cols).astype(BF16)
            value = value * (first + i < info_ref[OWN_COUNT]).astype(F32)
            one, two = one + fold(value), two + fold(value * value)
    put_sums(sums_ref, one, two)


def reduce_chunk(info, pieces, chunk, w_reduce, before, images, plan, staged):
    pixels, cols = plan
    first, share = chunk
    count, mid = len(pieces), w_reduce.shape[1]
    ins = [info] + list(pieces) + [w_reduce] + ([] if before is None else [before])
    return kernel_call(
        functools.partial(reduce_kernel, first, plan, count), "reduce", ins,
        [((share, pixels, mid), F32), ((share, cols, mid), BF16), sums_out(first + share == images and not staged, mid)],
        flops=2 * pieces[0].size * count * mid,
    )


def each_image(chunks, body, carry, step=1):
    first = 0
    for refs in chunks:
        count = refs[0].shape[0]
        start = first
        carry = lax.fori_loop(
            0, count // step, lambda i, c, refs=refs, start=start: body(refs, i * step, start + i * step, c), carry
        )
        first += count
    return carry


def fill_windows(window_ref, slot, value, cols):
    rows, chans = value.shape
    place = lax.broadcasted_iota(jnp.int32, value.shape, 0) % cols
    left = jnp.where(place == 0, 0.0, pltpu.roll(value, 1, 0))
    right = jnp.where(place == cols - 1, 0.0, pltpu.roll(value, rows - 1, 0))
    window_ref[slot, :, 0:chans] = left.astype(BF16)
    window_ref[slot, :, chans : 2 * chans] = value.astype(BF16)
    window_ref[slot, :, 2 * chans : 3 * chans] = right.astype(BF16)


def with_edges(info_ref, own, edge):
    low = (info_ref[HEIGHT_AT] > 0).astype(F32)
    return jnp.concatenate([edge * low, own, edge * (1.0 - low)], 0)


def conv_forward_kernel(
    per_image, group_images, count, info_ref, *refs
):
    fields = list(zip(refs[:count], refs[count : 2 * count]))
    sums_one_ref, par_ref, mat_ref, act_ref, out_ref, out_edge_ref, sums_ref, window_ref = refs[2 * count :]
    images, pixels, chans = act_ref.shape
    cols = out_edge_ref.shape[1]
    average, inv_std = norm_of(sums_one_ref, pixel_count(info_ref, per_image))
    scale, bias = inv_std * par_ref[0:1, :], par_ref[1:2, :]

    def activate(v, keep):
        pre = (v - average) * scale + bias
        return pre * sigmoid(pre) * keep

    def fill(refs, at, image, nothing):
        keep = (image < info_ref[OWN_COUNT]).astype(F32)
        own = activate(refs[0][at], keep)
        edge = activate(refs[1][at].astype(F32), keep)
        act_ref[image] = own.astype(BF16)
        fill_windows(window_ref, image, with_edges(info_ref, own, edge), cols)
        return nothing

    def convolve(step, sums):
        first = step * group_images
        total = None
        for i in range(3):
            piece = window_ref[pl.ds(first, group_images), i * cols : i * cols + pixels, :]
            term = dot(piece.reshape(group_images * pixels, 3 * chans), mat_ref[i], 1, 0)
            total = term if total is None else total + term
        out_ref[pl.ds(first, group_images)] = total.reshape(group_images, pixels, chans)
        for i in range(group_images):
            out_edge_ref[first + i] = edge_rows(info_ref, out_ref, first + i, cols).astype(BF16)
        return sums[0] + fold(total), sums[1] + fold(total * total)

    each_image(fields, fill, 0)
    zero = jnp.zeros((8, chans), F32)
    put_sums(sums_ref, *lax.fori_loop(0, images // group_images, convolve, (zero, zero)))


def conv_forward(info, reduced, edges, sums_one, params, matrices, per_image):
    images = sum(v.shape[0] for v in reduced)
    pixels, chans = reduced[0].shape[1:]
    cols = edges[0].shape[1]
    shape = (images, pixels, chans)
    return kernel_call(
        functools.partial(conv_forward_kernel, per_image, 4, len(reduced)), "conv_forward",
        [info, *reduced, *edges, sums_one, params, matrices],
        [(shape, BF16), (shape, F32), ((images, cols, chans), BF16), sums_out(True, chans)],
        [pltpu.VMEM((images, pixels + 2 * cols, 3 * chans), BF16)],
    )


def act_two_kernel(chunk, plan, per_image, info_ref, grp_ref, sums_ref, par_ref, out_ref):
    pixels, cols = plan
    first, images = chunk
    average, inv_std = norm_of(sums_ref, pixel_count(info_ref, per_image))
    scale, bias = inv_std * par_ref[2:3, :], par_ref[3:4, :]
    for i in range(images):
        image = first + i
        pre = (grp_ref[image] - average) * scale + bias
        act = pre * sigmoid(pre) * (image < info_ref[OWN_COUNT]).astype(F32)
        out_ref[i * pixels : (i + 1) * pixels] = act.astype(BF16)


def act_two_chunk(info, grouped, sums_two, params, chunk, plan, per_image):
    pixels, cols = plan
    shape = (chunk[1] * pixels, grouped.shape[2])
    return kernel_call(
        functools.partial(act_two_kernel, chunk, plan, per_image), "act_two",
        [info, grouped, sums_two, params], [(shape, BF16)],
    )[0]


def expand_kernel(first, plan, count, mid, info_ref, *refs):
    pixels, cols = plan
    acts, weights = refs[:count], refs[count : 2 * count]
    before_ref = None if len(refs) == 2 * count + 2 else refs[2 * count]
    out_ref, sums_ref = refs[-2:]
    images = out_ref.shape[0]
    one, two = before_sums(before_ref, out_ref.shape[2])
    step = min(4, images)
    for start in range(0, images, step):
        total = None
        for a_ref, w_ref in zip(acts, weights):
            term = dot(a_ref[start * pixels : (start + step) * pixels, :], w_ref[...], 1, 0)
            total = term if total is None else total + term
        out_ref[start : start + step] = total.reshape(step, pixels, total.shape[1])
        for i in range(step):
            keep = (first + start + i < info_ref[OWN_COUNT]).astype(F32)
            value = total[i * pixels : (i + 1) * pixels] * keep
            one, two = one + fold(value), two + fold(value * value)
    put_sums(sums_ref, one, two)


def expand_chunk(info, acts, weights, chunk, before, images, plan):
    pixels, cols = plan
    first, share = chunk
    count, mid, out = len(acts), acts[0].shape[1], weights[0].shape[1]
    ins = [info] + list(acts) + list(weights) + ([] if before is None else [before])
    return kernel_call(
        functools.partial(expand_kernel, first, plan, count, mid), "expand", ins,
        [((share, pixels, out), F32), sums_out(first + share == images, out)],
    )


def output_kernel(per_image, count, info_ref, *refs):
    expanded = [[v] for v in refs[:count]]
    in_ref, go_ref, sums_three_ref, par_ref, out_ref, grad_ref, sums_ref = refs[count:]
    average, inv_std = norm_of(sums_three_ref, pixel_count(info_ref, per_image))
    gain, bias = par_ref[0:1, :], par_ref[1:2, :]
    chans = out_ref.shape[2]

    def body(refs, at, image, sums):
        keep = (image < info_ref[OWN_COUNT]).astype(F32)
        normalized = (refs[0][at] - average) * inv_std
        summed = normalized * gain + bias + in_ref[image].astype(F32)
        logistic = sigmoid(summed)
        out_ref[image] = (summed * logistic * keep).astype(BF16)
        slope = logistic * (1.0 + summed * (1.0 - logistic))
        grad = go_ref[image].astype(F32) * (slope * keep)
        grad_ref[image] = grad
        return sums[0] + fold(grad), sums[1] + fold(grad * normalized)

    zero = jnp.zeros((8, chans), F32)
    put_sums(sums_ref, *each_image(expanded, body, (zero, zero)))


def output_pass(info, expanded, field, grad_output, sums_three, params, per_image):
    return kernel_call(
        functools.partial(output_kernel, per_image, len(expanded)), "output",
        [info, *expanded, field, grad_output, sums_three, params],
        [(field.shape, BF16), (field.shape, F32), sums_out(True, field.shape[2])],
    )


def at_image(refs, image):
    for ref in refs:
        if image < ref.shape[0]:
            return ref[image]
        image -= ref.shape[0]


def back_expand_kernel(first, plan, count, mid, fields, per_image, info_ref, *refs):
    pixels, cols = plan
    expanded, refs = refs[:fields], refs[fields:]
    grad_ref, sums_three_ref, grads_ref, par_ref = refs[:4]
    weights = refs[4 : 4 + count]
    out_ref, near_ref, far_ref = refs[-3:]
    total = pixel_count(info_ref, per_image)
    average, inv_std = norm_of(sums_three_ref, total)
    grads = jnp.sum(grads_ref[...], 0)
    scale = inv_std * par_ref[0:1, :]
    bias_part, gain_part = grads[0:1] / total, grads[1:2] / total * inv_std
    for i in range(out_ref.shape[0] // pixels):
        image = first + i
        value = grad_ref[image] - (bias_part + (at_image(expanded, image) - average) * gain_part)
        value = value * (scale * (image < info_ref[OWN_COUNT]).astype(F32))
        out_ref[i * pixels : (i + 1) * pixels, :] = value.astype(BF16)
    for k in range(count):
        term = dot(out_ref[...], weights[k][...], 1, 1)
        to = slice((k // 2) * mid, (k // 2 + 1) * mid)
        if k % 2 == 0:
            near_ref[:, to] = term
        else:
            far_ref[:, to] = term.astype(BF16)


def back_expand_chunk(info, grad_summed, expanded, sums_three, grads_three, params, weights, chunk, mid, plan, per_image):
    pixels, cols = plan
    count, out = len(weights), grad_summed.shape[2]
    block, half = chunk[1] * pixels, count // 2 * mid
    return kernel_call(
        functools.partial(back_expand_kernel, chunk[0], plan, count, mid, len(expanded), per_image), "back_expand",
        [info, *expanded, grad_summed, sums_three, grads_three, params, *weights],
        [((block, out), BF16), ((block, half), F32), ((block, half), BF16)],
        flops=2 * block * mid * count * out,
    )


def pair_sum_kernel(info_ref, near_ref, far_ref, own_ref, *send_refs):
    mid = own_ref.shape[1]
    for k, ref in enumerate((own_ref,) + send_refs):
        at = slice(k * mid, (k + 1) * mid)
        ref[...] = (near_ref[:, at] + far_ref[:, at].astype(F32)).astype(ref.dtype)


def pair_sum(info, near, far, mid):
    rows, half = near.shape
    return kernel_call(
        pair_sum_kernel, "pair_sum", [info, near, far],
        [((rows, mid), F32 if k == 0 else BF16) for k in range(half // mid)],
    )


def slope_two_kernel(first, plan, count, per_image, info_ref, own_ref, *refs):
    pixels, cols = plan
    arrived, refs = refs[:count], refs[count:]
    grp_ref, sums_two_ref, par_ref = refs[:3]
    before_ref = None if len(refs) == 6 else refs[3]
    out_ref, edge_ref, sums_ref = refs[-3:]
    average, inv_std = norm_of(sums_two_ref, pixel_count(info_ref, per_image))
    gain, bias = par_ref[2:3, :], par_ref[3:4, :]
    one, two = before_sums(before_ref, grp_ref.shape[2])
    for i in range(out_ref.shape[0]):
        image = first + i
        at = slice(i * pixels, (i + 1) * pixels)
        grad = own_ref[at, :]
        for ref in arrived:
            grad = grad + ref[at, :].astype(F32)
        normalized = (grp_ref[image] - average) * inv_std
        keep = (image < info_ref[OWN_COUNT]).astype(F32)
        grad = grad * (silu_slope(normalized * gain + bias) * keep)
        out_ref[i] = grad
        edge_ref[i] = edge_rows(info_ref, out_ref, i, cols).astype(BF16)
        one, two = one + fold(grad), two + fold(grad * normalized)
    put_sums(sums_ref, one, two)


def slope_two_chunk(info, own, arrived, grouped, sums_two, params, chunk, before, plan, per_image, staged):
    pixels, cols = plan
    first, share = chunk
    images, mid = grouped.shape[0], grouped.shape[2]
    ins = [info, own] + list(arrived) + [grouped, sums_two, params] + ([] if before is None else [before])
    return kernel_call(
        functools.partial(slope_two_kernel, first, plan, len(arrived), per_image), "slope_two", ins,
        [((share, pixels, mid), F32), ((share, cols, mid), BF16), sums_out(first + share == images and not staged, mid)],
    )


def conv_backward_kernel(
    per_image, group_images, group, d_count, red_count, info_ref, *refs
):
    d_fields, refs = list(zip(refs[:d_count], refs[d_count : 2 * d_count])), refs[2 * d_count :]
    reduced, refs = [[v] for v in refs[:red_count]], refs[red_count:]
    grp_ref, g_edge_ref, act_ref, sums_two_ref, grads_two_ref, sums_one_ref, par_ref, mat_ref = refs[:8]
    out_ref, sums_ref, kernel_ref, window_ref, turned_ref = refs[8:]
    images, pixels, chans = act_ref.shape
    cols = g_edge_ref.shape[1]
    total_pixels = pixel_count(info_ref, per_image)
    avg_two, inv_two = norm_of(sums_two_ref, total_pixels)
    grads = jnp.sum(grads_two_ref[...], 0)
    bias_part, gain_part = grads[0:1] / total_pixels, grads[1:2] / total_pixels * inv_two
    scale_two = inv_two * par_ref[2:3, :]
    avg_one, inv_one = norm_of(sums_one_ref, total_pixels)
    gain_one, bias_one = par_ref[0:1, :], par_ref[1:2, :]

    def input_grad(d, grouped, keep):
        return (d - (bias_part + (grouped - avg_two) * gain_part)) * (scale_two * keep)

    def fill(refs, at, image, nothing):
        keep = (image < info_ref[OWN_COUNT]).astype(F32)
        own = input_grad(refs[0][at], grp_ref[image], keep)
        edge = input_grad(refs[1][at].astype(F32), g_edge_ref[image].astype(F32), keep)
        fill_windows(window_ref, image, with_edges(info_ref, own, edge), cols)
        turned_ref[:, pl.ds(pl.multiple_of(image * pixels, pixels), pixels)] = act_ref[image].T
        return nothing

    def convolve(refs, at, first, sums):
        grad = None
        for i in range(3):
            piece = window_ref[pl.ds(first, group_images), i * cols : i * cols + pixels, :]
            term = dot(piece.reshape(group_images * pixels, 3 * chans), mat_ref[i], 1, 0)
            grad = term if grad is None else grad + term
        one, two = sums
        for i in range(group_images):
            image = first + i
            keep = (image < info_ref[OWN_COUNT]).astype(F32)
            normalized = (refs[0][at + i] - avg_one) * inv_one
            slope = silu_slope(normalized * gain_one + bias_one)
            d_one = grad[i * pixels : (i + 1) * pixels] * (slope * keep)
            out_ref[image] = d_one
            one, two = one + fold(d_one), two + fold(d_one * normalized)
        return one, two

    each_image(d_fields, fill, 0)
    zero = jnp.zeros((8, chans), F32)
    put_sums(sums_ref, *each_image(reduced, convolve, (zero, zero), group_images))
    same = (
        lax.broadcasted_iota(jnp.int32, (chans, 3 * chans), 0) // group
        == lax.broadcasted_iota(jnp.int32, (chans, 3 * chans), 1) % chans // group
    )
    for i in range(3):
        total = None
        for first in range(0, images, group_images):
            piece = window_ref[first : first + group_images, i * cols : i * cols + pixels, :]
            turned = turned_ref[:, first * pixels : (first + group_images) * pixels]
            term = dot(turned, piece.reshape(group_images * pixels, 3 * chans), 1, 0)
            total = term if total is None else total + term
        total = jnp.sum(jnp.where(same, total, 0.0).reshape(chans // group, group, 3 * chans), 0)
        for j in range(3):
            kernel_ref[3 * (2 - i) + 2 - j] = total[:, j * chans : (j + 1) * chans].astype(kernel_ref.dtype)


def conv_backward(info, d_two, d_edges, grouped, g_edge, reduced, acts, sums_two, grads_two, sums_one, params, matrices,
                  group, per_image):
    images, pixels, chans = grouped.shape
    cols = g_edge.shape[1]
    return kernel_call(
        functools.partial(conv_backward_kernel, per_image, 4, group, len(d_two), len(reduced)), "conv_backward",
        [info, *d_two, *d_edges, *reduced, grouped, g_edge, acts, sums_two, grads_two, sums_one, params, matrices],
        [(grouped.shape, F32), sums_out(True, chans), ((9, group, chans), F32)],
        [
            pltpu.VMEM((images, pixels + 2 * cols, 3 * chans), BF16),
            pltpu.VMEM((chans, images * pixels), BF16),
        ],
    )


def grad_reduced_kernel(per_image, count, info_ref, *refs):
    reduced = [[v] for v in refs[:count]]
    d_ref, sums_one_ref, grads_ref, par_ref, out_ref = refs[count:]
    pixels = d_ref.shape[1]
    total = pixel_count(info_ref, per_image)
    average, inv_std = norm_of(sums_one_ref, total)
    grads = jnp.sum(grads_ref[...], 0)
    bias_part, gain_part = grads[0:1] / total, grads[1:2] / total * inv_std
    scale = inv_std * par_ref[0:1, :]

    def body(refs, at, image, nothing):
        value = d_ref[image] - (bias_part + (refs[0][at] - average) * gain_part)
        value = value * (scale * (image < info_ref[OWN_COUNT]).astype(F32))
        out_ref[pl.ds(pl.multiple_of(image * pixels, pixels), pixels), :] = value.astype(BF16)
        return nothing

    each_image(reduced, body, 0)


def grad_reduced(info, d_one, reduced, sums_one, grads_one, params, per_image):
    images, pixels, mid = d_one.shape
    return kernel_call(
        functools.partial(grad_reduced_kernel, per_image, len(reduced)), "grad_reduced",
        [info, *reduced, d_one, sums_one, grads_one, params], [((images * pixels, mid), BF16)],
    )[0]


def input_grad_kernel(count, info_ref, grad_ref, *refs):
    pieces, weights, out_ref = refs[:count], refs[count : 2 * count], refs[-1]
    rows = 512

    def body(step, nothing):
        at = pl.ds(pl.multiple_of(step * rows, rows), rows)
        total = grad_ref[at, :]
        for p_ref, w_ref in zip(pieces, weights):
            total = total + dot(p_ref[at, :], w_ref[...], 1, 1)
        out_ref[at, :] = total.astype(BF16)
        return nothing

    lax.fori_loop(0, grad_ref.shape[0] // rows, body, 0)


def input_grad(info, grad_summed, pieces, weights):
    return kernel_call(
        functools.partial(input_grad_kernel, len(pieces)), "input_grad", [info, grad_summed] + list(pieces) + list(weights),
        [(grad_summed.shape, BF16)],
    )[0]


def cut_columns_kernel(info_ref, in_ref, *refs):
    for k, ref in enumerate(refs):
        part = ref.shape[1]
        ref[...] = in_ref[:, pl.ds(pl.multiple_of((info_ref[CHAN_AT] ^ k) * part, part), part)]


def cut_columns(info, value, count):
    rows, part = value.shape[0], value.shape[1] // count
    return kernel_call(cut_columns_kernel, "cut_columns", [info, value], [((rows, part), BF16)] * count)


def cut_rows_kernel(info_ref, in_ref, *refs):
    for k, ref in enumerate(refs):
        part = ref.shape[0]
        ref[...] = in_ref[pl.ds(pl.multiple_of((info_ref[CHAN_AT] ^ k) * part, part), part), :]


def cut_rows(info, value, count):
    part, cols = value.shape[0] // count, value.shape[1]
    return kernel_call(cut_rows_kernel, "cut_rows", [info, value], [((part, cols), BF16)] * count)


def sum_vectors_kernel(*refs):
    half = len(refs) // 3
    for ref, out_one, out_two in zip(refs[:half], refs[half::2], refs[half + 1 :: 2]):
        sums = jnp.sum(ref[...], 0)
        out_one[...] = sums[0:1]
        out_two[...] = sums[1:2]


def sum_vectors(values):
    outs = [((1, v.shape[2]), F32) for v in values for _ in range(2)]
    return [v.reshape(-1) for v in kernel_call(sum_vectors_kernel, "sum_vectors", list(values), outs)]


REDUCE_STEPS = (("height", 1, HEIGHT_AT), ("batch", 1, NEAR_AT), ("batch", 2, FAR_AT))
EXPAND_STEPS = (("height", 1, HEIGHT_AT), ("batch", 1, NEAR_AT), ("batch", 2, FAR_AT))


def part_of(info_ref, steps):
    number = 0
    for _, _, field in steps:
        number = number * 2 + info_ref[field]
    return number


def send_half(pair, step):
    return pair[0], permute(pair[1], step[0], step[1])


def split(at, keep_ref, send_ref, all_ref, arrived_ref):
    half = keep_ref.shape[0]
    for to, ref in ((at, keep_ref), (1 - at, send_ref)):
        value = all_ref[pl.ds(to * half, half)]
        if arrived_ref is not None:
            value = value + arrived_ref[pl.ds(to * half, half)].astype(F32)
        ref[...] = value.astype(ref.dtype)


def split_first_kernel(make, field, info_ref, *refs):
    keep_ref, send_ref, all_ref = refs[-3:]
    make(refs[:-3], all_ref)
    split(info_ref[field], keep_ref, send_ref, all_ref, None)


def split_first(info, make, step, name, ins, shape):
    half = (shape[0] // 2,) + shape[1:]
    return kernel_call(
        functools.partial(split_first_kernel, make, step[2]), name, [info] + ins, [(half, F32), (half, BF16)],
        [pltpu.VMEM(shape, F32)],
    )


def split_next_kernel(field, info_ref, keep_ref, arrived_ref, out_ref, send_ref):
    split(info_ref[field], out_ref, send_ref, keep_ref, arrived_ref)


def split_next(info, pair, step):
    half = (pair[0].shape[0] // 2,) + pair[0].shape[1:]
    return kernel_call(
        functools.partial(split_next_kernel, step[2]), "split_next", [info, *pair], [(half, F32), (half, BF16)]
    )


def add_kernel(info_ref, first_ref, second_ref, out_ref):
    out_ref[...] = (first_ref[...] + second_ref[...].astype(F32)).astype(BF16)


def add_last(info, pair):
    return kernel_call(add_kernel, "add_last", [info, *pair], [(pair[0].shape, BF16)])[0]


def join_kernel(info_ref, *refs):
    size = refs[0].shape[0]
    for k, ref in enumerate(refs[:-1]):
        refs[-1][k * size : (k + 1) * size] = ref[...]


def join(info, *values):
    shape = (values[0].shape[0] * len(values),) + values[0].shape[1:]
    return kernel_call(join_kernel, "join", [info, *values], [(shape, BF16)])[0]


def send_back(value, step):
    return value, permute(value, step[0], step[1])


def reduce_grad_make(places, spans, extra, refs, all_ref):
    grad_ref = refs[places * len(spans)]
    parts = all_ref.shape[0]
    per = parts // places
    for k in range(places):
        total = None
        for c, (first, end) in enumerate(spans):
            term = dot(refs[k * len(spans) + c][...], grad_ref[first:end, :], 0, 0)
            total = term if total is None else total + term
        size = total.shape[0] // per
        all_ref[k * per : (k + 1) * per, 0:size, :] = total.reshape(per, size, total.shape[1])
    if extra:
        more = refs[-1][...]
        more = more.reshape(-1, more.shape[2])
        room = parts * extra - more.shape[0]
        more = jnp.concatenate([more, jnp.zeros((room, more.shape[1]), F32)], 0)
        all_ref[:, size : size + extra, :] = more.reshape(parts, extra, more.shape[1])


def reduce_grad(info, inputs, grad, parts, more):
    spans = spans_of(inputs[0])
    rows, mid = len(inputs) * inputs[0][0].shape[1], grad.shape[1]
    extra = 0 if more is None else -(-more.shape[0] * more.shape[1] // (8 * parts)) * 8
    ins = [v for piece in inputs for v in piece] + [grad] + ([] if more is None else [more])
    return split_first(
        info, functools.partial(reduce_grad_make, len(inputs), tuple(spans), extra), REDUCE_STEPS[0], "reduce_grad", ins,
        (parts, rows // parts + extra, mid),
    )


def spans_of(values):
    spans, at = [], 0
    for value in values:
        spans.append((at, at + value.shape[0]))
        at += value.shape[0]
    return spans


def expand_grad_make(count, chunks, refs, all_ref):
    acts, grads = refs[: count * chunks], refs[count * chunks :]
    parts, wide, out = all_ref.shape
    size = wide // count
    for k in range(count):
        total = None
        own = acts[k * chunks : (k + 1) * chunks]
        for a_ref, (a_first, a_end) in zip(own, spans_of(own)):
            for g_ref, (g_first, g_end) in zip(grads, spans_of(grads)):
                first, end = max(a_first, g_first), min(a_end, g_end)
                if first < end:
                    term = dot(a_ref[first - a_first : end - a_first, :], g_ref[first - g_first : end - g_first, :], 0, 0)
                    total = term if total is None else total + term
        all_ref[:, k * size : (k + 1) * size, :] = total.reshape(parts, size, out)


def expand_grad(info, acts, grads, parts):
    count, mid, out = len(acts), acts[0][0].shape[1], grads[0].shape[1]
    return split_first(
        info, functools.partial(expand_grad_make, count, len(acts[0])), EXPAND_STEPS[0], "expand_grad",
        [a for piece in acts for a in piece] + list(grads), (parts, count * mid // parts, out),
    )


def cut_places_kernel(info_ref, keep_ref, arrived_ref, *refs):
    size = refs[0].shape[0]
    total = (keep_ref[0] + arrived_ref[0].astype(F32)).astype(BF16)
    for k, ref in enumerate(refs):
        ref[...] = total[k * size : (k + 1) * size, :]


def cut_places(info, pair, count):
    rows, out = pair[0].shape[1:]
    return kernel_call(cut_places_kernel, "cut_places", [info, *pair], [((rows // count, out), BF16)] * count)


def place_reduce_kernel(count, info_ref, *refs):
    out_ref, group_ref, more_ref = refs[4:]
    me, number = info_ref[CHAN_AT], part_of(info_ref, REDUCE_STEPS)
    part = out_ref.shape[0] // count
    batches = refs[0].shape[0]
    size = refs[2].shape[1]
    extra = refs[0].shape[1] - size
    for half in range(2):
        for other in range(2):
            ref = refs[2 * half + other]
            for k in range(batches):
                at = number ^ (other * batches + k)
                row = at * size
                to = (me ^ (half * (count // 2) + row // part)) * part + row % part
                out_ref[pl.ds(pl.multiple_of(to, size), size), :] = ref[k, 0:size, :].astype(F32)
                if half == 0:
                    more_ref[pl.ds(pl.multiple_of(at * extra, 8), extra), :] = ref[k, size:, :].astype(F32)
    group_ref[...] = more_ref[0 : group_ref.shape[0], :]


def place_reduce(info, halves, count, part, group_rows):
    batches, rows, mid = halves[0][0].shape
    extra = rows - halves[1][0].shape[1]
    return kernel_call(
        functools.partial(place_reduce_kernel, count), "place_reduce", [info] + [v for pair in halves for v in pair],
        [((part * count, mid), F32), ((group_rows, mid), F32)], [pltpu.VMEM((2 * batches * extra, mid), F32)],
    )


def place_expand_kernel(count, info_ref, own_ref, arrived_ref, out_ref):
    me, number = info_ref[CHAN_AT], part_of(info_ref, EXPAND_STEPS)
    batches, rows, out = own_ref.shape
    size = rows // count
    for other, ref in enumerate((own_ref, arrived_ref)):
        for k in range(batches):
            row = (number ^ (other * batches + k)) * size
            for place in range(count):
                to = pl.ds(pl.multiple_of((me ^ place) * out, out), out)
                out_ref[pl.ds(pl.multiple_of(row, size), size), to] = ref[k, place * size : (place + 1) * size, :].astype(F32)


def place_expand(info, pair, count, mid):
    out = pair[0].shape[2]
    return kernel_call(
        functools.partial(place_expand_kernel, count), "place_expand", [info] + list(pair), [((mid, out * count), F32)]
    )[0]


def plain_weight_grads(inputs, grad, acts, grad_expanded, grad_group):
    count, me = len(inputs), lax.axis_index("chan")
    part, mid = inputs[0][0].shape[1], grad.shape[1]
    grad_reduce = jnp.zeros((part * count, mid), BF16)
    grad_expand = jnp.zeros((mid, part * count), BF16)
    for k in range(count):
        block = dot(jnp.concatenate(inputs[k], 0), grad, 0, 0).astype(BF16)
        grad_reduce = lax.dynamic_update_slice(grad_reduce, block, ((me ^ k) * part, 0))
        block = dot(jnp.concatenate(acts[k], 0), jnp.concatenate(grad_expanded, 0), 0, 0).astype(BF16)
        block = swap(block, k) if k else block
        grad_expand = lax.dynamic_update_slice(grad_expand, block, (0, (me ^ k) * part))
    return [lax.psum(v, REDUCE_AXES).astype(F32) for v in (grad_reduce, grad_expand, grad_group.astype(BF16))]


def shards(
    block_input, w_reduce, w_group, w_expand, gain_one, bias_one, gain_two, bias_two,
    gain_three, bias_three, image_counts, grad_output,
):
    chan_size = lax.axis_size("chan")
    me = lax.axis_index("chan")
    height_at = lax.axis_index("height")
    images, rows, cols, out_part = block_input.shape
    mid_part, group = w_group.shape[3], w_group.shape[2]
    pixels = rows * cols
    per_image = float(pixels * lax.axis_size("height"))
    plan = (pixels, cols)
    distances = range(2, chan_size, 2)
    own_count = jnp.sum(
        jnp.where(jnp.arange(image_counts.shape[0]) == lax.axis_index("batch"), image_counts, 0)
    )
    batch_at = lax.axis_index("batch")
    info = jnp.stack(
        [
            own_count, jnp.sum(image_counts), height_at, me, jnp.where(height_at == 0, pixels - cols, 0),
            batch_at & 1, (batch_at >> 1) & 1,
        ]
    ).astype(jnp.int32)
    parts = lax.axis_size(REDUCE_AXES)
    staged = (lax.axis_size("height"), lax.axis_size("batch")) == (2, 4)

    def edge_swap(edge):
        return permute(edge, "height", 1)

    def sums_of(sums, *waits):
        return staged_sums(sums, *waits) if staged else spread_sums(sums)

    def gather(value, *waits):
        pieces = [value, swap(value, 1)]
        for k in distances:
            pieces.append(swap(value, k))
            pieces.append(swap(after(pieces[k], *waits) if waits else pieces[k], 1))
        return pieces

    field = block_input.reshape(images * pixels, out_part)
    matrices, matrices_back, mid_params, out_params = prepare(
        info, w_group, (gain_one, bias_one, gain_two, bias_two), (gain_three, bias_three)
    )
    columns = cut_columns(info, w_expand, chan_size)
    rows_back = cut_rows(info, w_reduce, chan_size)
    weights = [columns[0], swap(columns[1], 1)]
    reduce_back = [rows_back[0], swap(rows_back[1], 1)]
    inputs = []
    for first, share in cut_images(REDUCE_CHUNKS):
        source = after(field, inputs[0][0], info) if first else field
        piece = lax.slice_in_dim(source, first * pixels, (first + share) * pixels)
        inputs.append(gather(piece, mid_params, weights[1], reduce_back[1]) if first else gather(piece))
    reduced, red_edges, sums = [], [], None
    for pieces, (first, share) in zip(inputs, cut_images(REDUCE_CHUNKS)):
        red, edge, sums = reduce_chunk(info, pieces, (first, share), w_reduce, sums, images, plan, False)
        reduced.append(red)
        red_edges.append(edge_swap(edge))
    inputs = [list(chunks) for chunks in zip(*inputs)]
    weights += [swap(after(columns[k], inputs[2][-1]), k) for k in range(2, chan_size)]
    sums_one = spread_sums(after(sums, *weights[2:]))

    acts_one, grouped, grp_edge, sums = conv_forward(
        info, reduced, red_edges, sums_one, mid_params, matrices, per_image
    )
    sums_two = spread_sums(sums)

    acts = []
    for chunk in cut_images(EXPAND_CHUNKS):
        acts.append(gather(act_two_chunk(info, grouped, sums_two, mid_params, chunk, plan, per_image)))
    expanded, sums = [], None
    for pieces, chunk in zip(acts, cut_images(EXPAND_CHUNKS)):
        out, sums = expand_chunk(info, pieces, weights, chunk, sums, images, plan)
        expanded.append(out)
    acts = [list(chunks) for chunks in zip(*acts)]
    sums_three = spread_sums(sums)
    output, grad_summed, sums = output_pass(
        info, expanded, field.reshape(images, pixels, out_part), grad_output.reshape(images, pixels, out_part), sums_three,
        out_params, per_image,
    )
    grads_three = spread_sums(sums)

    grad_expanded, halves = [], []
    for chunk in cut_images(BACK_CHUNKS):
        grad, near, far = back_expand_chunk(
            info, grad_summed, expanded, sums_three, grads_three, out_params, weights, chunk, mid_part, plan, per_image
        )
        grad_expanded.append(grad)
        halves.append((near, swap(far, 1)))
    own, sent = [], []
    for near, far in halves:
        summed = pair_sum(info, near, far, mid_part)
        own.append(summed[0])
        sent.append([swap(value, k) for value, k in zip(summed[1:], distances)])
    grp_edge = edge_swap(after(grp_edge, own[0]))
    if staged:
        expand_pair = send_half(expand_grad(info, acts, grad_expanded, parts), EXPAND_STEPS[0])
    d_two, d_edges, sums, turn = [], [], None, info
    for c, chunk in enumerate(cut_images(BACK_CHUNKS)):
        if staged and c == 1:
            pair = split_next(after(info, d_two[0]), expand_pair, EXPAND_STEPS[1])
            turn = after(info, pair[0])
            expand_pair = send_half(pair, EXPAND_STEPS[1])
        grad, edge, sums = slope_two_chunk(
            turn, own[c], sent[c], grouped, sums_two, mid_params, chunk, sums, plan, per_image, staged
        )
        d_two.append(grad)
        d_edges.append(edge_swap(edge))
    grads_two = sums_of(sums, grp_edge, *d_edges)
    turn = info
    if staged:
        pair = split_next(after(info, grads_two), expand_pair, EXPAND_STEPS[2])
        turn = after(info, pair[0])
        expand_pair = send_half(pair, EXPAND_STEPS[2])

    d_one, sums, grad_group = conv_backward(
        turn, d_two, d_edges, grouped, grp_edge, reduced, acts_one, sums_two, grads_two, sums_one, mid_params,
        matrices_back, group, per_image,
    )
    if staged:
        reduce_back.append(swap(after(rows_back[2], d_two[-1]), 2))
        places = cut_places(after(info, d_one, reduce_back[2]), expand_pair, chan_size)
        sums = after(sums, places[0])
    grads_one = spread_sums(sums)

    grad = grad_reduced(info, d_one, reduced, sums_one, grads_one, mid_params, per_image)
    grad_field = grad_summed.reshape(images * pixels, out_part)
    if staged:
        half = chan_size // 2
        pairs, turn = [], after(info, grad)

        def in_turn(call, *args):
            nonlocal turn
            result = call(turn, *args)
            turn = after(info, result[0] if isinstance(result, (list, tuple)) else result)
            return result

        def first_half(i):
            own = inputs[i * half : (i + 1) * half]
            pair = in_turn(reduce_grad, own, grad, parts, None if i else grad_group)
            pairs.append(send_half(pair, REDUCE_STEPS[0]))

        def next_half(i, step):
            pairs[i] = send_half(in_turn(split_next, pairs[i], REDUCE_STEPS[step]), REDUCE_STEPS[step])

        def last_half(i):
            pairs[i] = send_back(in_turn(add_last, pairs[i]), REDUCE_STEPS[2])

        def back_half(i, step):
            pairs[i] = send_back(in_turn(join, *pairs[i]), REDUCE_STEPS[step])

        first_half(0)
        first_half(1)
        places = [v if k == 0 else swap(after(v, turn), k) for k, v in enumerate(places)]
        next_half(0, 1)
        next_half(1, 1)
        back = in_turn(join, *places)
        back = send_back(back.reshape((1,) + back.shape), EXPAND_STEPS[2])
        far_grads = [swap(after(grad, turn), k) for k in distances]
        next_half(0, 2)
        next_half(1, 2)
        back = send_back(in_turn(join, *back), EXPAND_STEPS[1])
        grads = [grad, swap(after(grad, turn), 1)]
        reduce_back += [swap(after(rows_back[k], *far_grads), k) for k in range(3, chan_size)]
        last_half(0)
        back = send_back(in_turn(join, *back), EXPAND_STEPS[0])
        last_half(1)
        back_half(0, 1)
        for value in far_grads:
            grads += [value, swap(after(value, turn), 1)]
        back_half(1, 1)
        back_half(0, 0)
        turn = after(turn, reduce_back[3])
        grad_expand = in_turn(place_expand, back, chan_size, mid_part)
        back_half(1, 0)
        grad_input = in_turn(input_grad, grad_field, grads, reduce_back)
        grad_reduce, grad_group = place_reduce(turn, pairs, chan_size, out_part, 9 * group)
    else:
        reduce_back += [swap(rows_back[k], k) for k in range(2, chan_size)]
        grad_input = input_grad(info, grad_field, gather(grad), reduce_back)
        grad_reduce, grad_expand, grad_group = plain_weight_grads(inputs, grad, acts, grad_expanded, grad_group)
    vectors = sum_vectors([grads_one, grads_two, grads_three])
    return (
        output.reshape(block_input.shape), grad_input.reshape(block_input.shape), grad_reduce,
        grad_group.reshape(w_group.shape), grad_expand,
        vectors[1], vectors[0], vectors[3], vectors[2], vectors[5], vectors[4],
    )


def solution(mesh):
    split = P("batch", "height", None, "chan")
    vector = P("chan")
    return jax.shard_map(
        shards,
        mesh=mesh,
        in_specs=(
            split, P(None, "chan"), P(None, None, None, "chan"), P("chan", None),
            vector, vector, vector, vector, vector, vector, P(), split,
        ),
        out_specs=(
            split, split, P(None, "chan"), P(None, None, None, "chan"), P("chan", None),
            vector, vector, vector, vector, vector, vector,
        ),
        check_vma=False,
    )
```

```python
import functools

import jax
import jax.numpy as jnp
from jax import lax
from jax.experimental import pallas as pl
from jax.experimental.pallas import tpu as pltpu
from jax.sharding import PartitionSpec as P

EPSILON = 1e-05
STAGE_COST = 1_500_000_000
LAST_PHASE = (
    "wz", "wr", "a0", "t", "b0", "c", "a1", "b1", "e0", "x", "a2", "b2", "e1", "o", "a3", "e2", "b3", "a4",
    "d", "b4", "we", "a5", "wa", "b5", "i", "p",
)
F32, BF16 = jnp.float32, jnp.bfloat16
REDUCE_AXES = ("height", "batch")
REDUCE_CHUNKS, EXPAND_CHUNKS, BACK_CHUNKS = (8, 8), (8, 8), (8, 8)
OWN_COUNT, TOTAL_COUNT, HEIGHT_AT, CHAN_AT, EDGE_ROW, NEAR_AT, FAR_AT = range(7)
VMEM = pl.BlockSpec(memory_space=pltpu.VMEM)
SMEM = pl.BlockSpec(memory_space=pltpu.SMEM)


def dot(a, b, left, right):
    return lax.dot_general(a, b, (((left,), (right,)), ((), ())), preferred_element_type=F32)


def kernel_call(body, name, ins, outs, scratch=(), alias=None, flops=0, room=16):
    return pl.pallas_call(
        body,
        in_specs=[SMEM if a.dtype == jnp.int32 else VMEM for a in ins],
        out_specs=[VMEM] * len(outs),
        out_shape=[jax.ShapeDtypeStruct(shape, dtype) for shape, dtype in outs],
        scratch_shapes=list(scratch),
        input_output_aliases=alias or {},
        compiler_params=pltpu.CompilerParams(vmem_limit_bytes=room << 20),
        cost_estimate=pl.CostEstimate(flops=flops, bytes_accessed=0, transcendentals=0),
        name=name,
    )(*ins)


def after(value, *others):
    return lax.optimization_barrier((value,) + others)[0]


def permute(value, axis, distance):
    count = lax.axis_size(axis)
    return lax.ppermute(value, axis, [(i, i ^ distance) for i in range(count)])


def swap(value, distance):
    return permute(value, "chan", distance)


def spread_sums(sent):
    return lax.all_to_all(sent, REDUCE_AXES, 0, 0)


def staged_sums(partial, *waits):
    chans = partial.shape[2]
    both = kernel_call(
        add_rows_kernel, "add_rows", [after(partial, *waits), permute(partial, "height", 1)], [((2, chans), F32)]
    )[0]
    others = [permute(both, "batch", k) for k in range(1, lax.axis_size("batch"))]
    return kernel_call(add_sums_kernel, "add_sums", [both] + others, [((1, 2, chans), F32)])[0]


def add_rows_kernel(own_ref, other_ref, out_ref):
    out_ref[...] = jnp.sum(own_ref[...] + other_ref[...], 1)


def add_sums_kernel(*refs):
    total = refs[0][...]
    for ref in refs[1:-1]:
        total = total + ref[...]
    refs[-1][0] = total


def norm_of(sums_ref, total):
    sums = jnp.sum(sums_ref[...], 0)
    average = sums[0:1] / total
    return average, lax.rsqrt(sums[1:2] / total - average * average + EPSILON)


def pixel_count(info_ref, per_image):
    return info_ref[TOTAL_COUNT].astype(F32) * per_image


def sigmoid(v):
    return 0.5 * jnp.tanh(0.5 * v) + 0.5


def silu_slope(v):
    logistic = sigmoid(v)
    return logistic * (1.0 + v * (1.0 - logistic))


def fold(values):
    rows, chans = values.shape
    return jnp.sum(values.reshape(rows // 8, 8, chans), 0)


def put_sums(out_ref, one, two):
    if out_ref.shape[1] == 8:
        out_ref[0] = one
        out_ref[1] = two
    else:
        both = jnp.concatenate([jnp.sum(one, 0, keepdims=True), jnp.sum(two, 0, keepdims=True)], 0)
        out_ref[...] = jnp.broadcast_to(both[None], out_ref.shape)


def sums_out(last, chans):
    return ((lax.axis_size(REDUCE_AXES), 2, chans) if last else (2, 8, chans), F32)


def before_sums(before_ref, chans):
    if before_ref is None:
        zero = jnp.zeros((8, chans), F32)
        return zero, zero
    return before_ref[0], before_ref[1]


def edge_rows(info_ref, ref, image, cols):
    return ref[image, pl.ds(pl.multiple_of(info_ref[EDGE_ROW], 16), cols), :]


def prepare_kernel(group, info_ref, taps_ref, mid_a, mid_b, mid_c, mid_d, out_a, out_b, fwd_ref, back_ref, mid_ref, out_ref):
    chans = taps_ref.shape[2]
    same = (
        lax.broadcasted_iota(jnp.int32, (chans, chans), 0) // group
        == lax.broadcasted_iota(jnp.int32, (chans, chans), 1) // group
    )
    for i in range(3):
        for j in range(3):
            wide = jnp.concatenate([taps_ref[3 * i + j].astype(F32)] * (chans // group), 0)
            wide = jnp.where(same, wide, 0.0)
            fwd_ref[i, j * chans : (j + 1) * chans, :] = wide.astype(BF16)
            back_ref[2 - i, (2 - j) * chans : (3 - j) * chans, :] = wide.T.astype(BF16)
    for row, ref in enumerate((mid_a, mid_b, mid_c, mid_d)):
        mid_ref[row : row + 1, :] = ref[...].astype(F32)
    for row, ref in enumerate((out_a, out_b)):
        out_ref[row : row + 1, :] = ref[...].astype(F32)


def prepare(info, kernel, mid_vectors, out_vectors):
    group, chans = kernel.shape[2], kernel.shape[3]
    wide = (3, 3 * chans, chans)
    rows = [v.reshape(1, -1) for v in list(mid_vectors) + list(out_vectors)]
    return kernel_call(
        functools.partial(prepare_kernel, group), "prepare", [info, kernel.reshape(9, group, chans)] + rows,
        [(wide, BF16), (wide, BF16), ((4, chans), F32), ((2, rows[-1].shape[1]), F32)],
    )


def cut_images(shares):
    return [(sum(shares[:i]), share) for i, share in enumerate(shares)]


def reduce_kernel(first, plan, count, info_ref, *refs):
    pixels, cols = plan
    pieces, w_ref, before_ref = refs[:count], refs[count], None if len(refs) == count + 4 else refs[count + 1]
    red_ref, edge_ref, sums_ref = refs[-3:]
    me = info_ref[CHAN_AT]
    part, images = pieces[0].shape[1], red_ref.shape[0]
    one, two = before_sums(before_ref, w_ref.shape[1])
    step = min(4, images)
    for start in range(0, images, step):
        total = None
        for k in range(count):
            rows = w_ref[pl.ds(pl.multiple_of((me ^ k) * part, part), part), :]
            term = dot(pieces[k][start * pixels : (start + step) * pixels, :], rows, 1, 0)
            total = term if total is None else total + term
        for i in range(start, start + step):
            value = total[(i - start) * pixels : (i - start + 1) * pixels]
            red_ref[i] = value
            edge_ref[i] = edge_rows(info_ref, red_ref, i, cols).astype(BF16)
            value = value * (first + i < info_ref[OWN_COUNT]).astype(F32)
            one, two = one + fold(value), two + fold(value * value)
    put_sums(sums_ref, one, two)


def reduce_chunk(info, pieces, chunk, w_reduce, before, images, plan, staged):
    pixels, cols = plan
    first, share = chunk
    count, mid = len(pieces), w_reduce.shape[1]
    ins = [info] + list(pieces) + [w_reduce] + ([] if before is None else [before])
    return kernel_call(
        functools.partial(reduce_kernel, first, plan, count), "reduce", ins,
        [((share, pixels, mid), F32), ((share, cols, mid), BF16), sums_out(first + share == images and not staged, mid)],
        flops=2 * pieces[0].size * count * mid,
    )


def each_image(chunks, body, carry, step=1):
    first = 0
    for refs in chunks:
        count = refs[0].shape[0]
        start = first
        carry = lax.fori_loop(
            0, count // step, lambda i, c, refs=refs, start=start: body(refs, i * step, start + i * step, c), carry
        )
        first += count
    return carry


def fill_windows(window_ref, slot, value, cols):
    rows, chans = value.shape
    place = lax.broadcasted_iota(jnp.int32, value.shape, 0) % cols
    left = jnp.where(place == 0, 0.0, pltpu.roll(value, 1, 0))
    right = jnp.where(place == cols - 1, 0.0, pltpu.roll(value, rows - 1, 0))
    window_ref[slot, :, 0:chans] = left.astype(BF16)
    window_ref[slot, :, chans : 2 * chans] = value.astype(BF16)
    window_ref[slot, :, 2 * chans : 3 * chans] = right.astype(BF16)


def with_edges(info_ref, own, edge):
    low = (info_ref[HEIGHT_AT] > 0).astype(F32)
    return jnp.concatenate([edge * low, own, edge * (1.0 - low)], 0)


def conv_forward_kernel(
    per_image, group_images, count, info_ref, *refs
):
    fields = list(zip(refs[:count], refs[count : 2 * count]))
    sums_one_ref, par_ref, mat_ref, act_ref, out_ref, out_edge_ref, sums_ref, window_ref = refs[2 * count :]
    images, pixels, chans = act_ref.shape
    cols = out_edge_ref.shape[1]
    average, inv_std = norm_of(sums_one_ref, pixel_count(info_ref, per_image))
    scale, bias = inv_std * par_ref[0:1, :], par_ref[1:2, :]

    def activate(v, keep):
        pre = (v - average) * scale + bias
        return pre * sigmoid(pre) * keep

    def fill(image):
        keep = (image < info_ref[OWN_COUNT]).astype(F32)
        own = activate(at_image([f[0] for f in fields], image), keep)
        edge = activate(at_image([f[1] for f in fields], image).astype(F32), keep)
        act_ref[image] = own.astype(BF16)
        fill_windows(window_ref, image, with_edges(info_ref, own, edge), cols)

    def convolve(first):
        total = None
        for i in range(3):
            piece = window_ref[first : first + group_images, i * cols : i * cols + pixels, :]
            term = dot(piece.reshape(group_images * pixels, 3 * chans), mat_ref[i], 1, 0)
            total = term if total is None else total + term
        out_ref[first : first + group_images] = total.reshape(group_images, pixels, chans)
        return fold(total), fold(total * total)

    one = two = jnp.zeros((8, chans), F32)
    for first in range(0, images + group_images, group_images):
        for image in range(first, min(first + group_images, images)):
            fill(image)
        if first:
            more = convolve(first - group_images)
            one, two = one + more[0], two + more[1]
    for image in range(images):
        out_edge_ref[image] = edge_rows(info_ref, out_ref, image, cols).astype(BF16)
    put_sums(sums_ref, one, two)


def conv_forward(info, reduced, edges, sums_one, params, matrices, per_image):
    images = sum(v.shape[0] for v in reduced)
    pixels, chans = reduced[0].shape[1:]
    cols = edges[0].shape[1]
    shape = (images, pixels, chans)
    return kernel_call(
        functools.partial(conv_forward_kernel, per_image, 4, len(reduced)), "conv_forward",
        [info, *reduced, *edges, sums_one, params, matrices],
        [(shape, BF16), (shape, F32), ((images, cols, chans), BF16), sums_out(True, chans)],
        [pltpu.VMEM((images, pixels + 2 * cols, 3 * chans), BF16)],
    )


def act_two_kernel(chunk, plan, per_image, info_ref, grp_ref, sums_ref, par_ref, out_ref):
    pixels, cols = plan
    first, images = chunk
    average, inv_std = norm_of(sums_ref, pixel_count(info_ref, per_image))
    scale, bias = inv_std * par_ref[2:3, :], par_ref[3:4, :]
    for i in range(images):
        image = first + i
        pre = (grp_ref[image] - average) * scale + bias
        act = pre * sigmoid(pre) * (image < info_ref[OWN_COUNT]).astype(F32)
        out_ref[i * pixels : (i + 1) * pixels] = act.astype(BF16)


def act_two_chunk(info, grouped, sums_two, params, chunk, plan, per_image):
    pixels, cols = plan
    shape = (chunk[1] * pixels, grouped.shape[2])
    return kernel_call(
        functools.partial(act_two_kernel, chunk, plan, per_image), "act_two",
        [info, grouped, sums_two, params], [(shape, BF16)],
    )[0]


def expand_kernel(first, plan, count, mid, info_ref, *refs):
    pixels, cols = plan
    acts, weights = refs[:count], refs[count : 2 * count]
    before_ref = None if len(refs) == 2 * count + 2 else refs[2 * count]
    out_ref, sums_ref = refs[-2:]
    images = out_ref.shape[0]
    one, two = before_sums(before_ref, out_ref.shape[2])
    step = min(4, images)
    for start in range(0, images, step):
        total = None
        for a_ref, w_ref in zip(acts, weights):
            term = dot(a_ref[start * pixels : (start + step) * pixels, :], w_ref[...], 1, 0)
            total = term if total is None else total + term
        out_ref[start : start + step] = total.reshape(step, pixels, total.shape[1])
        for i in range(step):
            keep = (first + start + i < info_ref[OWN_COUNT]).astype(F32)
            value = total[i * pixels : (i + 1) * pixels] * keep
            one, two = one + fold(value), two + fold(value * value)
    put_sums(sums_ref, one, two)


def expand_chunk(info, acts, weights, chunk, before, images, plan):
    pixels, cols = plan
    first, share = chunk
    count, mid, out = len(acts), acts[0].shape[1], weights[0].shape[1]
    ins = [info] + list(acts) + list(weights) + ([] if before is None else [before])
    return kernel_call(
        functools.partial(expand_kernel, first, plan, count, mid), "expand", ins,
        [((share, pixels, out), F32), sums_out(first + share == images, out)],
    )


def output_kernel(per_image, count, info_ref, *refs):
    expanded = [[v] for v in refs[:count]]
    in_ref, go_ref, sums_three_ref, par_ref, out_ref, grad_ref, sums_ref = refs[count:]
    average, inv_std = norm_of(sums_three_ref, pixel_count(info_ref, per_image))
    gain, bias = par_ref[0:1, :], par_ref[1:2, :]
    chans = out_ref.shape[2]

    def body(refs, at, image, sums):
        keep = (image < info_ref[OWN_COUNT]).astype(F32)
        normalized = (refs[0][at] - average) * inv_std
        summed = normalized * gain + bias + in_ref[image].astype(F32)
        logistic = sigmoid(summed)
        out_ref[image] = (summed * logistic * keep).astype(BF16)
        slope = logistic * (1.0 + summed * (1.0 - logistic))
        grad = go_ref[image].astype(F32) * (slope * keep)
        grad_ref[image] = grad
        return sums[0] + fold(grad), sums[1] + fold(grad * normalized)

    zero = jnp.zeros((8, chans), F32)
    put_sums(sums_ref, *each_image(expanded, body, (zero, zero)))


def output_pass(info, expanded, field, grad_output, sums_three, params, per_image):
    return kernel_call(
        functools.partial(output_kernel, per_image, len(expanded)), "output",
        [info, *expanded, field, grad_output, sums_three, params],
        [(field.shape, BF16), (field.shape, F32), sums_out(True, field.shape[2])],
    )


def at_image(refs, image):
    for ref in refs:
        if image < ref.shape[0]:
            return ref[image]
        image -= ref.shape[0]


def back_expand_kernel(first, plan, count, mid, fields, per_image, info_ref, *refs):
    pixels, cols = plan
    expanded, refs = refs[:fields], refs[fields:]
    grad_ref, sums_three_ref, grads_ref, par_ref = refs[:4]
    weights = refs[4 : 4 + count]
    out_ref, near_ref, far_ref = refs[-3:]
    total = pixel_count(info_ref, per_image)
    average, inv_std = norm_of(sums_three_ref, total)
    grads = jnp.sum(grads_ref[...], 0)
    scale = inv_std * par_ref[0:1, :]
    bias_part, gain_part = grads[0:1] / total, grads[1:2] / total * inv_std
    for i in range(out_ref.shape[0] // pixels):
        image = first + i
        value = grad_ref[image] - (bias_part + (at_image(expanded, image) - average) * gain_part)
        value = value * (scale * (image < info_ref[OWN_COUNT]).astype(F32))
        out_ref[i * pixels : (i + 1) * pixels, :] = value.astype(BF16)
    for k in range(count):
        term = dot(out_ref[...], weights[k][...], 1, 1)
        to = slice((k // 2) * mid, (k // 2 + 1) * mid)
        if k % 2 == 0:
            near_ref[:, to] = term
        else:
            far_ref[:, to] = term.astype(BF16)


def back_expand_chunk(info, grad_summed, expanded, sums_three, grads_three, params, weights, chunk, mid, plan, per_image):
    pixels, cols = plan
    count, out = len(weights), grad_summed.shape[2]
    block, half = chunk[1] * pixels, count // 2 * mid
    return kernel_call(
        functools.partial(back_expand_kernel, chunk[0], plan, count, mid, len(expanded), per_image), "back_expand",
        [info, *expanded, grad_summed, sums_three, grads_three, params, *weights],
        [((block, out), BF16), ((block, half), F32), ((block, half), BF16)],
        flops=2 * block * mid * count * out,
    )


def pair_sum_kernel(info_ref, near_ref, far_ref, own_ref, *send_refs):
    mid = own_ref.shape[1]
    for k, ref in enumerate((own_ref,) + send_refs):
        at = slice(k * mid, (k + 1) * mid)
        ref[...] = (near_ref[:, at] + far_ref[:, at].astype(F32)).astype(ref.dtype)


def pair_sum(info, near, far, mid):
    rows, half = near.shape
    return kernel_call(
        pair_sum_kernel, "pair_sum", [info, near, far],
        [((rows, mid), F32 if k == 0 else BF16) for k in range(half // mid)],
    )


def slope_two_kernel(first, plan, count, per_image, info_ref, own_ref, *refs):
    pixels, cols = plan
    arrived, refs = refs[:count], refs[count:]
    grp_ref, sums_two_ref, par_ref = refs[:3]
    before_ref = None if len(refs) == 6 else refs[3]
    out_ref, edge_ref, sums_ref = refs[-3:]
    average, inv_std = norm_of(sums_two_ref, pixel_count(info_ref, per_image))
    gain, bias = par_ref[2:3, :], par_ref[3:4, :]
    one, two = before_sums(before_ref, grp_ref.shape[2])
    for i in range(out_ref.shape[0]):
        image = first + i
        at = slice(i * pixels, (i + 1) * pixels)
        grad = own_ref[at, :]
        for ref in arrived:
            grad = grad + ref[at, :].astype(F32)
        normalized = (grp_ref[image] - average) * inv_std
        keep = (image < info_ref[OWN_COUNT]).astype(F32)
        grad = grad * (silu_slope(normalized * gain + bias) * keep)
        out_ref[i] = grad
        edge_ref[i] = edge_rows(info_ref, out_ref, i, cols).astype(BF16)
        one, two = one + fold(grad), two + fold(grad * normalized)
    put_sums(sums_ref, one, two)


def slope_two_chunk(info, own, arrived, grouped, sums_two, params, chunk, before, plan, per_image, staged):
    pixels, cols = plan
    first, share = chunk
    images, mid = grouped.shape[0], grouped.shape[2]
    ins = [info, own] + list(arrived) + [grouped, sums_two, params] + ([] if before is None else [before])
    return kernel_call(
        functools.partial(slope_two_kernel, first, plan, len(arrived), per_image), "slope_two", ins,
        [((share, pixels, mid), F32), ((share, cols, mid), BF16), sums_out(first + share == images and not staged, mid)],
    )


def conv_backward_kernel(
    per_image, group_images, d_count, red_count, info_ref, *refs
):
    d_fields, refs = list(zip(refs[:d_count], refs[d_count : 2 * d_count])), refs[2 * d_count :]
    reduced, refs = refs[:red_count], refs[red_count:]
    grp_ref, g_edge_ref, sums_two_ref, grads_two_ref, sums_one_ref, par_ref, mat_ref = refs[:7]
    out_ref, sums_ref, window_ref = refs[7:]
    images, pixels, chans = grp_ref.shape
    cols = g_edge_ref.shape[1]
    total_pixels = pixel_count(info_ref, per_image)
    avg_two, inv_two = norm_of(sums_two_ref, total_pixels)
    grads = jnp.sum(grads_two_ref[...], 0)
    bias_part, gain_part = grads[0:1] / total_pixels, grads[1:2] / total_pixels * inv_two
    scale_two = inv_two * par_ref[2:3, :]
    avg_one, inv_one = norm_of(sums_one_ref, total_pixels)
    gain_one, bias_one = par_ref[0:1, :], par_ref[1:2, :]

    def input_grad(d, grouped, keep):
        return (d - (bias_part + (grouped - avg_two) * gain_part)) * (scale_two * keep)

    def fill(image):
        keep = (image < info_ref[OWN_COUNT]).astype(F32)
        own = input_grad(at_image([f[0] for f in d_fields], image), grp_ref[image], keep)
        edge = at_image([f[1] for f in d_fields], image).astype(F32)
        edge = input_grad(edge, g_edge_ref[image].astype(F32), keep)
        fill_windows(window_ref, image, with_edges(info_ref, own, edge), cols)

    def convolve(first, one, two):
        grad = None
        for i in range(3):
            piece = window_ref[first : first + group_images, i * cols : i * cols + pixels, :]
            term = dot(piece.reshape(group_images * pixels, 3 * chans), mat_ref[i], 1, 0)
            grad = term if grad is None else grad + term
        for i in range(group_images):
            image = first + i
            keep = (image < info_ref[OWN_COUNT]).astype(F32)
            normalized = (at_image(reduced, image) - avg_one) * inv_one
            slope = silu_slope(normalized * gain_one + bias_one)
            d_one = grad[i * pixels : (i + 1) * pixels] * (slope * keep)
            out_ref[image] = d_one
            one, two = one + fold(d_one), two + fold(d_one * normalized)
        return one, two

    one = two = jnp.zeros((8, chans), F32)
    for first in range(0, images + group_images, group_images):
        for image in range(first, min(first + group_images, images)):
            fill(image)
        if first:
            one, two = convolve(first - group_images, one, two)
    put_sums(sums_ref, one, two)


def tap_grads_kernel(group, cols, step, info_ref, act_ref, window_ref, out_ref, turned_ref):
    images, pixels, chans = act_ref.shape
    for image in range(images):
        turned_ref[:, image * pixels : (image + 1) * pixels] = act_ref[image].T
    same = (
        lax.broadcasted_iota(jnp.int32, (chans, 3 * chans), 0) // group
        == lax.broadcasted_iota(jnp.int32, (chans, 3 * chans), 1) % chans // group
    )
    for i in range(3):
        total = None
        for first in range(0, images, step):
            piece = window_ref[first : first + step, i * cols : i * cols + pixels, :]
            turned = turned_ref[:, first * pixels : (first + step) * pixels]
            term = dot(turned, piece.reshape(step * pixels, 3 * chans), 1, 0)
            total = term if total is None else total + term
        total = jnp.sum(jnp.where(same, total, 0.0).reshape(chans // group, group, 3 * chans), 0)
        for j in range(3):
            out_ref[3 * (2 - i) + 2 - j] = total[:, j * chans : (j + 1) * chans]


def tap_grads(info, acts, windows, group, cols):
    images, pixels, chans = acts.shape
    return kernel_call(
        functools.partial(tap_grads_kernel, group, cols, 4), "tap_grads", [info, acts, windows], [((9, group, chans), F32)],
        [pltpu.VMEM((chans, images * pixels), BF16)],
    )[0]


def conv_backward(info, d_two, d_edges, grouped, g_edge, reduced, sums_two, grads_two, sums_one, params, matrices, per_image):
    images, pixels, chans = grouped.shape
    cols = g_edge.shape[1]
    return kernel_call(
        functools.partial(conv_backward_kernel, per_image, 4, len(d_two), len(reduced)), "conv_backward",
        [info, *d_two, *d_edges, *reduced, grouped, g_edge, sums_two, grads_two, sums_one, params, matrices],
        [(grouped.shape, F32), sums_out(True, chans), ((images, pixels + 2 * cols, 3 * chans), BF16)],
    )


def grad_reduced_kernel(per_image, count, info_ref, *refs):
    reduced = [[v] for v in refs[:count]]
    d_ref, sums_one_ref, grads_ref, par_ref, out_ref = refs[count:]
    pixels = d_ref.shape[1]
    total = pixel_count(info_ref, per_image)
    average, inv_std = norm_of(sums_one_ref, total)
    grads = jnp.sum(grads_ref[...], 0)
    bias_part, gain_part = grads[0:1] / total, grads[1:2] / total * inv_std
    scale = inv_std * par_ref[0:1, :]

    def body(refs, at, image, nothing):
        value = d_ref[image] - (bias_part + (refs[0][at] - average) * gain_part)
        value = value * (scale * (image < info_ref[OWN_COUNT]).astype(F32))
        out_ref[pl.ds(pl.multiple_of(image * pixels, pixels), pixels), :] = value.astype(BF16)
        return nothing

    each_image(reduced, body, 0)


def grad_reduced(info, d_one, reduced, sums_one, grads_one, params, per_image):
    images, pixels, mid = d_one.shape
    return kernel_call(
        functools.partial(grad_reduced_kernel, per_image, len(reduced)), "grad_reduced",
        [info, *reduced, d_one, sums_one, grads_one, params], [((images * pixels, mid), BF16)],
    )[0]


def input_grad_kernel(count, info_ref, grad_ref, *refs):
    pieces, weights, out_ref = refs[:count], refs[count : 2 * count], refs[-1]
    rows = 512

    def body(step, nothing):
        at = pl.ds(pl.multiple_of(step * rows, rows), rows)
        total = grad_ref[at, :]
        for p_ref, w_ref in zip(pieces, weights):
            total = total + dot(p_ref[at, :], w_ref[...], 1, 1)
        out_ref[at, :] = total.astype(BF16)
        return nothing

    lax.fori_loop(0, grad_ref.shape[0] // rows, body, 0)


def input_grad(info, grad_summed, pieces, weights):
    return kernel_call(
        functools.partial(input_grad_kernel, len(pieces)), "input_grad", [info, grad_summed] + list(pieces) + list(weights),
        [(grad_summed.shape, BF16)],
    )[0]


def cut_columns_kernel(info_ref, in_ref, *refs):
    for k, ref in enumerate(refs):
        part = ref.shape[1]
        ref[...] = in_ref[:, pl.ds(pl.multiple_of((info_ref[CHAN_AT] ^ k) * part, part), part)]


def cut_columns(info, value, count):
    rows, part = value.shape[0], value.shape[1] // count
    return kernel_call(cut_columns_kernel, "cut_columns", [info, value], [((rows, part), BF16)] * count)


def cut_rows_kernel(info_ref, in_ref, *refs):
    for k, ref in enumerate(refs):
        part = ref.shape[0]
        ref[...] = in_ref[pl.ds(pl.multiple_of((info_ref[CHAN_AT] ^ k) * part, part), part), :]


def cut_rows(info, value, count):
    part, cols = value.shape[0] // count, value.shape[1]
    return kernel_call(cut_rows_kernel, "cut_rows", [info, value], [((part, cols), BF16)] * count)


def sum_vectors_kernel(*refs):
    half = len(refs) // 3
    for ref, out_one, out_two in zip(refs[:half], refs[half::2], refs[half + 1 :: 2]):
        sums = jnp.sum(ref[...], 0)
        out_one[...] = sums[0:1]
        out_two[...] = sums[1:2]


def sum_vectors(values):
    outs = [((1, v.shape[2]), F32) for v in values for _ in range(2)]
    return [v.reshape(-1) for v in kernel_call(sum_vectors_kernel, "sum_vectors", list(values), outs)]


REDUCE_STEPS = (("height", 1, HEIGHT_AT), ("batch", 1, NEAR_AT), ("batch", 2, FAR_AT))
EXPAND_STEPS = (("height", 1, HEIGHT_AT), ("batch", 1, NEAR_AT), ("batch", 2, FAR_AT))


def part_of(info_ref, steps):
    number = 0
    for _, _, field in steps:
        number = number * 2 + info_ref[field]
    return number


def send_half(pair, step):
    return pair[0], permute(pair[1], step[0], step[1])


def split(at, keep_ref, send_ref, all_ref, arrived_ref):
    half = keep_ref.shape[0]
    for to, ref in ((at, keep_ref), (1 - at, send_ref)):
        value = all_ref[pl.ds(to * half, half)]
        if arrived_ref is not None:
            value = value + arrived_ref[pl.ds(to * half, half)].astype(F32)
        ref[...] = value.astype(ref.dtype)


def split_first_kernel(make, field, info_ref, *refs):
    keep_ref, send_ref, all_ref = refs[-3:]
    make(refs[:-3], all_ref)
    split(info_ref[field], keep_ref, send_ref, all_ref, None)


def split_first(info, make, step, name, ins, shape):
    half = (shape[0] // 2,) + shape[1:]
    return kernel_call(
        functools.partial(split_first_kernel, make, step[2]), name, [info] + ins, [(half, F32), (half, BF16)],
        [pltpu.VMEM(shape, F32)],
    )


def split_next_kernel(field, info_ref, keep_ref, arrived_ref, out_ref, send_ref):
    split(info_ref[field], out_ref, send_ref, keep_ref, arrived_ref)


def split_next(info, pair, step):
    half = (pair[0].shape[0] // 2,) + pair[0].shape[1:]
    return kernel_call(
        functools.partial(split_next_kernel, step[2]), "split_next", [info, *pair], [(half, F32), (half, BF16)], flops=STAGE_COST
    )


def add_kernel(info_ref, first_ref, second_ref, out_ref):
    out_ref[...] = (first_ref[...] + second_ref[...].astype(F32)).astype(BF16)


def add_last(info, pair):
    return kernel_call(add_kernel, "add_last", [info, *pair], [(pair[0].shape, BF16)], flops=STAGE_COST)[0]


def join_kernel(info_ref, *refs):
    size = refs[0].shape[0]
    for k, ref in enumerate(refs[:-1]):
        refs[-1][k * size : (k + 1) * size] = ref[...]


def join(info, *values):
    shape = (values[0].shape[0] * len(values),) + values[0].shape[1:]
    return kernel_call(join_kernel, "join", [info, *values], [(shape, BF16)], flops=STAGE_COST)[0]


def send_back(value, step):
    return value, permute(value, step[0], step[1])


def reduce_grad_make(places, spans, extra, refs, all_ref):
    grad_ref = refs[places * len(spans)]
    parts = all_ref.shape[0]
    per = parts // places
    for k in range(places):
        total = None
        for c, (first, end) in enumerate(spans):
            term = dot(refs[k * len(spans) + c][...], grad_ref[first:end, :], 0, 0)
            total = term if total is None else total + term
        size = total.shape[0] // per
        all_ref[k * per : (k + 1) * per, 0:size, :] = total.reshape(per, size, total.shape[1])
    if extra:
        more = refs[-1][...]
        more = more.reshape(-1, more.shape[2])
        room = parts * extra - more.shape[0]
        more = jnp.concatenate([more, jnp.zeros((room, more.shape[1]), F32)], 0)
        all_ref[:, size : size + extra, :] = more.reshape(parts, extra, more.shape[1])


def reduce_grad(info, inputs, grad, parts, more):
    spans = spans_of(inputs[0])
    rows, mid = len(inputs) * inputs[0][0].shape[1], grad.shape[1]
    extra = 0 if more is None else -(-more.shape[0] * more.shape[1] // (8 * parts)) * 8
    ins = [v for piece in inputs for v in piece] + [grad] + ([] if more is None else [more])
    return split_first(
        info, functools.partial(reduce_grad_make, len(inputs), tuple(spans), extra), REDUCE_STEPS[0], "reduce_grad", ins,
        (parts, rows // parts + extra, mid),
    )


def spans_of(values):
    spans, at = [], 0
    for value in values:
        spans.append((at, at + value.shape[0]))
        at += value.shape[0]
    return spans


def expand_grad_make(count, chunks, refs, all_ref):
    acts, grads = refs[: count * chunks], refs[count * chunks :]
    parts, wide, out = all_ref.shape
    size = wide // count
    for k in range(count):
        total = None
        own = acts[k * chunks : (k + 1) * chunks]
        for a_ref, (a_first, a_end) in zip(own, spans_of(own)):
            for g_ref, (g_first, g_end) in zip(grads, spans_of(grads)):
                first, end = max(a_first, g_first), min(a_end, g_end)
                if first < end:
                    term = dot(a_ref[first - a_first : end - a_first, :], g_ref[first - g_first : end - g_first, :], 0, 0)
                    total = term if total is None else total + term
        all_ref[:, k * size : (k + 1) * size, :] = total.reshape(parts, size, out)


def expand_grad(info, acts, grads, parts):
    count, mid, out = len(acts), acts[0][0].shape[1], grads[0].shape[1]
    return split_first(
        info, functools.partial(expand_grad_make, count, len(acts[0])), EXPAND_STEPS[0], "expand_grad",
        [a for piece in acts for a in piece] + list(grads), (parts, count * mid // parts, out),
    )


def cut_places_kernel(info_ref, keep_ref, arrived_ref, *refs):
    size = refs[0].shape[0]
    total = (keep_ref[0] + arrived_ref[0].astype(F32)).astype(BF16)
    for k, ref in enumerate(refs):
        ref[...] = total[k * size : (k + 1) * size, :]


def cut_places(info, pair, count):
    rows, out = pair[0].shape[1:]
    return kernel_call(cut_places_kernel, "cut_places", [info, *pair], [((rows // count, out), BF16)] * count)


def place_reduce_kernel(count, info_ref, *refs):
    out_ref, group_ref, more_ref = refs[4:]
    me, number = info_ref[CHAN_AT], part_of(info_ref, REDUCE_STEPS)
    part = out_ref.shape[0] // count
    batches = refs[0].shape[0]
    size = refs[0].shape[1]
    extra = refs[2].shape[1] - size
    for half in range(2):
        for other in range(2):
            ref = refs[2 * half + other]
            for k in range(batches):
                at = number ^ (other * batches + k)
                row = at * size
                to = (me ^ (half * (count // 2) + row // part)) * part + row % part
                out_ref[pl.ds(pl.multiple_of(to, size), size), :] = ref[k, 0:size, :].astype(F32)
                if half == 1:
                    more_ref[pl.ds(pl.multiple_of(at * extra, 8), extra), :] = ref[k, size:, :].astype(F32)
    group_ref[...] = more_ref[0 : group_ref.shape[0], :]


def place_reduce(info, halves, count, part, group_rows):
    batches, rows, mid = halves[1][0].shape
    extra = rows - halves[0][0].shape[1]
    return kernel_call(
        functools.partial(place_reduce_kernel, count), "place_reduce", [info] + [v for pair in halves for v in pair],
        [((part * count, mid), F32), ((group_rows, mid), F32)], [pltpu.VMEM((2 * batches * extra, mid), F32)],
    )


def place_expand_kernel(count, info_ref, own_ref, arrived_ref, out_ref):
    me, number = info_ref[CHAN_AT], part_of(info_ref, EXPAND_STEPS)
    batches, rows, out = own_ref.shape
    size = rows // count
    for other, ref in enumerate((own_ref, arrived_ref)):
        for k in range(batches):
            row = (number ^ (other * batches + k)) * size
            for place in range(count):
                to = pl.ds(pl.multiple_of((me ^ place) * out, out), out)
                out_ref[pl.ds(pl.multiple_of(row, size), size), to] = ref[k, place * size : (place + 1) * size, :].astype(F32)


def place_expand(info, pair, count, mid):
    out = pair[0].shape[2]
    return kernel_call(
        functools.partial(place_expand_kernel, count), "place_expand", [info] + list(pair), [((mid, out * count), F32)]
    )[0]


def plain_weight_grads(inputs, grad, acts, grad_expanded, grad_group):
    count, me = len(inputs), lax.axis_index("chan")
    part, mid = inputs[0][0].shape[1], grad.shape[1]
    grad_reduce = jnp.zeros((part * count, mid), BF16)
    grad_expand = jnp.zeros((mid, part * count), BF16)
    for k in range(count):
        block = dot(jnp.concatenate(inputs[k], 0), grad, 0, 0).astype(BF16)
        grad_reduce = lax.dynamic_update_slice(grad_reduce, block, ((me ^ k) * part, 0))
        block = dot(jnp.concatenate(acts[k], 0), jnp.concatenate(grad_expanded, 0), 0, 0).astype(BF16)
        block = swap(block, k) if k else block
        grad_expand = lax.dynamic_update_slice(grad_expand, block, (0, (me ^ k) * part))
    return [lax.psum(v, REDUCE_AXES).astype(F32) for v in (grad_reduce, grad_expand, grad_group.astype(BF16))]


def shards(
    block_input, w_reduce, w_group, w_expand, gain_one, bias_one, gain_two, bias_two,
    gain_three, bias_three, image_counts, grad_output,
):
    chan_size = lax.axis_size("chan")
    me = lax.axis_index("chan")
    height_at = lax.axis_index("height")
    images, rows, cols, out_part = block_input.shape
    mid_part, group = w_group.shape[3], w_group.shape[2]
    pixels = rows * cols
    per_image = float(pixels * lax.axis_size("height"))
    plan = (pixels, cols)
    distances = range(2, chan_size, 2)
    own_count = jnp.sum(
        jnp.where(jnp.arange(image_counts.shape[0]) == lax.axis_index("batch"), image_counts, 0)
    )
    batch_at = lax.axis_index("batch")
    info = jnp.stack(
        [
            own_count, jnp.sum(image_counts), height_at, me, jnp.where(height_at == 0, pixels - cols, 0),
            batch_at & 1, (batch_at >> 1) & 1,
        ]
    ).astype(jnp.int32)
    parts = lax.axis_size(REDUCE_AXES)
    staged = (lax.axis_size("height"), lax.axis_size("batch")) == (2, 4)

    def edge_swap(edge):
        return permute(edge, "height", 1)

    def sums_of(sums, *waits):
        return staged_sums(sums, *waits) if staged else spread_sums(sums)

    def gather(value, *waits):
        pieces = [value, swap(value, 1)]
        for k in distances:
            pieces.append(swap(value, k))
            pieces.append(swap(after(pieces[k], *waits) if waits else pieces[k], 1))
        return pieces

    field = block_input.reshape(images * pixels, out_part)
    matrices, matrices_back, mid_params, out_params = prepare(
        info, w_group, (gain_one, bias_one, gain_two, bias_two), (gain_three, bias_three)
    )
    columns = cut_columns(info, w_expand, chan_size)
    rows_back = cut_rows(info, w_reduce, chan_size)
    weights = [columns[0], swap(columns[1], 1)]
    reduce_back = [rows_back[0], swap(rows_back[1], 1)]
    inputs = []
    for first, share in cut_images(REDUCE_CHUNKS):
        source = after(field, inputs[0][0], info) if first else field
        piece = lax.slice_in_dim(source, first * pixels, (first + share) * pixels)
        inputs.append(gather(piece, mid_params, weights[1], reduce_back[1]) if first else gather(piece))
    reduced, red_edges, sums = [], [], None
    for pieces, (first, share) in zip(inputs, cut_images(REDUCE_CHUNKS)):
        red, edge, sums = reduce_chunk(info, pieces, (first, share), w_reduce, sums, images, plan, False)
        reduced.append(red)
        red_edges.append(edge_swap(edge))
    inputs = [list(chunks) for chunks in zip(*inputs)]
    weights += [swap(after(columns[k], inputs[2][-1]), k) for k in range(2, chan_size)]
    late_back = [swap(after(rows_back[k], inputs[2][-1]), k) for k in range(3, chan_size)]
    sums_one = spread_sums(sums)

    acts_one, grouped, grp_edge, sums = conv_forward(
        info, reduced, red_edges, sums_one, mid_params, matrices, per_image
    )
    sums_two = spread_sums(after(sums, *weights[2:], *late_back))

    acts = []
    for chunk in cut_images(EXPAND_CHUNKS):
        acts.append(gather(act_two_chunk(info, grouped, sums_two, mid_params, chunk, plan, per_image)))
    expanded, sums = [], None
    for pieces, chunk in zip(acts, cut_images(EXPAND_CHUNKS)):
        out, sums = expand_chunk(info, pieces, weights, chunk, sums, images, plan)
        expanded.append(out)
    acts = [list(chunks) for chunks in zip(*acts)]
    sums_three = spread_sums(sums)
    output, grad_summed, sums = output_pass(
        info, expanded, field.reshape(images, pixels, out_part), grad_output.reshape(images, pixels, out_part), sums_three,
        out_params, per_image,
    )
    grads_three = spread_sums(sums)

    grad_expanded, halves = [], []
    for chunk in cut_images(BACK_CHUNKS):
        grad, near, far = back_expand_chunk(
            info, grad_summed, expanded, sums_three, grads_three, out_params, weights, chunk, mid_part, plan, per_image
        )
        grad_expanded.append(grad)
        halves.append((near, swap(far, 1)))
    own, sent = [], []
    for near, far in halves:
        summed = pair_sum(info, near, far, mid_part)
        own.append(summed[0])
        sent.append([swap(value, k) for value, k in zip(summed[1:], distances)])
    grp_edge = edge_swap(after(grp_edge, own[0]))
    if staged:
        expand_pair = send_half(expand_grad(info, acts, grad_expanded, parts), EXPAND_STEPS[0])
    d_two, d_edges, sums, turn = [], [], None, info
    for c, chunk in enumerate(cut_images(BACK_CHUNKS)):
        if staged and c == 1:
            pair = split_next(after(info, d_two[0]), expand_pair, EXPAND_STEPS[1])
            turn = after(info, pair[0])
            expand_pair = send_half(pair, EXPAND_STEPS[1])
        grad, edge, sums = slope_two_chunk(
            turn, own[c], sent[c], grouped, sums_two, mid_params, chunk, sums, plan, per_image, staged
        )
        d_two.append(grad)
        d_edges.append(edge_swap(edge))
    if staged:
        sums = after(sums, expand_pair[1], grp_edge, d_edges[0])
    grads_two = sums_of(sums, d_edges[-1])
    turn = info
    if staged:
        pair = split_next(after(info, grads_two), expand_pair, EXPAND_STEPS[2])
        turn = after(info, pair[0])
        expand_pair = send_half(pair, EXPAND_STEPS[2])

    d_one, sums, windows = conv_backward(
        turn, d_two, d_edges, grouped, grp_edge, reduced, sums_two, grads_two, sums_one, mid_params, matrices_back, per_image
    )
    if staged:
        reduce_back.append(swap(after(rows_back[2], grads_two), 2))
    grads_one = spread_sums(sums)

    grad = grad_reduced(info, d_one, reduced, sums_one, grads_one, mid_params, per_image)
    grad_field = grad_summed.reshape(images * pixels, out_part)
    if staged:
        half = chan_size // 2
        pairs, turn = [], after(info, grad)

        def in_turn(call, *args):
            nonlocal turn
            result = call(turn, *args)
            turn = after(info, result[0] if isinstance(result, (list, tuple)) else result)
            return result

        def first_half(i):
            own = inputs[i * half : (i + 1) * half]
            pairs.append(send_half(in_turn(reduce_grad, own, grad, parts, taps if i else None), REDUCE_STEPS[0]))

        def next_half(i, step):
            pairs[i] = send_half(in_turn(split_next, pairs[i], REDUCE_STEPS[step]), REDUCE_STEPS[step])

        def last_half(i):
            pairs[i] = send_back(in_turn(add_last, pairs[i]), REDUCE_STEPS[2])

        def back_half(i, step):
            pairs[i] = send_back(in_turn(join, *pairs[i]), REDUCE_STEPS[step])

        reduce_back += late_back
        for word in LAST_PHASE:
            kind, place = word[0], word[1:]
            if kind in "ab":
                i = "ab".index(kind)
                if place == "0":
                    first_half(i)
                elif place in ("1", "2"):
                    next_half(i, int(place))
                elif place == "3":
                    last_half(i)
                else:
                    back_half(i, 5 - int(place))
            elif word == "t":
                taps = in_turn(tap_grads, acts_one, windows, group, cols)
            elif word == "c":
                places = in_turn(cut_places, expand_pair, chan_size)
                places = [v if k == 0 else swap(v, k) for k, v in enumerate(places)]
            elif word == "e0":
                back = in_turn(join, *places)
                back = send_back(back.reshape((1,) + back.shape), EXPAND_STEPS[2])
            elif kind == "e":
                back = send_back(in_turn(join, *back), EXPAND_STEPS[2 - int(place)])
            elif word == "x":
                far_grads = [swap(after(grad, turn), k) for k in distances]
            elif word == "o":
                grads = [grad, swap(after(grad, turn), 1)]
            elif word == "d":
                for value in far_grads:
                    grads += [value, swap(after(value, turn), 1)]
            elif word == "p":
                grad_expand = in_turn(place_expand, back, chan_size, mid_part)
            elif word == "i":
                grad_input = in_turn(input_grad, grad_field, grads, reduce_back)
            elif word == "wo":
                turn = after(turn, grads[1])
            elif word == "wd":
                turn = after(turn, *grads[2:])
            elif word == "wz":
                turn = after(turn, expand_pair[1])
            elif word == "wr":
                turn = after(turn, *reduce_back[2:])
            elif word == "wa":
                turn = after(turn, pairs[0][1])
            elif word == "wb":
                turn = after(turn, pairs[1][1])
            elif word == "we":
                turn = after(turn, back[1])
        grad_reduce, grad_group = place_reduce(turn, pairs, chan_size, out_part, 9 * group)
    else:
        reduce_back += [swap(rows_back[2], 2)] + late_back
        grad_input = input_grad(info, grad_field, gather(grad), reduce_back)
        grad_group = tap_grads(info, acts_one, windows, group, cols)
        grad_reduce, grad_expand, grad_group = plain_weight_grads(inputs, grad, acts, grad_expanded, grad_group)
    vectors = sum_vectors([grads_one, grads_two, grads_three])
    return (
        output.reshape(block_input.shape), grad_input.reshape(block_input.shape), grad_reduce,
        grad_group.reshape(w_group.shape), grad_expand,
        vectors[1], vectors[0], vectors[3], vectors[2], vectors[5], vectors[4],
    )


def solution(mesh):
    split = P("batch", "height", None, "chan")
    vector = P("chan")
    return jax.shard_map(
        shards,
        mesh=mesh,
        in_specs=(
            split, P(None, "chan"), P(None, None, None, "chan"), P("chan", None),
            vector, vector, vector, vector, vector, vector, P(), split,
        ),
        out_specs=(
            split, split, P(None, "chan"), P(None, None, None, "chan"), P("chan", None),
            vector, vector, vector, vector, vector, vector,
        ),
        check_vma=False,
    )
```

```python
import functools

import jax
import jax.numpy as jnp
from jax import lax
from jax.experimental import pallas as pl
from jax.experimental.pallas import tpu as pltpu
from jax.sharding import PartitionSpec as P

EPSILON = 1e-05
STAGE_COST = 2_200_000_000
LAST_PHASE = (
    "wz", "wr", "a0", "t", "b0", "c", "a1", "b1", "e0", "x", "a2", "b2", "e1", "o", "a3", "e2", "b3", "a4",
    "d", "b4", "we", "a5", "wa", "b5", "i", "p",
)
F32, BF16 = jnp.float32, jnp.bfloat16
REDUCE_AXES = ("height", "batch")
REDUCE_CHUNKS, EXPAND_CHUNKS, BACK_CHUNKS = (8, 8), (8, 8), (8, 8)
OWN_COUNT, TOTAL_COUNT, HEIGHT_AT, CHAN_AT, EDGE_ROW, NEAR_AT, FAR_AT = range(7)
VMEM = pl.BlockSpec(memory_space=pltpu.VMEM)
SMEM = pl.BlockSpec(memory_space=pltpu.SMEM)
FAR = pl.BlockSpec(memory_space=pl.ANY)


def dot(a, b, left, right):
    return lax.dot_general(a, b, (((left,), (right,)), ((), ())), preferred_element_type=F32)


def kernel_call(body, name, ins, outs, scratch=(), alias=None, flops=0, room=16, far_outs=0):
    return pl.pallas_call(
        body,
        in_specs=[SMEM if a.dtype == jnp.int32 else VMEM for a in ins],
        out_specs=[FAR] * far_outs + [VMEM] * (len(outs) - far_outs),
        out_shape=[jax.ShapeDtypeStruct(shape, dtype) for shape, dtype in outs],
        scratch_shapes=list(scratch),
        input_output_aliases=alias or {},
        compiler_params=pltpu.CompilerParams(vmem_limit_bytes=room << 20),
        cost_estimate=pl.CostEstimate(flops=flops, bytes_accessed=0, transcendentals=0),
        name=name,
    )(*ins)


def after(value, *others):
    return lax.optimization_barrier((value,) + others)[0]


def permute(value, axis, distance):
    count = lax.axis_size(axis)
    return lax.ppermute(value, axis, [(i, i ^ distance) for i in range(count)])


def swap(value, distance):
    return permute(value, "chan", distance)


def spread_sums(sent):
    return lax.all_to_all(sent, REDUCE_AXES, 0, 0)


def staged_sums(partial, *waits):
    chans = partial.shape[2]
    both = kernel_call(
        add_rows_kernel, "add_rows", [after(partial, *waits), permute(partial, "height", 1)], [((2, chans), F32)]
    )[0]
    others = [permute(both, "batch", k) for k in range(1, lax.axis_size("batch"))]
    return kernel_call(add_sums_kernel, "add_sums", [both] + others, [((1, 2, chans), F32)])[0]


def add_rows_kernel(own_ref, other_ref, out_ref):
    out_ref[...] = jnp.sum(own_ref[...] + other_ref[...], 1)


def add_sums_kernel(*refs):
    total = refs[0][...]
    for ref in refs[1:-1]:
        total = total + ref[...]
    refs[-1][0] = total


def norm_of(sums_ref, total):
    sums = jnp.sum(sums_ref[...], 0)
    average = sums[0:1] / total
    return average, lax.rsqrt(sums[1:2] / total - average * average + EPSILON)


def pixel_count(info_ref, per_image):
    return info_ref[TOTAL_COUNT].astype(F32) * per_image


def sigmoid(v):
    return 0.5 * jnp.tanh(0.5 * v) + 0.5


def silu_slope(v):
    logistic = sigmoid(v)
    return logistic * (1.0 + v * (1.0 - logistic))


def fold(values):
    rows, chans = values.shape
    return jnp.sum(values.reshape(rows // 8, 8, chans), 0)


def put_sums(out_ref, one, two):
    if out_ref.shape[1] == 8:
        out_ref[0] = one
        out_ref[1] = two
    else:
        both = jnp.concatenate([jnp.sum(one, 0, keepdims=True), jnp.sum(two, 0, keepdims=True)], 0)
        out_ref[...] = jnp.broadcast_to(both[None], out_ref.shape)


def sums_out(last, chans):
    return ((lax.axis_size(REDUCE_AXES), 2, chans) if last else (2, 8, chans), F32)


def before_sums(before_ref, chans):
    if before_ref is None:
        zero = jnp.zeros((8, chans), F32)
        return zero, zero
    return before_ref[0], before_ref[1]


def edge_rows(info_ref, ref, image, cols):
    return ref[image, pl.ds(pl.multiple_of(info_ref[EDGE_ROW], 16), cols), :]


def prepare_kernel(group, info_ref, taps_ref, mid_a, mid_b, mid_c, mid_d, out_a, out_b, fwd_ref, back_ref, mid_ref, out_ref):
    chans = taps_ref.shape[2]
    same = (
        lax.broadcasted_iota(jnp.int32, (chans, chans), 0) // group
        == lax.broadcasted_iota(jnp.int32, (chans, chans), 1) // group
    )
    for i in range(3):
        for j in range(3):
            wide = jnp.concatenate([taps_ref[3 * i + j].astype(F32)] * (chans // group), 0)
            wide = jnp.where(same, wide, 0.0)
            fwd_ref[i, j * chans : (j + 1) * chans, :] = wide.astype(BF16)
            back_ref[2 - i, (2 - j) * chans : (3 - j) * chans, :] = wide.T.astype(BF16)
    for row, ref in enumerate((mid_a, mid_b, mid_c, mid_d)):
        mid_ref[row : row + 1, :] = ref[...].astype(F32)
    for row, ref in enumerate((out_a, out_b)):
        out_ref[row : row + 1, :] = ref[...].astype(F32)


def prepare(info, kernel, mid_vectors, out_vectors):
    group, chans = kernel.shape[2], kernel.shape[3]
    wide = (3, 3 * chans, chans)
    rows = [v.reshape(1, -1) for v in list(mid_vectors) + list(out_vectors)]
    return kernel_call(
        functools.partial(prepare_kernel, group), "prepare", [info, kernel.reshape(9, group, chans)] + rows,
        [(wide, BF16), (wide, BF16), ((4, chans), F32), ((2, rows[-1].shape[1]), F32)],
    )


def cut_images(shares):
    return [(sum(shares[:i]), share) for i, share in enumerate(shares)]


def reduce_kernel(first, plan, count, info_ref, *refs):
    pixels, cols = plan
    pieces, w_ref, before_ref = refs[:count], refs[count], None if len(refs) == count + 4 else refs[count + 1]
    red_ref, edge_ref, sums_ref = refs[-3:]
    me = info_ref[CHAN_AT]
    part, images = pieces[0].shape[1], red_ref.shape[0]
    one, two = before_sums(before_ref, w_ref.shape[1])
    step = min(4, images)
    for start in range(0, images, step):
        total = None
        for k in range(count):
            rows = w_ref[pl.ds(pl.multiple_of((me ^ k) * part, part), part), :]
            term = dot(pieces[k][start * pixels : (start + step) * pixels, :], rows, 1, 0)
            total = term if total is None else total + term
        for i in range(start, start + step):
            value = total[(i - start) * pixels : (i - start + 1) * pixels]
            red_ref[i] = value
            edge_ref[i] = edge_rows(info_ref, red_ref, i, cols).astype(BF16)
            value = value * (first + i < info_ref[OWN_COUNT]).astype(F32)
            one, two = one + fold(value), two + fold(value * value)
    put_sums(sums_ref, one, two)


def reduce_chunk(info, pieces, chunk, w_reduce, before, images, plan, staged):
    pixels, cols = plan
    first, share = chunk
    count, mid = len(pieces), w_reduce.shape[1]
    ins = [info] + list(pieces) + [w_reduce] + ([] if before is None else [before])
    return kernel_call(
        functools.partial(reduce_kernel, first, plan, count), "reduce", ins,
        [((share, pixels, mid), F32), ((share, cols, mid), BF16), sums_out(first + share == images and not staged, mid)],
        flops=2 * pieces[0].size * count * mid,
    )


def each_image(chunks, body, carry, step=1):
    first = 0
    for refs in chunks:
        count = refs[0].shape[0]
        start = first
        carry = lax.fori_loop(
            0, count // step, lambda i, c, refs=refs, start=start: body(refs, i * step, start + i * step, c), carry
        )
        first += count
    return carry


def fill_windows(window_ref, slot, value, cols):
    rows, chans = value.shape
    place = lax.broadcasted_iota(jnp.int32, value.shape, 0) % cols
    left = jnp.where(place == 0, 0.0, pltpu.roll(value, 1, 0))
    right = jnp.where(place == cols - 1, 0.0, pltpu.roll(value, rows - 1, 0))
    window_ref[slot, :, 0:chans] = left.astype(BF16)
    window_ref[slot, :, chans : 2 * chans] = value.astype(BF16)
    window_ref[slot, :, 2 * chans : 3 * chans] = right.astype(BF16)


def with_edges(info_ref, own, edge):
    low = (info_ref[HEIGHT_AT] > 0).astype(F32)
    return jnp.concatenate([edge * low, own, edge * (1.0 - low)], 0)


def conv_forward_kernel(
    per_image, group_images, count, info_ref, *refs
):
    fields = list(zip(refs[:count], refs[count : 2 * count]))
    sums_one_ref, par_ref, mat_ref, act_ref, out_ref, out_edge_ref, sums_ref, window_ref = refs[2 * count :]
    images, pixels, chans = act_ref.shape
    cols = out_edge_ref.shape[1]
    average, inv_std = norm_of(sums_one_ref, pixel_count(info_ref, per_image))
    scale, bias = inv_std * par_ref[0:1, :], par_ref[1:2, :]

    def activate(v, keep):
        pre = (v - average) * scale + bias
        return pre * sigmoid(pre) * keep

    def fill(image):
        keep = (image < info_ref[OWN_COUNT]).astype(F32)
        own = activate(at_image([f[0] for f in fields], image), keep)
        edge = activate(at_image([f[1] for f in fields], image).astype(F32), keep)
        act_ref[image] = own.astype(BF16)
        fill_windows(window_ref, image, with_edges(info_ref, own, edge), cols)

    def convolve(first):
        total = None
        for i in range(3):
            piece = window_ref[first : first + group_images, i * cols : i * cols + pixels, :]
            term = dot(piece.reshape(group_images * pixels, 3 * chans), mat_ref[i], 1, 0)
            total = term if total is None else total + term
        out_ref[first : first + group_images] = total.reshape(group_images, pixels, chans)
        return fold(total), fold(total * total)

    one = two = jnp.zeros((8, chans), F32)
    for first in range(0, images + group_images, group_images):
        for image in range(first, min(first + group_images, images)):
            fill(image)
        if first:
            more = convolve(first - group_images)
            one, two = one + more[0], two + more[1]
    for image in range(images):
        out_edge_ref[image] = edge_rows(info_ref, out_ref, image, cols).astype(BF16)
    put_sums(sums_ref, one, two)


def conv_forward(info, reduced, edges, sums_one, params, matrices, per_image):
    images = sum(v.shape[0] for v in reduced)
    pixels, chans = reduced[0].shape[1:]
    cols = edges[0].shape[1]
    shape = (images, pixels, chans)
    return kernel_call(
        functools.partial(conv_forward_kernel, per_image, 4, len(reduced)), "conv_forward",
        [info, *reduced, *edges, sums_one, params, matrices],
        [(shape, BF16), (shape, F32), ((images, cols, chans), BF16), sums_out(True, chans)],
        [pltpu.VMEM((images, pixels + 2 * cols, 3 * chans), BF16)],
    )


def act_two_kernel(chunk, plan, per_image, info_ref, grp_ref, sums_ref, par_ref, out_ref):
    pixels, cols = plan
    first, images = chunk
    average, inv_std = norm_of(sums_ref, pixel_count(info_ref, per_image))
    scale, bias = inv_std * par_ref[2:3, :], par_ref[3:4, :]
    for i in range(images):
        image = first + i
        pre = (grp_ref[image] - average) * scale + bias
        act = pre * sigmoid(pre) * (image < info_ref[OWN_COUNT]).astype(F32)
        out_ref[i * pixels : (i + 1) * pixels] = act.astype(BF16)


def act_two_chunk(info, grouped, sums_two, params, chunk, plan, per_image):
    pixels, cols = plan
    shape = (chunk[1] * pixels, grouped.shape[2])
    return kernel_call(
        functools.partial(act_two_kernel, chunk, plan, per_image), "act_two",
        [info, grouped, sums_two, params], [(shape, BF16)],
    )[0]


def expand_kernel(first, plan, count, mid, info_ref, *refs):
    pixels, cols = plan
    acts, weights = refs[:count], refs[count : 2 * count]
    before_ref = None if len(refs) == 2 * count + 2 else refs[2 * count]
    out_ref, sums_ref = refs[-2:]
    images = out_ref.shape[0]
    one, two = before_sums(before_ref, out_ref.shape[2])
    step = min(4, images)
    for start in range(0, images, step):
        total = None
        for a_ref, w_ref in zip(acts, weights):
            term = dot(a_ref[start * pixels : (start + step) * pixels, :], w_ref[...], 1, 0)
            total = term if total is None else total + term
        out_ref[start : start + step] = total.reshape(step, pixels, total.shape[1])
        for i in range(step):
            keep = (first + start + i < info_ref[OWN_COUNT]).astype(F32)
            value = total[i * pixels : (i + 1) * pixels] * keep
            one, two = one + fold(value), two + fold(value * value)
    put_sums(sums_ref, one, two)


def expand_chunk(info, acts, weights, chunk, before, images, plan):
    pixels, cols = plan
    first, share = chunk
    count, mid, out = len(acts), acts[0].shape[1], weights[0].shape[1]
    ins = [info] + list(acts) + list(weights) + ([] if before is None else [before])
    return kernel_call(
        functools.partial(expand_kernel, first, plan, count, mid), "expand", ins,
        [((share, pixels, out), F32), sums_out(first + share == images, out)],
    )


def output_kernel(per_image, count, info_ref, *refs):
    expanded = [[v] for v in refs[:count]]
    in_ref, go_ref, sums_three_ref, par_ref, far_ref, grad_ref, sums_ref, out_ref, done_ref = refs[count:]
    average, inv_std = norm_of(sums_three_ref, pixel_count(info_ref, per_image))
    gain, bias = par_ref[0:1, :], par_ref[1:2, :]
    chans = out_ref.shape[2]

    def body(refs, at, image, sums):
        keep = (image < info_ref[OWN_COUNT]).astype(F32)
        normalized = (refs[0][at] - average) * inv_std
        summed = normalized * gain + bias + in_ref[image].astype(F32)
        logistic = sigmoid(summed)
        out_ref[image] = (summed * logistic * keep).astype(BF16)
        slope = logistic * (1.0 + summed * (1.0 - logistic))
        grad = go_ref[image].astype(F32) * (slope * keep)
        grad_ref[image] = grad
        pltpu.make_async_copy(out_ref.at[image], far_ref.at[image], done_ref.at[image]).start()
        return sums[0] + fold(grad), sums[1] + fold(grad * normalized)

    zero = jnp.zeros((8, chans), F32)
    put_sums(sums_ref, *each_image(expanded, body, (zero, zero)))
    for image in range(out_ref.shape[0]):
        pltpu.make_async_copy(out_ref.at[image], far_ref.at[image], done_ref.at[image]).wait()


def output_pass(info, expanded, field, grad_output, sums_three, params, per_image):
    return kernel_call(
        functools.partial(output_kernel, per_image, len(expanded)), "output",
        [info, *expanded, field, grad_output, sums_three, params],
        [(field.shape, BF16), (field.shape, F32), sums_out(True, field.shape[2])],
        [pltpu.VMEM(field.shape, BF16), pltpu.SemaphoreType.DMA((field.shape[0],))], far_outs=1,
    )


def at_image(refs, image):
    for ref in refs:
        if image < ref.shape[0]:
            return ref[image]
        image -= ref.shape[0]


def back_expand_kernel(first, plan, count, mid, fields, per_image, info_ref, *refs):
    pixels, cols = plan
    expanded, refs = refs[:fields], refs[fields:]
    grad_ref, sums_three_ref, grads_ref, par_ref = refs[:4]
    weights = refs[4 : 4 + count]
    out_ref, near_ref, far_ref = refs[-3:]
    total = pixel_count(info_ref, per_image)
    average, inv_std = norm_of(sums_three_ref, total)
    grads = jnp.sum(grads_ref[...], 0)
    scale = inv_std * par_ref[0:1, :]
    bias_part, gain_part = grads[0:1] / total, grads[1:2] / total * inv_std
    for i in range(out_ref.shape[0] // pixels):
        image = first + i
        value = grad_ref[image] - (bias_part + (at_image(expanded, image) - average) * gain_part)
        value = value * (scale * (image < info_ref[OWN_COUNT]).astype(F32))
        out_ref[i * pixels : (i + 1) * pixels, :] = value.astype(BF16)
    for k in range(count):
        term = dot(out_ref[...], weights[k][...], 1, 1)
        to = slice((k // 2) * mid, (k // 2 + 1) * mid)
        if k % 2 == 0:
            near_ref[:, to] = term
        else:
            far_ref[:, to] = term.astype(BF16)


def back_expand_chunk(info, grad_summed, expanded, sums_three, grads_three, params, weights, chunk, mid, plan, per_image):
    pixels, cols = plan
    count, out = len(weights), grad_summed.shape[2]
    block, half = chunk[1] * pixels, count // 2 * mid
    return kernel_call(
        functools.partial(back_expand_kernel, chunk[0], plan, count, mid, len(expanded), per_image), "back_expand",
        [info, *expanded, grad_summed, sums_three, grads_three, params, *weights],
        [((block, out), BF16), ((block, half), F32), ((block, half), BF16)],
        flops=2 * block * mid * count * out,
    )


def pair_sum_kernel(info_ref, near_ref, far_ref, own_ref, *send_refs):
    mid = own_ref.shape[1]
    for k, ref in enumerate((own_ref,) + send_refs):
        at = slice(k * mid, (k + 1) * mid)
        ref[...] = (near_ref[:, at] + far_ref[:, at].astype(F32)).astype(ref.dtype)


def pair_sum(info, near, far, mid):
    rows, half = near.shape
    return kernel_call(
        pair_sum_kernel, "pair_sum", [info, near, far],
        [((rows, mid), F32 if k == 0 else BF16) for k in range(half // mid)],
    )


def slope_two_kernel(first, plan, count, per_image, info_ref, own_ref, *refs):
    pixels, cols = plan
    arrived, refs = refs[:count], refs[count:]
    grp_ref, sums_two_ref, par_ref = refs[:3]
    before_ref = None if len(refs) == 6 else refs[3]
    out_ref, edge_ref, sums_ref = refs[-3:]
    average, inv_std = norm_of(sums_two_ref, pixel_count(info_ref, per_image))
    gain, bias = par_ref[2:3, :], par_ref[3:4, :]
    one, two = before_sums(before_ref, grp_ref.shape[2])
    for i in range(out_ref.shape[0]):
        image = first + i
        at = slice(i * pixels, (i + 1) * pixels)
        grad = own_ref[at, :]
        for ref in arrived:
            grad = grad + ref[at, :].astype(F32)
        normalized = (grp_ref[image] - average) * inv_std
        keep = (image < info_ref[OWN_COUNT]).astype(F32)
        grad = grad * (silu_slope(normalized * gain + bias) * keep)
        out_ref[i] = grad
        edge_ref[i] = edge_rows(info_ref, out_ref, i, cols).astype(BF16)
        one, two = one + fold(grad), two + fold(grad * normalized)
    put_sums(sums_ref, one, two)


def slope_two_chunk(info, own, arrived, grouped, sums_two, params, chunk, before, plan, per_image, staged):
    pixels, cols = plan
    first, share = chunk
    images, mid = grouped.shape[0], grouped.shape[2]
    ins = [info, own] + list(arrived) + [grouped, sums_two, params] + ([] if before is None else [before])
    return kernel_call(
        functools.partial(slope_two_kernel, first, plan, len(arrived), per_image), "slope_two", ins,
        [((share, pixels, mid), F32), ((share, cols, mid), BF16), sums_out(first + share == images and not staged, mid)],
    )


def conv_backward_kernel(
    per_image, group_images, d_count, red_count, info_ref, *refs
):
    d_fields, refs = list(zip(refs[:d_count], refs[d_count : 2 * d_count])), refs[2 * d_count :]
    reduced, refs = refs[:red_count], refs[red_count:]
    grp_ref, g_edge_ref, sums_two_ref, grads_two_ref, sums_one_ref, par_ref, mat_ref = refs[:7]
    out_ref, sums_ref, window_ref = refs[7:]
    images, pixels, chans = grp_ref.shape
    cols = g_edge_ref.shape[1]
    total_pixels = pixel_count(info_ref, per_image)
    avg_two, inv_two = norm_of(sums_two_ref, total_pixels)
    grads = jnp.sum(grads_two_ref[...], 0)
    bias_part, gain_part = grads[0:1] / total_pixels, grads[1:2] / total_pixels * inv_two
    scale_two = inv_two * par_ref[2:3, :]
    avg_one, inv_one = norm_of(sums_one_ref, total_pixels)
    gain_one, bias_one = par_ref[0:1, :], par_ref[1:2, :]

    def input_grad(d, grouped, keep):
        return (d - (bias_part + (grouped - avg_two) * gain_part)) * (scale_two * keep)

    def fill(image):
        keep = (image < info_ref[OWN_COUNT]).astype(F32)
        own = input_grad(at_image([f[0] for f in d_fields], image), grp_ref[image], keep)
        edge = at_image([f[1] for f in d_fields], image).astype(F32)
        edge = input_grad(edge, g_edge_ref[image].astype(F32), keep)
        fill_windows(window_ref, image, with_edges(info_ref, own, edge), cols)

    def convolve(first, one, two):
        grad = None
        for i in range(3):
            piece = window_ref[first : first + group_images, i * cols : i * cols + pixels, :]
            term = dot(piece.reshape(group_images * pixels, 3 * chans), mat_ref[i], 1, 0)
            grad = term if grad is None else grad + term
        for i in range(group_images):
            image = first + i
            keep = (image < info_ref[OWN_COUNT]).astype(F32)
            normalized = (at_image(reduced, image) - avg_one) * inv_one
            slope = silu_slope(normalized * gain_one + bias_one)
            d_one = grad[i * pixels : (i + 1) * pixels] * (slope * keep)
            out_ref[image] = d_one
            one, two = one + fold(d_one), two + fold(d_one * normalized)
        return one, two

    one = two = jnp.zeros((8, chans), F32)
    for first in range(0, images + group_images, group_images):
        for image in range(first, min(first + group_images, images)):
            fill(image)
        if first:
            one, two = convolve(first - group_images, one, two)
    put_sums(sums_ref, one, two)


def tap_grads_kernel(group, cols, step, info_ref, act_ref, window_ref, out_ref, turned_ref):
    images, pixels, chans = act_ref.shape
    for image in range(images):
        turned_ref[:, image * pixels : (image + 1) * pixels] = act_ref[image].T
    same = (
        lax.broadcasted_iota(jnp.int32, (chans, 3 * chans), 0) // group
        == lax.broadcasted_iota(jnp.int32, (chans, 3 * chans), 1) % chans // group
    )
    for i in range(3):
        total = None
        for first in range(0, images, step):
            piece = window_ref[first : first + step, i * cols : i * cols + pixels, :]
            turned = turned_ref[:, first * pixels : (first + step) * pixels]
            term = dot(turned, piece.reshape(step * pixels, 3 * chans), 1, 0)
            total = term if total is None else total + term
        total = jnp.sum(jnp.where(same, total, 0.0).reshape(chans // group, group, 3 * chans), 0)
        for j in range(3):
            out_ref[3 * (2 - i) + 2 - j] = total[:, j * chans : (j + 1) * chans]


def tap_grads(info, acts, windows, group, cols):
    images, pixels, chans = acts.shape
    return kernel_call(
        functools.partial(tap_grads_kernel, group, cols, 4), "tap_grads", [info, acts, windows], [((9, group, chans), F32)],
        [pltpu.VMEM((chans, images * pixels), BF16)],
    )[0]


def conv_backward(info, d_two, d_edges, grouped, g_edge, reduced, sums_two, grads_two, sums_one, params, matrices, per_image):
    images, pixels, chans = grouped.shape
    cols = g_edge.shape[1]
    return kernel_call(
        functools.partial(conv_backward_kernel, per_image, 4, len(d_two), len(reduced)), "conv_backward",
        [info, *d_two, *d_edges, *reduced, grouped, g_edge, sums_two, grads_two, sums_one, params, matrices],
        [(grouped.shape, F32), sums_out(True, chans), ((images, pixels + 2 * cols, 3 * chans), BF16)],
    )


def grad_reduced_kernel(per_image, count, info_ref, *refs):
    reduced = [[v] for v in refs[:count]]
    d_ref, sums_one_ref, grads_ref, par_ref, out_ref = refs[count:]
    pixels = d_ref.shape[1]
    total = pixel_count(info_ref, per_image)
    average, inv_std = norm_of(sums_one_ref, total)
    grads = jnp.sum(grads_ref[...], 0)
    bias_part, gain_part = grads[0:1] / total, grads[1:2] / total * inv_std
    scale = inv_std * par_ref[0:1, :]

    def body(refs, at, image, nothing):
        value = d_ref[image] - (bias_part + (refs[0][at] - average) * gain_part)
        value = value * (scale * (image < info_ref[OWN_COUNT]).astype(F32))
        out_ref[pl.ds(pl.multiple_of(image * pixels, pixels), pixels), :] = value.astype(BF16)
        return nothing

    each_image(reduced, body, 0)


def grad_reduced(info, d_one, reduced, sums_one, grads_one, params, per_image):
    images, pixels, mid = d_one.shape
    return kernel_call(
        functools.partial(grad_reduced_kernel, per_image, len(reduced)), "grad_reduced",
        [info, *reduced, d_one, sums_one, grads_one, params], [((images * pixels, mid), BF16)],
    )[0]


def input_grad_kernel(count, info_ref, grad_ref, *refs):
    pieces, weights, out_ref = refs[:count], refs[count : 2 * count], refs[-1]
    rows = 512

    def body(step, nothing):
        at = pl.ds(pl.multiple_of(step * rows, rows), rows)
        total = grad_ref[at, :]
        for p_ref, w_ref in zip(pieces, weights):
            total = total + dot(p_ref[at, :], w_ref[...], 1, 1)
        out_ref[at, :] = total.astype(BF16)
        return nothing

    lax.fori_loop(0, grad_ref.shape[0] // rows, body, 0)


def input_grad(info, grad_summed, pieces, weights):
    return kernel_call(
        functools.partial(input_grad_kernel, len(pieces)), "input_grad", [info, grad_summed] + list(pieces) + list(weights),
        [(grad_summed.shape, BF16)],
    )[0]


def cut_columns_kernel(info_ref, in_ref, *refs):
    for k, ref in enumerate(refs):
        part = ref.shape[1]
        ref[...] = in_ref[:, pl.ds(pl.multiple_of((info_ref[CHAN_AT] ^ k) * part, part), part)]


def cut_columns(info, value, count):
    rows, part = value.shape[0], value.shape[1] // count
    return kernel_call(cut_columns_kernel, "cut_columns", [info, value], [((rows, part), BF16)] * count)


def cut_rows_kernel(info_ref, in_ref, *refs):
    for k, ref in enumerate(refs):
        part = ref.shape[0]
        ref[...] = in_ref[pl.ds(pl.multiple_of((info_ref[CHAN_AT] ^ k) * part, part), part), :]


def cut_rows(info, value, count):
    part, cols = value.shape[0] // count, value.shape[1]
    return kernel_call(cut_rows_kernel, "cut_rows", [info, value], [((part, cols), BF16)] * count)


def sum_vectors_kernel(*refs):
    half = len(refs) // 3
    for ref, out_one, out_two in zip(refs[:half], refs[half::2], refs[half + 1 :: 2]):
        sums = jnp.sum(ref[...], 0)
        out_one[...] = sums[0:1]
        out_two[...] = sums[1:2]


def sum_vectors(values):
    outs = [((1, v.shape[2]), F32) for v in values for _ in range(2)]
    return [v.reshape(-1) for v in kernel_call(sum_vectors_kernel, "sum_vectors", list(values), outs)]


REDUCE_STEPS = (("height", 1, HEIGHT_AT), ("batch", 1, NEAR_AT), ("batch", 2, FAR_AT))
EXPAND_STEPS = (("height", 1, HEIGHT_AT), ("batch", 1, NEAR_AT), ("batch", 2, FAR_AT))


def part_of(info_ref, steps):
    number = 0
    for _, _, field in steps:
        number = number * 2 + info_ref[field]
    return number


def send_half(pair, step):
    return pair[0], permute(pair[1], step[0], step[1])


def split(at, keep_ref, send_ref, all_ref, arrived_ref):
    half = keep_ref.shape[0]
    for to, ref in ((at, keep_ref), (1 - at, send_ref)):
        value = all_ref[pl.ds(to * half, half)]
        if arrived_ref is not None:
            value = value + arrived_ref[pl.ds(to * half, half)].astype(F32)
        ref[...] = value.astype(ref.dtype)


def split_first_kernel(make, field, info_ref, *refs):
    keep_ref, send_ref, all_ref = refs[-3:]
    make(refs[:-3], all_ref)
    split(info_ref[field], keep_ref, send_ref, all_ref, None)


def split_first(info, make, step, name, ins, shape):
    half = (shape[0] // 2,) + shape[1:]
    return kernel_call(
        functools.partial(split_first_kernel, make, step[2]), name, [info] + ins, [(half, F32), (half, BF16)],
        [pltpu.VMEM(shape, F32)],
    )


def split_next_kernel(field, info_ref, keep_ref, arrived_ref, out_ref, send_ref):
    split(info_ref[field], out_ref, send_ref, keep_ref, arrived_ref)


def split_next(info, pair, step):
    half = (pair[0].shape[0] // 2,) + pair[0].shape[1:]
    return kernel_call(
        functools.partial(split_next_kernel, step[2]), "split_next", [info, *pair], [(half, F32), (half, BF16)], flops=STAGE_COST
    )


def add_kernel(info_ref, first_ref, second_ref, out_ref):
    out_ref[...] = (first_ref[...] + second_ref[...].astype(F32)).astype(BF16)


def add_last(info, pair):
    return kernel_call(add_kernel, "add_last", [info, *pair], [(pair[0].shape, BF16)], flops=STAGE_COST)[0]


def join_kernel(info_ref, *refs):
    size = refs[0].shape[0]
    for k, ref in enumerate(refs[:-1]):
        refs[-1][k * size : (k + 1) * size] = ref[...]


def join(info, *values):
    shape = (values[0].shape[0] * len(values),) + values[0].shape[1:]
    return kernel_call(join_kernel, "join", [info, *values], [(shape, BF16)], flops=STAGE_COST)[0]


def send_back(value, step):
    return value, permute(value, step[0], step[1])


def reduce_grad_make(places, spans, extra, refs, all_ref):
    grad_ref = refs[places * len(spans)]
    parts = all_ref.shape[0]
    per = parts // places
    for k in range(places):
        total = None
        for c, (first, end) in enumerate(spans):
            term = dot(refs[k * len(spans) + c][...], grad_ref[first:end, :], 0, 0)
            total = term if total is None else total + term
        size = total.shape[0] // per
        all_ref[k * per : (k + 1) * per, 0:size, :] = total.reshape(per, size, total.shape[1])
    if extra:
        more = refs[-1][...]
        more = more.reshape(-1, more.shape[2])
        room = parts * extra - more.shape[0]
        more = jnp.concatenate([more, jnp.zeros((room, more.shape[1]), F32)], 0)
        all_ref[:, size : size + extra, :] = more.reshape(parts, extra, more.shape[1])


def reduce_grad(info, inputs, grad, parts, more):
    spans = spans_of(inputs[0])
    rows, mid = len(inputs) * inputs[0][0].shape[1], grad.shape[1]
    extra = 0 if more is None else -(-more.shape[0] * more.shape[1] // (8 * parts)) * 8
    ins = [v for piece in inputs for v in piece] + [grad] + ([] if more is None else [more])
    return split_first(
        info, functools.partial(reduce_grad_make, len(inputs), tuple(spans), extra), REDUCE_STEPS[0], "reduce_grad", ins,
        (parts, rows // parts + extra, mid),
    )


def spans_of(values):
    spans, at = [], 0
    for value in values:
        spans.append((at, at + value.shape[0]))
        at += value.shape[0]
    return spans


def expand_grad_make(count, chunks, refs, all_ref):
    acts, grads = refs[: count * chunks], refs[count * chunks :]
    parts, wide, out = all_ref.shape
    size = wide // count
    for k in range(count):
        total = None
        own = acts[k * chunks : (k + 1) * chunks]
        for a_ref, (a_first, a_end) in zip(own, spans_of(own)):
            for g_ref, (g_first, g_end) in zip(grads, spans_of(grads)):
                first, end = max(a_first, g_first), min(a_end, g_end)
                if first < end:
                    term = dot(a_ref[first - a_first : end - a_first, :], g_ref[first - g_first : end - g_first, :], 0, 0)
                    total = term if total is None else total + term
        all_ref[:, k * size : (k + 1) * size, :] = total.reshape(parts, size, out)


def expand_grad(info, acts, grads, parts):
    count, mid, out = len(acts), acts[0][0].shape[1], grads[0].shape[1]
    return split_first(
        info, functools.partial(expand_grad_make, count, len(acts[0])), EXPAND_STEPS[0], "expand_grad",
        [a for piece in acts for a in piece] + list(grads), (parts, count * mid // parts, out),
    )


def cut_places_kernel(info_ref, keep_ref, arrived_ref, *refs):
    size = refs[0].shape[0]
    total = (keep_ref[0] + arrived_ref[0].astype(F32)).astype(BF16)
    for k, ref in enumerate(refs):
        ref[...] = total[k * size : (k + 1) * size, :]


def cut_places(info, pair, count):
    rows, out = pair[0].shape[1:]
    return kernel_call(cut_places_kernel, "cut_places", [info, *pair], [((rows // count, out), BF16)] * count)


def place_reduce_kernel(count, info_ref, *refs):
    out_ref, group_ref, more_ref = refs[4:]
    me, number = info_ref[CHAN_AT], part_of(info_ref, REDUCE_STEPS)
    part = out_ref.shape[0] // count
    batches = refs[0].shape[0]
    size = refs[0].shape[1]
    extra = refs[2].shape[1] - size
    for half in range(2):
        for other in range(2):
            ref = refs[2 * half + other]
            for k in range(batches):
                at = number ^ (other * batches + k)
                row = at * size
                to = (me ^ (half * (count // 2) + row // part)) * part + row % part
                out_ref[pl.ds(pl.multiple_of(to, size), size), :] = ref[k, 0:size, :].astype(F32)
                if half == 1:
                    more_ref[pl.ds(pl.multiple_of(at * extra, 8), extra), :] = ref[k, size:, :].astype(F32)
    group_ref[...] = more_ref[0 : group_ref.shape[0], :]


def place_reduce(info, halves, count, part, group_rows):
    batches, rows, mid = halves[1][0].shape
    extra = rows - halves[0][0].shape[1]
    return kernel_call(
        functools.partial(place_reduce_kernel, count), "place_reduce", [info] + [v for pair in halves for v in pair],
        [((part * count, mid), F32), ((group_rows, mid), F32)], [pltpu.VMEM((2 * batches * extra, mid), F32)],
    )


def place_expand_kernel(count, info_ref, own_ref, arrived_ref, out_ref):
    me, number = info_ref[CHAN_AT], part_of(info_ref, EXPAND_STEPS)
    batches, rows, out = own_ref.shape
    size = rows // count
    for other, ref in enumerate((own_ref, arrived_ref)):
        for k in range(batches):
            row = (number ^ (other * batches + k)) * size
            for place in range(count):
                to = pl.ds(pl.multiple_of((me ^ place) * out, out), out)
                out_ref[pl.ds(pl.multiple_of(row, size), size), to] = ref[k, place * size : (place + 1) * size, :].astype(F32)


def place_expand(info, pair, count, mid):
    out = pair[0].shape[2]
    return kernel_call(
        functools.partial(place_expand_kernel, count), "place_expand", [info] + list(pair), [((mid, out * count), F32)]
    )[0]


def plain_weight_grads(inputs, grad, acts, grad_expanded, grad_group):
    count, me = len(inputs), lax.axis_index("chan")
    part, mid = inputs[0][0].shape[1], grad.shape[1]
    grad_reduce = jnp.zeros((part * count, mid), BF16)
    grad_expand = jnp.zeros((mid, part * count), BF16)
    for k in range(count):
        block = dot(jnp.concatenate(inputs[k], 0), grad, 0, 0).astype(BF16)
        grad_reduce = lax.dynamic_update_slice(grad_reduce, block, ((me ^ k) * part, 0))
        block = dot(jnp.concatenate(acts[k], 0), jnp.concatenate(grad_expanded, 0), 0, 0).astype(BF16)
        block = swap(block, k) if k else block
        grad_expand = lax.dynamic_update_slice(grad_expand, block, (0, (me ^ k) * part))
    return [lax.psum(v, REDUCE_AXES).astype(F32) for v in (grad_reduce, grad_expand, grad_group.astype(BF16))]


def shards(
    block_input, w_reduce, w_group, w_expand, gain_one, bias_one, gain_two, bias_two,
    gain_three, bias_three, image_counts, grad_output,
):
    chan_size = lax.axis_size("chan")
    me = lax.axis_index("chan")
    height_at = lax.axis_index("height")
    images, rows, cols, out_part = block_input.shape
    mid_part, group = w_group.shape[3], w_group.shape[2]
    pixels = rows * cols
    per_image = float(pixels * lax.axis_size("height"))
    plan = (pixels, cols)
    distances = range(2, chan_size, 2)
    own_count = jnp.sum(
        jnp.where(jnp.arange(image_counts.shape[0]) == lax.axis_index("batch"), image_counts, 0)
    )
    batch_at = lax.axis_index("batch")
    info = jnp.stack(
        [
            own_count, jnp.sum(image_counts), height_at, me, jnp.where(height_at == 0, pixels - cols, 0),
            batch_at & 1, (batch_at >> 1) & 1,
        ]
    ).astype(jnp.int32)
    parts = lax.axis_size(REDUCE_AXES)
    staged = (lax.axis_size("height"), lax.axis_size("batch")) == (2, 4)

    def edge_swap(edge):
        return permute(edge, "height", 1)

    def sums_of(sums, *waits):
        return staged_sums(sums, *waits) if staged else spread_sums(sums)

    def gather(value, *waits):
        pieces = [value, swap(value, 1)]
        for k in distances:
            pieces.append(swap(value, k))
            pieces.append(swap(after(pieces[k], *waits) if waits else pieces[k], 1))
        return pieces

    field = block_input.reshape(images * pixels, out_part)
    matrices, matrices_back, mid_params, out_params = prepare(
        info, w_group, (gain_one, bias_one, gain_two, bias_two), (gain_three, bias_three)
    )
    columns = cut_columns(info, w_expand, chan_size)
    rows_back = cut_rows(info, w_reduce, chan_size)
    weights = [columns[0], swap(columns[1], 1)]
    reduce_back = [rows_back[0], swap(rows_back[1], 1)]
    inputs = []
    for first, share in cut_images(REDUCE_CHUNKS):
        source = after(field, inputs[0][0], info) if first else field
        piece = lax.slice_in_dim(source, first * pixels, (first + share) * pixels)
        inputs.append(gather(piece, mid_params, weights[1], reduce_back[1]) if first else gather(piece))
    reduced, red_edges, sums = [], [], None
    for pieces, (first, share) in zip(inputs, cut_images(REDUCE_CHUNKS)):
        red, edge, sums = reduce_chunk(info, pieces, (first, share), w_reduce, sums, images, plan, False)
        reduced.append(red)
        red_edges.append(edge_swap(edge))
    inputs = [list(chunks) for chunks in zip(*inputs)]
    weights += [swap(after(columns[k], inputs[2][-1]), k) for k in range(2, chan_size)]
    late_back = [swap(after(rows_back[k], inputs[2][-1]), k) for k in range(3, chan_size)]
    sums_one = spread_sums(sums)

    acts_one, grouped, grp_edge, sums = conv_forward(
        info, reduced, red_edges, sums_one, mid_params, matrices, per_image
    )
    sums_two = spread_sums(after(sums, *weights[2:], *late_back))

    acts = []
    for chunk in cut_images(EXPAND_CHUNKS):
        acts.append(gather(act_two_chunk(info, grouped, sums_two, mid_params, chunk, plan, per_image)))
    expanded, sums = [], None
    for pieces, chunk in zip(acts, cut_images(EXPAND_CHUNKS)):
        out, sums = expand_chunk(info, pieces, weights, chunk, sums, images, plan)
        expanded.append(out)
    acts = [list(chunks) for chunks in zip(*acts)]
    sums_three = spread_sums(sums)
    output, grad_summed, sums = output_pass(
        info, expanded, field.reshape(images, pixels, out_part), grad_output.reshape(images, pixels, out_part), sums_three,
        out_params, per_image,
    )
    grads_three = spread_sums(sums)

    grad_expanded, halves = [], []
    for chunk in cut_images(BACK_CHUNKS):
        grad, near, far = back_expand_chunk(
            info, grad_summed, expanded, sums_three, grads_three, out_params, weights, chunk, mid_part, plan, per_image
        )
        grad_expanded.append(grad)
        halves.append((near, swap(far, 1)))
    own, sent = [], []
    for near, far in halves:
        summed = pair_sum(info, near, far, mid_part)
        own.append(summed[0])
        sent.append([swap(value, k) for value, k in zip(summed[1:], distances)])
    grp_edge = edge_swap(after(grp_edge, own[0]))
    if staged:
        expand_pair = send_half(expand_grad(info, acts, grad_expanded, parts), EXPAND_STEPS[0])
    d_two, d_edges, sums, turn = [], [], None, info
    for c, chunk in enumerate(cut_images(BACK_CHUNKS)):
        if staged and c == 1:
            pair = split_next(after(info, d_two[0]), expand_pair, EXPAND_STEPS[1])
            turn = after(info, pair[0])
            expand_pair = send_half(pair, EXPAND_STEPS[1])
        grad, edge, sums = slope_two_chunk(
            turn, own[c], sent[c], grouped, sums_two, mid_params, chunk, sums, plan, per_image, staged
        )
        d_two.append(grad)
        d_edges.append(edge_swap(edge))
    if staged:
        sums = after(sums, expand_pair[1], grp_edge, d_edges[0])
    grads_two = sums_of(sums, d_edges[-1])
    turn = info
    if staged:
        pair = split_next(after(info, grads_two), expand_pair, EXPAND_STEPS[2])
        turn = after(info, pair[0])
        expand_pair = send_half(pair, EXPAND_STEPS[2])

    d_one, sums, windows = conv_backward(
        turn, d_two, d_edges, grouped, grp_edge, reduced, sums_two, grads_two, sums_one, mid_params, matrices_back, per_image
    )
    if staged:
        reduce_back.append(swap(after(rows_back[2], grads_two), 2))
    grads_one = spread_sums(sums)

    grad = grad_reduced(info, d_one, reduced, sums_one, grads_one, mid_params, per_image)
    grad_field = grad_summed.reshape(images * pixels, out_part)
    if staged:
        half = chan_size // 2
        pairs, turn = [], after(info, grad)

        def in_turn(call, *args):
            nonlocal turn
            result = call(turn, *args)
            turn = after(info, result[0] if isinstance(result, (list, tuple)) else result)
            return result

        def first_half(i):
            own = inputs[i * half : (i + 1) * half]
            pairs.append(send_half(in_turn(reduce_grad, own, grad, parts, taps if i else None), REDUCE_STEPS[0]))

        def next_half(i, step):
            pairs[i] = send_half(in_turn(split_next, pairs[i], REDUCE_STEPS[step]), REDUCE_STEPS[step])

        def last_half(i):
            pairs[i] = send_back(in_turn(add_last, pairs[i]), REDUCE_STEPS[2])

        def back_half(i, step):
            pairs[i] = send_back(in_turn(join, *pairs[i]), REDUCE_STEPS[step])

        reduce_back += late_back
        for word in LAST_PHASE:
            kind, place = word[0], word[1:]
            if kind in "ab":
                i = "ab".index(kind)
                if place == "0":
                    first_half(i)
                elif place in ("1", "2"):
                    next_half(i, int(place))
                elif place == "3":
                    last_half(i)
                else:
                    back_half(i, 5 - int(place))
            elif word == "t":
                taps = in_turn(tap_grads, acts_one, windows, group, cols)
            elif word == "c":
                places = in_turn(cut_places, expand_pair, chan_size)
                places = [v if k == 0 else swap(v, k) for k, v in enumerate(places)]
            elif word == "e0":
                back = in_turn(join, *places)
                back = send_back(back.reshape((1,) + back.shape), EXPAND_STEPS[2])
            elif kind == "e":
                back = send_back(in_turn(join, *back), EXPAND_STEPS[2 - int(place)])
            elif word == "x":
                far_grads = [swap(after(grad, turn), k) for k in distances]
            elif word == "o":
                grads = [grad, swap(after(grad, turn), 1)]
            elif word == "d":
                for value in far_grads:
                    grads += [value, swap(after(value, turn), 1)]
            elif word == "p":
                grad_expand = in_turn(place_expand, back, chan_size, mid_part)
            elif word == "i":
                grad_input = in_turn(input_grad, grad_field, grads, reduce_back)
            elif word == "wo":
                turn = after(turn, grads[1])
            elif word == "wd":
                turn = after(turn, *grads[2:])
            elif word == "wz":
                turn = after(turn, expand_pair[1])
            elif word == "wr":
                turn = after(turn, *reduce_back[2:])
            elif word == "wa":
                turn = after(turn, pairs[0][1])
            elif word == "wb":
                turn = after(turn, pairs[1][1])
            elif word == "we":
                turn = after(turn, back[1])
        grad_reduce, grad_group = place_reduce(turn, pairs, chan_size, out_part, 9 * group)
    else:
        reduce_back += [swap(rows_back[2], 2)] + late_back
        grad_input = input_grad(info, grad_field, gather(grad), reduce_back)
        grad_group = tap_grads(info, acts_one, windows, group, cols)
        grad_reduce, grad_expand, grad_group = plain_weight_grads(inputs, grad, acts, grad_expanded, grad_group)
    vectors = sum_vectors([grads_one, grads_two, grads_three])
    return (
        output.reshape(block_input.shape), grad_input.reshape(block_input.shape), grad_reduce,
        grad_group.reshape(w_group.shape), grad_expand,
        vectors[1], vectors[0], vectors[3], vectors[2], vectors[5], vectors[4],
    )


def solution(mesh):
    split = P("batch", "height", None, "chan")
    vector = P("chan")
    return jax.shard_map(
        shards,
        mesh=mesh,
        in_specs=(
            split, P(None, "chan"), P(None, None, None, "chan"), P("chan", None),
            vector, vector, vector, vector, vector, vector, P(), split,
        ),
        out_specs=(
            split, split, P(None, "chan"), P(None, None, None, "chan"), P("chan", None),
            vector, vector, vector, vector, vector, vector,
        ),
        check_vma=False,
    )
```

```python
import functools

import jax
import jax.numpy as jnp
from jax import lax
from jax.experimental import pallas as pl
from jax.experimental.pallas import tpu as pltpu
from jax.sharding import PartitionSpec as P

EPSILON = 1e-05
SPLIT_COST, ADD_COST, STAGE_COST = 1_800_000_000, 3_000_000_000, 2_200_000_000
LAST_PHASE = (
    "wz", "wr", "a0", "t", "b0", "c", "a1", "b1", "e0", "x", "a2", "b2", "e1", "o", "a3", "e2", "b3", "a4",
    "d", "b4", "we", "a5", "wa", "b5", "i", "p",
)
F32, BF16 = jnp.float32, jnp.bfloat16
REDUCE_AXES = ("height", "batch")
REDUCE_CHUNKS, EXPAND_CHUNKS, BACK_CHUNKS = (8, 8), (8, 8), (8, 8)
OWN_COUNT, TOTAL_COUNT, HEIGHT_AT, CHAN_AT, EDGE_ROW, NEAR_AT, FAR_AT = range(7)
VMEM = pl.BlockSpec(memory_space=pltpu.VMEM)
SMEM = pl.BlockSpec(memory_space=pltpu.SMEM)
FAR = pl.BlockSpec(memory_space=pl.ANY)


def dot(a, b, left, right):
    return lax.dot_general(a, b, (((left,), (right,)), ((), ())), preferred_element_type=F32)


def kernel_call(body, name, ins, outs, scratch=(), alias=None, flops=0, room=16, far_outs=0):
    return pl.pallas_call(
        body,
        in_specs=[SMEM if a.dtype == jnp.int32 else VMEM for a in ins],
        out_specs=[FAR] * far_outs + [VMEM] * (len(outs) - far_outs),
        out_shape=[jax.ShapeDtypeStruct(shape, dtype) for shape, dtype in outs],
        scratch_shapes=list(scratch),
        input_output_aliases=alias or {},
        compiler_params=pltpu.CompilerParams(vmem_limit_bytes=room << 20),
        cost_estimate=pl.CostEstimate(flops=flops, bytes_accessed=0, transcendentals=0),
        name=name,
    )(*ins)


def after(value, *others):
    return lax.optimization_barrier((value,) + others)[0]


def permute(value, axis, distance):
    count = lax.axis_size(axis)
    return lax.ppermute(value, axis, [(i, i ^ distance) for i in range(count)])


def swap(value, distance):
    return permute(value, "chan", distance)


def spread_sums(sent):
    return lax.all_to_all(sent, REDUCE_AXES, 0, 0)


def staged_sums(partial, *waits):
    chans = partial.shape[2]
    both = kernel_call(
        add_rows_kernel, "add_rows", [after(partial, *waits), permute(partial, "height", 1)], [((2, chans), F32)]
    )[0]
    others = [permute(both, "batch", k) for k in range(1, lax.axis_size("batch"))]
    return kernel_call(add_sums_kernel, "add_sums", [both] + others, [((1, 2, chans), F32)])[0]


def add_rows_kernel(own_ref, other_ref, out_ref):
    out_ref[...] = jnp.sum(own_ref[...] + other_ref[...], 1)


def add_sums_kernel(*refs):
    total = refs[0][...]
    for ref in refs[1:-1]:
        total = total + ref[...]
    refs[-1][0] = total


def norm_of(sums_ref, total):
    sums = jnp.sum(sums_ref[...], 0)
    average = sums[0:1] / total
    return average, lax.rsqrt(sums[1:2] / total - average * average + EPSILON)


def pixel_count(info_ref, per_image):
    return info_ref[TOTAL_COUNT].astype(F32) * per_image


def sigmoid(v):
    return 0.5 * jnp.tanh(0.5 * v) + 0.5


def silu_slope(v):
    logistic = sigmoid(v)
    return logistic * (1.0 + v * (1.0 - logistic))


def fold(values):
    rows, chans = values.shape
    return jnp.sum(values.reshape(rows // 8, 8, chans), 0)


def put_sums(out_ref, one, two):
    if out_ref.shape[1] == 8:
        out_ref[0] = one
        out_ref[1] = two
    else:
        both = jnp.concatenate([jnp.sum(one, 0, keepdims=True), jnp.sum(two, 0, keepdims=True)], 0)
        out_ref[...] = jnp.broadcast_to(both[None], out_ref.shape)


def sums_out(last, chans):
    return ((lax.axis_size(REDUCE_AXES), 2, chans) if last else (2, 8, chans), F32)


def before_sums(before_ref, chans):
    if before_ref is None:
        zero = jnp.zeros((8, chans), F32)
        return zero, zero
    return before_ref[0], before_ref[1]


def edge_rows(info_ref, ref, image, cols):
    return ref[image, pl.ds(pl.multiple_of(info_ref[EDGE_ROW], 16), cols), :]


def prepare_kernel(group, info_ref, taps_ref, mid_a, mid_b, mid_c, mid_d, out_a, out_b, fwd_ref, back_ref, mid_ref, out_ref):
    chans = taps_ref.shape[2]
    same = (
        lax.broadcasted_iota(jnp.int32, (chans, chans), 0) // group
        == lax.broadcasted_iota(jnp.int32, (chans, chans), 1) // group
    )
    for i in range(3):
        for j in range(3):
            wide = jnp.concatenate([taps_ref[3 * i + j].astype(F32)] * (chans // group), 0)
            wide = jnp.where(same, wide, 0.0)
            fwd_ref[i, j * chans : (j + 1) * chans, :] = wide.astype(BF16)
            back_ref[2 - i, (2 - j) * chans : (3 - j) * chans, :] = wide.T.astype(BF16)
    for row, ref in enumerate((mid_a, mid_b, mid_c, mid_d)):
        mid_ref[row : row + 1, :] = ref[...].astype(F32)
    for row, ref in enumerate((out_a, out_b)):
        out_ref[row : row + 1, :] = ref[...].astype(F32)


def prepare(info, kernel, mid_vectors, out_vectors):
    group, chans = kernel.shape[2], kernel.shape[3]
    wide = (3, 3 * chans, chans)
    rows = [v.reshape(1, -1) for v in list(mid_vectors) + list(out_vectors)]
    return kernel_call(
        functools.partial(prepare_kernel, group), "prepare", [info, kernel.reshape(9, group, chans)] + rows,
        [(wide, BF16), (wide, BF16), ((4, chans), F32), ((2, rows[-1].shape[1]), F32)],
    )


def cut_images(shares):
    return [(sum(shares[:i]), share) for i, share in enumerate(shares)]


def reduce_kernel(first, plan, count, info_ref, *refs):
    pixels, cols = plan
    pieces, w_ref, before_ref = refs[:count], refs[count], None if len(refs) == count + 4 else refs[count + 1]
    red_ref, edge_ref, sums_ref = refs[-3:]
    me = info_ref[CHAN_AT]
    part, images = pieces[0].shape[1], red_ref.shape[0]
    one, two = before_sums(before_ref, w_ref.shape[1])
    step = min(4, images)
    for start in range(0, images, step):
        total = None
        for k in range(count):
            rows = w_ref[pl.ds(pl.multiple_of((me ^ k) * part, part), part), :]
            term = dot(pieces[k][start * pixels : (start + step) * pixels, :], rows, 1, 0)
            total = term if total is None else total + term
        for i in range(start, start + step):
            value = total[(i - start) * pixels : (i - start + 1) * pixels]
            red_ref[i] = value
            edge_ref[i] = edge_rows(info_ref, red_ref, i, cols).astype(BF16)
            value = value * (first + i < info_ref[OWN_COUNT]).astype(F32)
            one, two = one + fold(value), two + fold(value * value)
    put_sums(sums_ref, one, two)


def reduce_chunk(info, pieces, chunk, w_reduce, before, images, plan, staged):
    pixels, cols = plan
    first, share = chunk
    count, mid = len(pieces), w_reduce.shape[1]
    ins = [info] + list(pieces) + [w_reduce] + ([] if before is None else [before])
    return kernel_call(
        functools.partial(reduce_kernel, first, plan, count), "reduce", ins,
        [((share, pixels, mid), F32), ((share, cols, mid), BF16), sums_out(first + share == images and not staged, mid)],
        flops=2 * pieces[0].size * count * mid,
    )


def each_image(chunks, body, carry, step=1):
    first = 0
    for refs in chunks:
        count = refs[0].shape[0]
        start = first
        carry = lax.fori_loop(
            0, count // step, lambda i, c, refs=refs, start=start: body(refs, i * step, start + i * step, c), carry
        )
        first += count
    return carry


def fill_windows(window_ref, slot, value, cols):
    rows, chans = value.shape
    place = lax.broadcasted_iota(jnp.int32, value.shape, 0) % cols
    left = jnp.where(place == 0, 0.0, pltpu.roll(value, 1, 0))
    right = jnp.where(place == cols - 1, 0.0, pltpu.roll(value, rows - 1, 0))
    window_ref[slot, :, 0:chans] = left.astype(BF16)
    window_ref[slot, :, chans : 2 * chans] = value.astype(BF16)
    window_ref[slot, :, 2 * chans : 3 * chans] = right.astype(BF16)


def with_edges(info_ref, own, edge):
    low = (info_ref[HEIGHT_AT] > 0).astype(F32)
    return jnp.concatenate([edge * low, own, edge * (1.0 - low)], 0)


def conv_forward_kernel(
    per_image, group_images, count, info_ref, *refs
):
    fields = list(zip(refs[:count], refs[count : 2 * count]))
    sums_one_ref, par_ref, mat_ref, act_ref, out_ref, out_edge_ref, sums_ref, window_ref = refs[2 * count :]
    images, pixels, chans = act_ref.shape
    cols = out_edge_ref.shape[1]
    average, inv_std = norm_of(sums_one_ref, pixel_count(info_ref, per_image))
    scale, bias = inv_std * par_ref[0:1, :], par_ref[1:2, :]

    def activate(v, keep):
        pre = (v - average) * scale + bias
        return pre * sigmoid(pre) * keep

    def fill(image):
        keep = (image < info_ref[OWN_COUNT]).astype(F32)
        own = activate(at_image([f[0] for f in fields], image), keep)
        edge = activate(at_image([f[1] for f in fields], image).astype(F32), keep)
        act_ref[image] = own.astype(BF16)
        fill_windows(window_ref, image, with_edges(info_ref, own, edge), cols)

    def convolve(first):
        total = None
        for i in range(3):
            piece = window_ref[first : first + group_images, i * cols : i * cols + pixels, :]
            term = dot(piece.reshape(group_images * pixels, 3 * chans), mat_ref[i], 1, 0)
            total = term if total is None else total + term
        out_ref[first : first + group_images] = total.reshape(group_images, pixels, chans)
        return fold(total), fold(total * total)

    one = two = jnp.zeros((8, chans), F32)
    for first in range(0, images + group_images, group_images):
        for image in range(first, min(first + group_images, images)):
            fill(image)
        if first:
            more = convolve(first - group_images)
            one, two = one + more[0], two + more[1]
    for image in range(images):
        out_edge_ref[image] = edge_rows(info_ref, out_ref, image, cols).astype(BF16)
    put_sums(sums_ref, one, two)


def conv_forward(info, reduced, edges, sums_one, params, matrices, per_image):
    images = sum(v.shape[0] for v in reduced)
    pixels, chans = reduced[0].shape[1:]
    cols = edges[0].shape[1]
    shape = (images, pixels, chans)
    return kernel_call(
        functools.partial(conv_forward_kernel, per_image, 4, len(reduced)), "conv_forward",
        [info, *reduced, *edges, sums_one, params, matrices],
        [(shape, BF16), (shape, F32), ((images, cols, chans), BF16), sums_out(True, chans)],
        [pltpu.VMEM((images, pixels + 2 * cols, 3 * chans), BF16)],
    )


def act_two_kernel(chunk, plan, per_image, info_ref, grp_ref, sums_ref, par_ref, out_ref):
    pixels, cols = plan
    first, images = chunk
    average, inv_std = norm_of(sums_ref, pixel_count(info_ref, per_image))
    scale, bias = inv_std * par_ref[2:3, :], par_ref[3:4, :]
    for i in range(images):
        image = first + i
        pre = (grp_ref[image] - average) * scale + bias
        act = pre * sigmoid(pre) * (image < info_ref[OWN_COUNT]).astype(F32)
        out_ref[i * pixels : (i + 1) * pixels] = act.astype(BF16)


def act_two_chunk(info, grouped, sums_two, params, chunk, plan, per_image):
    pixels, cols = plan
    shape = (chunk[1] * pixels, grouped.shape[2])
    return kernel_call(
        functools.partial(act_two_kernel, chunk, plan, per_image), "act_two",
        [info, grouped, sums_two, params], [(shape, BF16)],
    )[0]


def expand_kernel(first, plan, count, mid, info_ref, *refs):
    pixels, cols = plan
    acts, weights = refs[:count], refs[count : 2 * count]
    before_ref = None if len(refs) == 2 * count + 2 else refs[2 * count]
    out_ref, sums_ref = refs[-2:]
    images = out_ref.shape[0]
    one, two = before_sums(before_ref, out_ref.shape[2])
    step = min(4, images)
    for start in range(0, images, step):
        total = None
        for a_ref, w_ref in zip(acts, weights):
            term = dot(a_ref[start * pixels : (start + step) * pixels, :], w_ref[...], 1, 0)
            total = term if total is None else total + term
        out_ref[start : start + step] = total.reshape(step, pixels, total.shape[1])
        for i in range(step):
            keep = (first + start + i < info_ref[OWN_COUNT]).astype(F32)
            value = total[i * pixels : (i + 1) * pixels] * keep
            one, two = one + fold(value), two + fold(value * value)
    put_sums(sums_ref, one, two)


def expand_chunk(info, acts, weights, chunk, before, images, plan):
    pixels, cols = plan
    first, share = chunk
    count, mid, out = len(acts), acts[0].shape[1], weights[0].shape[1]
    ins = [info] + list(acts) + list(weights) + ([] if before is None else [before])
    return kernel_call(
        functools.partial(expand_kernel, first, plan, count, mid), "expand", ins,
        [((share, pixels, out), F32), sums_out(first + share == images, out)],
    )


def output_kernel(per_image, count, info_ref, *refs):
    expanded = [[v] for v in refs[:count]]
    in_ref, go_ref, sums_three_ref, par_ref, far_ref, grad_ref, sums_ref, out_ref, done_ref = refs[count:]
    average, inv_std = norm_of(sums_three_ref, pixel_count(info_ref, per_image))
    gain, bias = par_ref[0:1, :], par_ref[1:2, :]
    chans = out_ref.shape[2]

    def body(refs, at, image, sums):
        keep = (image < info_ref[OWN_COUNT]).astype(F32)
        normalized = (refs[0][at] - average) * inv_std
        summed = normalized * gain + bias + in_ref[image].astype(F32)
        logistic = sigmoid(summed)
        out_ref[image] = (summed * logistic * keep).astype(BF16)
        slope = logistic * (1.0 + summed * (1.0 - logistic))
        grad = go_ref[image].astype(F32) * (slope * keep)
        grad_ref[image] = grad
        pltpu.make_async_copy(out_ref.at[image], far_ref.at[image], done_ref.at[image]).start()
        return sums[0] + fold(grad), sums[1] + fold(grad * normalized)

    zero = jnp.zeros((8, chans), F32)
    put_sums(sums_ref, *each_image(expanded, body, (zero, zero)))
    for image in range(out_ref.shape[0]):
        pltpu.make_async_copy(out_ref.at[image], far_ref.at[image], done_ref.at[image]).wait()


def output_pass(info, expanded, field, grad_output, sums_three, params, per_image):
    return kernel_call(
        functools.partial(output_kernel, per_image, len(expanded)), "output",
        [info, *expanded, field, grad_output, sums_three, params],
        [(field.shape, BF16), (field.shape, F32), sums_out(True, field.shape[2])],
        [pltpu.VMEM(field.shape, BF16), pltpu.SemaphoreType.DMA((field.shape[0],))], far_outs=1,
    )


def at_image(refs, image):
    for ref in refs:
        if image < ref.shape[0]:
            return ref[image]
        image -= ref.shape[0]


def back_expand_kernel(first, plan, count, mid, fields, per_image, info_ref, *refs):
    pixels, cols = plan
    expanded, refs = refs[:fields], refs[fields:]
    grad_ref, sums_three_ref, grads_ref, par_ref = refs[:4]
    weights = refs[4 : 4 + count]
    out_ref, near_ref, far_ref = refs[-3:]
    total = pixel_count(info_ref, per_image)
    average, inv_std = norm_of(sums_three_ref, total)
    grads = jnp.sum(grads_ref[...], 0)
    scale = inv_std * par_ref[0:1, :]
    bias_part, gain_part = grads[0:1] / total, grads[1:2] / total * inv_std
    for i in range(out_ref.shape[0] // pixels):
        image = first + i
        value = grad_ref[image] - (bias_part + (at_image(expanded, image) - average) * gain_part)
        value = value * (scale * (image < info_ref[OWN_COUNT]).astype(F32))
        out_ref[i * pixels : (i + 1) * pixels, :] = value.astype(BF16)
    for k in range(count):
        term = dot(out_ref[...], weights[k][...], 1, 1)
        to = slice((k // 2) * mid, (k // 2 + 1) * mid)
        if k % 2 == 0:
            near_ref[:, to] = term
        else:
            far_ref[:, to] = term.astype(BF16)


def back_expand_chunk(info, grad_summed, expanded, sums_three, grads_three, params, weights, chunk, mid, plan, per_image):
    pixels, cols = plan
    count, out = len(weights), grad_summed.shape[2]
    block, half = chunk[1] * pixels, count // 2 * mid
    return kernel_call(
        functools.partial(back_expand_kernel, chunk[0], plan, count, mid, len(expanded), per_image), "back_expand",
        [info, *expanded, grad_summed, sums_three, grads_three, params, *weights],
        [((block, out), BF16), ((block, half), F32), ((block, half), BF16)],
        flops=2 * block * mid * count * out,
    )


def pair_sum_kernel(info_ref, near_ref, far_ref, own_ref, *send_refs):
    mid = own_ref.shape[1]
    for k, ref in enumerate((own_ref,) + send_refs):
        at = slice(k * mid, (k + 1) * mid)
        ref[...] = (near_ref[:, at] + far_ref[:, at].astype(F32)).astype(ref.dtype)


def pair_sum(info, near, far, mid):
    rows, half = near.shape
    return kernel_call(
        pair_sum_kernel, "pair_sum", [info, near, far],
        [((rows, mid), F32 if k == 0 else BF16) for k in range(half // mid)],
    )


def slope_two_kernel(first, plan, count, per_image, info_ref, own_ref, *refs):
    pixels, cols = plan
    arrived, refs = refs[:count], refs[count:]
    grp_ref, sums_two_ref, par_ref = refs[:3]
    before_ref = None if len(refs) == 6 else refs[3]
    out_ref, edge_ref, sums_ref = refs[-3:]
    average, inv_std = norm_of(sums_two_ref, pixel_count(info_ref, per_image))
    gain, bias = par_ref[2:3, :], par_ref[3:4, :]
    one, two = before_sums(before_ref, grp_ref.shape[2])
    for i in range(out_ref.shape[0]):
        image = first + i
        at = slice(i * pixels, (i + 1) * pixels)
        grad = own_ref[at, :]
        for ref in arrived:
            grad = grad + ref[at, :].astype(F32)
        normalized = (grp_ref[image] - average) * inv_std
        keep = (image < info_ref[OWN_COUNT]).astype(F32)
        grad = grad * (silu_slope(normalized * gain + bias) * keep)
        out_ref[i] = grad
        edge_ref[i] = edge_rows(info_ref, out_ref, i, cols).astype(BF16)
        one, two = one + fold(grad), two + fold(grad * normalized)
    put_sums(sums_ref, one, two)


def slope_two_chunk(info, own, arrived, grouped, sums_two, params, chunk, before, plan, per_image, staged):
    pixels, cols = plan
    first, share = chunk
    images, mid = grouped.shape[0], grouped.shape[2]
    ins = [info, own] + list(arrived) + [grouped, sums_two, params] + ([] if before is None else [before])
    return kernel_call(
        functools.partial(slope_two_kernel, first, plan, len(arrived), per_image), "slope_two", ins,
        [((share, pixels, mid), F32), ((share, cols, mid), BF16), sums_out(first + share == images and not staged, mid)],
    )


def conv_backward_kernel(
    per_image, group_images, d_count, red_count, info_ref, *refs
):
    d_fields, refs = list(zip(refs[:d_count], refs[d_count : 2 * d_count])), refs[2 * d_count :]
    reduced, refs = refs[:red_count], refs[red_count:]
    grp_ref, g_edge_ref, sums_two_ref, grads_two_ref, sums_one_ref, par_ref, mat_ref = refs[:7]
    out_ref, sums_ref, window_ref = refs[7:]
    images, pixels, chans = grp_ref.shape
    cols = g_edge_ref.shape[1]
    total_pixels = pixel_count(info_ref, per_image)
    avg_two, inv_two = norm_of(sums_two_ref, total_pixels)
    grads = jnp.sum(grads_two_ref[...], 0)
    bias_part, gain_part = grads[0:1] / total_pixels, grads[1:2] / total_pixels * inv_two
    scale_two = inv_two * par_ref[2:3, :]
    avg_one, inv_one = norm_of(sums_one_ref, total_pixels)
    gain_one, bias_one = par_ref[0:1, :], par_ref[1:2, :]

    def input_grad(d, grouped, keep):
        return (d - (bias_part + (grouped - avg_two) * gain_part)) * (scale_two * keep)

    def fill(image):
        keep = (image < info_ref[OWN_COUNT]).astype(F32)
        own = input_grad(at_image([f[0] for f in d_fields], image), grp_ref[image], keep)
        edge = at_image([f[1] for f in d_fields], image).astype(F32)
        edge = input_grad(edge, g_edge_ref[image].astype(F32), keep)
        fill_windows(window_ref, image, with_edges(info_ref, own, edge), cols)

    def convolve(first, one, two):
        grad = None
        for i in range(3):
            piece = window_ref[first : first + group_images, i * cols : i * cols + pixels, :]
            term = dot(piece.reshape(group_images * pixels, 3 * chans), mat_ref[i], 1, 0)
            grad = term if grad is None else grad + term
        for i in range(group_images):
            image = first + i
            keep = (image < info_ref[OWN_COUNT]).astype(F32)
            normalized = (at_image(reduced, image) - avg_one) * inv_one
            slope = silu_slope(normalized * gain_one + bias_one)
            d_one = grad[i * pixels : (i + 1) * pixels] * (slope * keep)
            out_ref[image] = d_one
            one, two = one + fold(d_one), two + fold(d_one * normalized)
        return one, two

    one = two = jnp.zeros((8, chans), F32)
    for first in range(0, images + group_images, group_images):
        for image in range(first, min(first + group_images, images)):
            fill(image)
        if first:
            one, two = convolve(first - group_images, one, two)
    put_sums(sums_ref, one, two)


def tap_grads_kernel(group, cols, step, info_ref, act_ref, window_ref, out_ref, turned_ref):
    images, pixels, chans = act_ref.shape
    for image in range(images):
        turned_ref[:, image * pixels : (image + 1) * pixels] = act_ref[image].T
    same = (
        lax.broadcasted_iota(jnp.int32, (chans, 3 * chans), 0) // group
        == lax.broadcasted_iota(jnp.int32, (chans, 3 * chans), 1) % chans // group
    )
    for i in range(3):
        total = None
        for first in range(0, images, step):
            piece = window_ref[first : first + step, i * cols : i * cols + pixels, :]
            turned = turned_ref[:, first * pixels : (first + step) * pixels]
            term = dot(turned, piece.reshape(step * pixels, 3 * chans), 1, 0)
            total = term if total is None else total + term
        total = jnp.sum(jnp.where(same, total, 0.0).reshape(chans // group, group, 3 * chans), 0)
        for j in range(3):
            out_ref[3 * (2 - i) + 2 - j] = total[:, j * chans : (j + 1) * chans]


def tap_grads(info, acts, windows, group, cols):
    images, pixels, chans = acts.shape
    return kernel_call(
        functools.partial(tap_grads_kernel, group, cols, 4), "tap_grads", [info, acts, windows], [((9, group, chans), F32)],
        [pltpu.VMEM((chans, images * pixels), BF16)],
    )[0]


def conv_backward(info, d_two, d_edges, grouped, g_edge, reduced, sums_two, grads_two, sums_one, params, matrices, per_image):
    images, pixels, chans = grouped.shape
    cols = g_edge.shape[1]
    return kernel_call(
        functools.partial(conv_backward_kernel, per_image, 4, len(d_two), len(reduced)), "conv_backward",
        [info, *d_two, *d_edges, *reduced, grouped, g_edge, sums_two, grads_two, sums_one, params, matrices],
        [(grouped.shape, F32), sums_out(True, chans), ((images, pixels + 2 * cols, 3 * chans), BF16)],
    )


def grad_reduced_kernel(per_image, count, info_ref, *refs):
    reduced = [[v] for v in refs[:count]]
    d_ref, sums_one_ref, grads_ref, par_ref, out_ref = refs[count:]
    pixels = d_ref.shape[1]
    total = pixel_count(info_ref, per_image)
    average, inv_std = norm_of(sums_one_ref, total)
    grads = jnp.sum(grads_ref[...], 0)
    bias_part, gain_part = grads[0:1] / total, grads[1:2] / total * inv_std
    scale = inv_std * par_ref[0:1, :]

    def body(refs, at, image, nothing):
        value = d_ref[image] - (bias_part + (refs[0][at] - average) * gain_part)
        value = value * (scale * (image < info_ref[OWN_COUNT]).astype(F32))
        out_ref[pl.ds(pl.multiple_of(image * pixels, pixels), pixels), :] = value.astype(BF16)
        return nothing

    each_image(reduced, body, 0)


def grad_reduced(info, d_one, reduced, sums_one, grads_one, params, per_image):
    images, pixels, mid = d_one.shape
    return kernel_call(
        functools.partial(grad_reduced_kernel, per_image, len(reduced)), "grad_reduced",
        [info, *reduced, d_one, sums_one, grads_one, params], [((images * pixels, mid), BF16)],
    )[0]


def input_grad_kernel(count, info_ref, grad_ref, *refs):
    pieces, weights, out_ref = refs[:count], refs[count : 2 * count], refs[-1]
    rows = 512

    def body(step, nothing):
        at = pl.ds(pl.multiple_of(step * rows, rows), rows)
        total = grad_ref[at, :]
        for p_ref, w_ref in zip(pieces, weights):
            total = total + dot(p_ref[at, :], w_ref[...], 1, 1)
        out_ref[at, :] = total.astype(BF16)
        return nothing

    lax.fori_loop(0, grad_ref.shape[0] // rows, body, 0)


def input_grad(info, grad_summed, pieces, weights):
    return kernel_call(
        functools.partial(input_grad_kernel, len(pieces)), "input_grad", [info, grad_summed] + list(pieces) + list(weights),
        [(grad_summed.shape, BF16)],
    )[0]


def cut_columns_kernel(info_ref, in_ref, *refs):
    for k, ref in enumerate(refs):
        part = ref.shape[1]
        ref[...] = in_ref[:, pl.ds(pl.multiple_of((info_ref[CHAN_AT] ^ k) * part, part), part)]


def cut_columns(info, value, count):
    rows, part = value.shape[0], value.shape[1] // count
    return kernel_call(cut_columns_kernel, "cut_columns", [info, value], [((rows, part), BF16)] * count)


def cut_rows_kernel(info_ref, in_ref, *refs):
    for k, ref in enumerate(refs):
        part = ref.shape[0]
        ref[...] = in_ref[pl.ds(pl.multiple_of((info_ref[CHAN_AT] ^ k) * part, part), part), :]


def cut_rows(info, value, count):
    part, cols = value.shape[0] // count, value.shape[1]
    return kernel_call(cut_rows_kernel, "cut_rows", [info, value], [((part, cols), BF16)] * count)


def sum_vectors_kernel(*refs):
    half = len(refs) // 3
    for ref, out_one, out_two in zip(refs[:half], refs[half::2], refs[half + 1 :: 2]):
        sums = jnp.sum(ref[...], 0)
        out_one[...] = sums[0:1]
        out_two[...] = sums[1:2]


def sum_vectors(values):
    outs = [((1, v.shape[2]), F32) for v in values for _ in range(2)]
    return [v.reshape(-1) for v in kernel_call(sum_vectors_kernel, "sum_vectors", list(values), outs)]


REDUCE_STEPS = (("height", 1, HEIGHT_AT), ("batch", 1, NEAR_AT), ("batch", 2, FAR_AT))
EXPAND_STEPS = (("height", 1, HEIGHT_AT), ("batch", 1, NEAR_AT), ("batch", 2, FAR_AT))


def part_of(info_ref, steps):
    number = 0
    for _, _, field in steps:
        number = number * 2 + info_ref[field]
    return number


def send_half(pair, step):
    return pair[0], permute(pair[1], step[0], step[1])


def split(at, keep_ref, send_ref, all_ref, arrived_ref):
    half = keep_ref.shape[0]
    for to, ref in ((at, keep_ref), (1 - at, send_ref)):
        value = all_ref[pl.ds(to * half, half)]
        if arrived_ref is not None:
            value = value + arrived_ref[pl.ds(to * half, half)].astype(F32)
        ref[...] = value.astype(ref.dtype)


def split_first_kernel(make, field, info_ref, *refs):
    keep_ref, send_ref, all_ref = refs[-3:]
    make(refs[:-3], all_ref)
    split(info_ref[field], keep_ref, send_ref, all_ref, None)


def split_first(info, make, step, name, ins, shape):
    half = (shape[0] // 2,) + shape[1:]
    return kernel_call(
        functools.partial(split_first_kernel, make, step[2]), name, [info] + ins, [(half, F32), (half, BF16)],
        [pltpu.VMEM(shape, F32)],
    )


def split_next_kernel(field, info_ref, keep_ref, arrived_ref, out_ref, send_ref):
    split(info_ref[field], out_ref, send_ref, keep_ref, arrived_ref)


def split_next(info, pair, step):
    half = (pair[0].shape[0] // 2,) + pair[0].shape[1:]
    return kernel_call(
        functools.partial(split_next_kernel, step[2]), "split_next", [info, *pair], [(half, F32), (half, BF16)], flops=SPLIT_COST
    )


def add_kernel(info_ref, first_ref, second_ref, out_ref):
    out_ref[...] = (first_ref[...] + second_ref[...].astype(F32)).astype(BF16)


def add_last(info, pair):
    return kernel_call(add_kernel, "add_last", [info, *pair], [(pair[0].shape, BF16)], flops=ADD_COST)[0]


def join_kernel(info_ref, *refs):
    size = refs[0].shape[0]
    for k, ref in enumerate(refs[:-1]):
        refs[-1][k * size : (k + 1) * size] = ref[...]


def join(info, *values):
    shape = (values[0].shape[0] * len(values),) + values[0].shape[1:]
    return kernel_call(join_kernel, "join", [info, *values], [(shape, BF16)], flops=STAGE_COST)[0]


def send_back(value, step):
    return value, permute(value, step[0], step[1])


def reduce_grad_make(places, spans, extra, refs, all_ref):
    grad_ref = refs[places * len(spans)]
    parts = all_ref.shape[0]
    per = parts // places
    for k in range(places):
        total = None
        for c, (first, end) in enumerate(spans):
            term = dot(refs[k * len(spans) + c][...], grad_ref[first:end, :], 0, 0)
            total = term if total is None else total + term
        size = total.shape[0] // per
        all_ref[k * per : (k + 1) * per, 0:size, :] = total.reshape(per, size, total.shape[1])
    if extra:
        more = refs[-1][...]
        more = more.reshape(-1, more.shape[2])
        room = parts * extra - more.shape[0]
        more = jnp.concatenate([more, jnp.zeros((room, more.shape[1]), F32)], 0)
        all_ref[:, size : size + extra, :] = more.reshape(parts, extra, more.shape[1])


def reduce_grad(info, inputs, grad, parts, more):
    spans = spans_of(inputs[0])
    rows, mid = len(inputs) * inputs[0][0].shape[1], grad.shape[1]
    extra = 0 if more is None else -(-more.shape[0] * more.shape[1] // (8 * parts)) * 8
    ins = [v for piece in inputs for v in piece] + [grad] + ([] if more is None else [more])
    return split_first(
        info, functools.partial(reduce_grad_make, len(inputs), tuple(spans), extra), REDUCE_STEPS[0], "reduce_grad", ins,
        (parts, rows // parts + extra, mid),
    )


def spans_of(values):
    spans, at = [], 0
    for value in values:
        spans.append((at, at + value.shape[0]))
        at += value.shape[0]
    return spans


def expand_grad_make(count, chunks, refs, all_ref):
    acts, grads = refs[: count * chunks], refs[count * chunks :]
    parts, wide, out = all_ref.shape
    size = wide // count
    for k in range(count):
        total = None
        own = acts[k * chunks : (k + 1) * chunks]
        for a_ref, (a_first, a_end) in zip(own, spans_of(own)):
            for g_ref, (g_first, g_end) in zip(grads, spans_of(grads)):
                first, end = max(a_first, g_first), min(a_end, g_end)
                if first < end:
                    term = dot(a_ref[first - a_first : end - a_first, :], g_ref[first - g_first : end - g_first, :], 0, 0)
                    total = term if total is None else total + term
        all_ref[:, k * size : (k + 1) * size, :] = total.reshape(parts, size, out)


def expand_grad(info, acts, grads, parts):
    count, mid, out = len(acts), acts[0][0].shape[1], grads[0].shape[1]
    return split_first(
        info, functools.partial(expand_grad_make, count, len(acts[0])), EXPAND_STEPS[0], "expand_grad",
        [a for piece in acts for a in piece] + list(grads), (parts, count * mid // parts, out),
    )


def cut_places_kernel(info_ref, keep_ref, arrived_ref, *refs):
    size = refs[0].shape[0]
    total = (keep_ref[0] + arrived_ref[0].astype(F32)).astype(BF16)
    for k, ref in enumerate(refs):
        ref[...] = total[k * size : (k + 1) * size, :]


def cut_places(info, pair, count):
    rows, out = pair[0].shape[1:]
    return kernel_call(cut_places_kernel, "cut_places", [info, *pair], [((rows // count, out), BF16)] * count)


def place_reduce_kernel(count, info_ref, *refs):
    out_ref, group_ref, more_ref = refs[4:]
    me, number = info_ref[CHAN_AT], part_of(info_ref, REDUCE_STEPS)
    part = out_ref.shape[0] // count
    batches = refs[0].shape[0]
    size = refs[0].shape[1]
    extra = refs[2].shape[1] - size
    for half in range(2):
        for other in range(2):
            ref = refs[2 * half + other]
            for k in range(batches):
                at = number ^ (other * batches + k)
                row = at * size
                to = (me ^ (half * (count // 2) + row // part)) * part + row % part
                out_ref[pl.ds(pl.multiple_of(to, size), size), :] = ref[k, 0:size, :].astype(F32)
                if half == 1:
                    more_ref[pl.ds(pl.multiple_of(at * extra, 8), extra), :] = ref[k, size:, :].astype(F32)
    group_ref[...] = more_ref[0 : group_ref.shape[0], :]


def place_reduce(info, halves, count, part, group_rows):
    batches, rows, mid = halves[1][0].shape
    extra = rows - halves[0][0].shape[1]
    return kernel_call(
        functools.partial(place_reduce_kernel, count), "place_reduce", [info] + [v for pair in halves for v in pair],
        [((part * count, mid), F32), ((group_rows, mid), F32)], [pltpu.VMEM((2 * batches * extra, mid), F32)],
    )


def place_expand_kernel(count, info_ref, own_ref, arrived_ref, out_ref):
    me, number = info_ref[CHAN_AT], part_of(info_ref, EXPAND_STEPS)
    batches, rows, out = own_ref.shape
    size = rows // count
    for other, ref in enumerate((own_ref, arrived_ref)):
        for k in range(batches):
            row = (number ^ (other * batches + k)) * size
            for place in range(count):
                to = pl.ds(pl.multiple_of((me ^ place) * out, out), out)
                out_ref[pl.ds(pl.multiple_of(row, size), size), to] = ref[k, place * size : (place + 1) * size, :].astype(F32)


def place_expand(info, pair, count, mid):
    out = pair[0].shape[2]
    return kernel_call(
        functools.partial(place_expand_kernel, count), "place_expand", [info] + list(pair), [((mid, out * count), F32)]
    )[0]


def plain_weight_grads(inputs, grad, acts, grad_expanded, grad_group):
    count, me = len(inputs), lax.axis_index("chan")
    part, mid = inputs[0][0].shape[1], grad.shape[1]
    grad_reduce = jnp.zeros((part * count, mid), BF16)
    grad_expand = jnp.zeros((mid, part * count), BF16)
    for k in range(count):
        block = dot(jnp.concatenate(inputs[k], 0), grad, 0, 0).astype(BF16)
        grad_reduce = lax.dynamic_update_slice(grad_reduce, block, ((me ^ k) * part, 0))
        block = dot(jnp.concatenate(acts[k], 0), jnp.concatenate(grad_expanded, 0), 0, 0).astype(BF16)
        block = swap(block, k) if k else block
        grad_expand = lax.dynamic_update_slice(grad_expand, block, (0, (me ^ k) * part))
    return [lax.psum(v, REDUCE_AXES).astype(F32) for v in (grad_reduce, grad_expand, grad_group.astype(BF16))]


def shards(
    block_input, w_reduce, w_group, w_expand, gain_one, bias_one, gain_two, bias_two,
    gain_three, bias_three, image_counts, grad_output,
):
    chan_size = lax.axis_size("chan")
    me = lax.axis_index("chan")
    height_at = lax.axis_index("height")
    images, rows, cols, out_part = block_input.shape
    mid_part, group = w_group.shape[3], w_group.shape[2]
    pixels = rows * cols
    per_image = float(pixels * lax.axis_size("height"))
    plan = (pixels, cols)
    distances = range(2, chan_size, 2)
    own_count = jnp.sum(
        jnp.where(jnp.arange(image_counts.shape[0]) == lax.axis_index("batch"), image_counts, 0)
    )
    batch_at = lax.axis_index("batch")
    info = jnp.stack(
        [
            own_count, jnp.sum(image_counts), height_at, me, jnp.where(height_at == 0, pixels - cols, 0),
            batch_at & 1, (batch_at >> 1) & 1,
        ]
    ).astype(jnp.int32)
    parts = lax.axis_size(REDUCE_AXES)
    staged = (lax.axis_size("height"), lax.axis_size("batch")) == (2, 4)

    def edge_swap(edge):
        return permute(edge, "height", 1)

    def sums_of(sums, *waits):
        return staged_sums(sums, *waits) if staged else spread_sums(sums)

    def gather(value, *waits):
        pieces = [value, swap(value, 1)]
        for k in distances:
            pieces.append(swap(value, k))
            pieces.append(swap(after(pieces[k], *waits) if waits else pieces[k], 1))
        return pieces

    field = block_input.reshape(images * pixels, out_part)
    matrices, matrices_back, mid_params, out_params = prepare(
        info, w_group, (gain_one, bias_one, gain_two, bias_two), (gain_three, bias_three)
    )
    columns = cut_columns(info, w_expand, chan_size)
    rows_back = cut_rows(info, w_reduce, chan_size)
    weights = [columns[0], swap(columns[1], 1)]
    reduce_back = [rows_back[0], swap(rows_back[1], 1)]
    inputs = []
    for first, share in cut_images(REDUCE_CHUNKS):
        source = after(field, inputs[0][0], info) if first else field
        piece = lax.slice_in_dim(source, first * pixels, (first + share) * pixels)
        inputs.append(gather(piece, mid_params, weights[1], reduce_back[1]) if first else gather(piece))
    reduced, red_edges, sums = [], [], None
    for pieces, (first, share) in zip(inputs, cut_images(REDUCE_CHUNKS)):
        red, edge, sums = reduce_chunk(info, pieces, (first, share), w_reduce, sums, images, plan, False)
        reduced.append(red)
        red_edges.append(edge_swap(edge))
    inputs = [list(chunks) for chunks in zip(*inputs)]
    weights += [swap(after(columns[k], inputs[2][-1]), k) for k in range(2, chan_size)]
    late_back = [swap(after(rows_back[k], inputs[2][-1]), k) for k in range(3, chan_size)]
    sums_one = spread_sums(sums)

    acts_one, grouped, grp_edge, sums = conv_forward(
        info, reduced, red_edges, sums_one, mid_params, matrices, per_image
    )
    sums_two = spread_sums(after(sums, *weights[2:], *late_back))

    acts = []
    for chunk in cut_images(EXPAND_CHUNKS):
        acts.append(gather(act_two_chunk(info, grouped, sums_two, mid_params, chunk, plan, per_image)))
    expanded, sums = [], None
    for pieces, chunk in zip(acts, cut_images(EXPAND_CHUNKS)):
        out, sums = expand_chunk(info, pieces, weights, chunk, sums, images, plan)
        expanded.append(out)
    acts = [list(chunks) for chunks in zip(*acts)]
    sums_three = spread_sums(sums)
    output, grad_summed, sums = output_pass(
        info, expanded, field.reshape(images, pixels, out_part), grad_output.reshape(images, pixels, out_part), sums_three,
        out_params, per_image,
    )
    grads_three = spread_sums(sums)

    grad_expanded, halves = [], []
    for chunk in cut_images(BACK_CHUNKS):
        grad, near, far = back_expand_chunk(
            info, grad_summed, expanded, sums_three, grads_three, out_params, weights, chunk, mid_part, plan, per_image
        )
        grad_expanded.append(grad)
        halves.append((near, swap(far, 1)))
    own, sent = [], []
    for near, far in halves:
        summed = pair_sum(info, near, far, mid_part)
        own.append(summed[0])
        sent.append([swap(value, k) for value, k in zip(summed[1:], distances)])
    grp_edge = edge_swap(after(grp_edge, own[0]))
    if staged:
        expand_pair = send_half(expand_grad(info, acts, grad_expanded, parts), EXPAND_STEPS[0])
    d_two, d_edges, sums, turn = [], [], None, info
    for c, chunk in enumerate(cut_images(BACK_CHUNKS)):
        if staged and c == 1:
            pair = split_next(after(info, d_two[0]), expand_pair, EXPAND_STEPS[1])
            turn = after(info, pair[0])
            expand_pair = send_half(pair, EXPAND_STEPS[1])
        grad, edge, sums = slope_two_chunk(
            turn, own[c], sent[c], grouped, sums_two, mid_params, chunk, sums, plan, per_image, staged
        )
        d_two.append(grad)
        d_edges.append(edge_swap(edge))
    if staged:
        sums = after(sums, expand_pair[1], grp_edge, d_edges[0])
    grads_two = sums_of(sums, d_edges[-1])
    turn = info
    if staged:
        pair = split_next(after(info, grads_two), expand_pair, EXPAND_STEPS[2])
        turn = after(info, pair[0])
        expand_pair = send_half(pair, EXPAND_STEPS[2])

    d_one, sums, windows = conv_backward(
        turn, d_two, d_edges, grouped, grp_edge, reduced, sums_two, grads_two, sums_one, mid_params, matrices_back, per_image
    )
    if staged:
        reduce_back.append(swap(after(rows_back[2], grads_two), 2))
    grads_one = spread_sums(sums)

    grad = grad_reduced(info, d_one, reduced, sums_one, grads_one, mid_params, per_image)
    grad_field = grad_summed.reshape(images * pixels, out_part)
    if staged:
        half = chan_size // 2
        pairs, turn = [], after(info, grad)

        def in_turn(call, *args):
            nonlocal turn
            result = call(turn, *args)
            turn = after(info, result[0] if isinstance(result, (list, tuple)) else result)
            return result

        def first_half(i):
            own = inputs[i * half : (i + 1) * half]
            pairs.append(send_half(in_turn(reduce_grad, own, grad, parts, taps if i else None), REDUCE_STEPS[0]))

        def next_half(i, step):
            pairs[i] = send_half(in_turn(split_next, pairs[i], REDUCE_STEPS[step]), REDUCE_STEPS[step])

        def last_half(i):
            pairs[i] = send_back(in_turn(add_last, pairs[i]), REDUCE_STEPS[2])

        def back_half(i, step):
            pairs[i] = send_back(in_turn(join, *pairs[i]), REDUCE_STEPS[step])

        reduce_back += late_back
        for word in LAST_PHASE:
            kind, place = word[0], word[1:]
            if kind in "ab":
                i = "ab".index(kind)
                if place == "0":
                    first_half(i)
                elif place in ("1", "2"):
                    next_half(i, int(place))
                elif place == "3":
                    last_half(i)
                else:
                    back_half(i, 5 - int(place))
            elif word == "t":
                taps = in_turn(tap_grads, acts_one, windows, group, cols)
            elif word == "c":
                places = in_turn(cut_places, expand_pair, chan_size)
                places = [v if k == 0 else swap(v, k) for k, v in enumerate(places)]
            elif word == "e0":
                back = in_turn(join, *places)
                back = send_back(back.reshape((1,) + back.shape), EXPAND_STEPS[2])
            elif kind == "e":
                back = send_back(in_turn(join, *back), EXPAND_STEPS[2 - int(place)])
            elif word == "x":
                far_grads = [swap(after(grad, turn), k) for k in distances]
            elif word == "o":
                grads = [grad, swap(after(grad, turn), 1)]
            elif word == "d":
                for value in far_grads:
                    grads += [value, swap(after(value, turn), 1)]
            elif word == "p":
                grad_expand = in_turn(place_expand, back, chan_size, mid_part)
            elif word == "i":
                grad_input = in_turn(input_grad, grad_field, grads, reduce_back)
            elif word == "wo":
                turn = after(turn, grads[1])
            elif word == "wd":
                turn = after(turn, *grads[2:])
            elif word == "wz":
                turn = after(turn, expand_pair[1])
            elif word == "wr":
                turn = after(turn, *reduce_back[2:])
            elif word == "wa":
                turn = after(turn, pairs[0][1])
            elif word == "wb":
                turn = after(turn, pairs[1][1])
            elif word == "we":
                turn = after(turn, back[1])
        grad_reduce, grad_group = place_reduce(turn, pairs, chan_size, out_part, 9 * group)
    else:
        reduce_back += [swap(rows_back[2], 2)] + late_back
        grad_input = input_grad(info, grad_field, gather(grad), reduce_back)
        grad_group = tap_grads(info, acts_one, windows, group, cols)
        grad_reduce, grad_expand, grad_group = plain_weight_grads(inputs, grad, acts, grad_expanded, grad_group)
    vectors = sum_vectors([grads_one, grads_two, grads_three])
    return (
        output.reshape(block_input.shape), grad_input.reshape(block_input.shape), grad_reduce,
        grad_group.reshape(w_group.shape), grad_expand,
        vectors[1], vectors[0], vectors[3], vectors[2], vectors[5], vectors[4],
    )


def solution(mesh):
    split = P("batch", "height", None, "chan")
    vector = P("chan")
    return jax.shard_map(
        shards,
        mesh=mesh,
        in_specs=(
            split, P(None, "chan"), P(None, None, None, "chan"), P("chan", None),
            vector, vector, vector, vector, vector, vector, P(), split,
        ),
        out_specs=(
            split, split, P(None, "chan"), P(None, None, None, "chan"), P("chan", None),
            vector, vector, vector, vector, vector, vector,
        ),
        check_vma=False,
    )
```

```python
import functools

import jax
import jax.numpy as jnp
from jax import lax
from jax.experimental import pallas as pl
from jax.experimental.pallas import tpu as pltpu
from jax.sharding import PartitionSpec as P

EPSILON = 1e-05
SPLIT_COST, ADD_COST, STAGE_COST = 1_800_000_000, 3_000_000_000, 2_200_000_000
LAST_PHASE = (
    "wz", "wr", "a0", "t", "b0", "c", "a1", "b1", "e0", "a2", "x", "b2", "e1", "o", "a3", "e2", "b3", "a4",
    "d", "b4", "we", "a5", "wa", "b5", "i", "p",
)
F32, BF16 = jnp.float32, jnp.bfloat16
REDUCE_AXES = ("height", "batch")
REDUCE_CHUNKS, EXPAND_CHUNKS, BACK_CHUNKS = (8, 8), (8, 8), (8, 8)
OWN_COUNT, TOTAL_COUNT, HEIGHT_AT, CHAN_AT, EDGE_ROW, NEAR_AT, FAR_AT = range(7)
VMEM = pl.BlockSpec(memory_space=pltpu.VMEM)
SMEM = pl.BlockSpec(memory_space=pltpu.SMEM)
FAR = pl.BlockSpec(memory_space=pl.ANY)


def dot(a, b, left, right):
    return lax.dot_general(a, b, (((left,), (right,)), ((), ())), preferred_element_type=F32)


def kernel_call(body, name, ins, outs, scratch=(), alias=None, flops=0, room=16, far_outs=0):
    return pl.pallas_call(
        body,
        in_specs=[SMEM if a.dtype == jnp.int32 else VMEM for a in ins],
        out_specs=[FAR] * far_outs + [VMEM] * (len(outs) - far_outs),
        out_shape=[jax.ShapeDtypeStruct(shape, dtype) for shape, dtype in outs],
        scratch_shapes=list(scratch),
        input_output_aliases=alias or {},
        compiler_params=pltpu.CompilerParams(vmem_limit_bytes=room << 20),
        cost_estimate=pl.CostEstimate(flops=flops, bytes_accessed=0, transcendentals=0),
        name=name,
    )(*ins)


def after(value, *others):
    return lax.optimization_barrier((value,) + others)[0]


def permute(value, axis, distance):
    count = lax.axis_size(axis)
    return lax.ppermute(value, axis, [(i, i ^ distance) for i in range(count)])


def swap(value, distance):
    return permute(value, "chan", distance)


def spread_sums(sent):
    return lax.all_to_all(sent, REDUCE_AXES, 0, 0)


def staged_sums(partial, *waits):
    chans = partial.shape[2]
    both = kernel_call(
        add_rows_kernel, "add_rows", [after(partial, *waits), permute(partial, "height", 1)], [((2, chans), F32)]
    )[0]
    others = [permute(both, "batch", k) for k in range(1, lax.axis_size("batch"))]
    return kernel_call(add_sums_kernel, "add_sums", [both] + others, [((1, 2, chans), F32)])[0]


def add_rows_kernel(own_ref, other_ref, out_ref):
    out_ref[...] = jnp.sum(own_ref[...] + other_ref[...], 1)


def add_sums_kernel(*refs):
    total = refs[0][...]
    for ref in refs[1:-1]:
        total = total + ref[...]
    refs[-1][0] = total


def norm_of(sums_ref, total):
    sums = jnp.sum(sums_ref[...], 0)
    average = sums[0:1] / total
    return average, lax.rsqrt(sums[1:2] / total - average * average + EPSILON)


def pixel_count(info_ref, per_image):
    return info_ref[TOTAL_COUNT].astype(F32) * per_image


def sigmoid(v):
    return 0.5 * jnp.tanh(0.5 * v) + 0.5


def silu_slope(v):
    logistic = sigmoid(v)
    return logistic * (1.0 + v * (1.0 - logistic))


def fold(values):
    rows, chans = values.shape
    return jnp.sum(values.reshape(rows // 8, 8, chans), 0)


def put_sums(out_ref, one, two):
    if out_ref.shape[1] == 8:
        out_ref[0] = one
        out_ref[1] = two
    else:
        both = jnp.concatenate([jnp.sum(one, 0, keepdims=True), jnp.sum(two, 0, keepdims=True)], 0)
        out_ref[...] = jnp.broadcast_to(both[None], out_ref.shape)


def sums_out(last, chans):
    return ((lax.axis_size(REDUCE_AXES), 2, chans) if last else (2, 8, chans), F32)


def before_sums(before_ref, chans):
    if before_ref is None:
        zero = jnp.zeros((8, chans), F32)
        return zero, zero
    return before_ref[0], before_ref[1]


def edge_rows(info_ref, ref, image, cols):
    return ref[image, pl.ds(pl.multiple_of(info_ref[EDGE_ROW], 16), cols), :]


def prepare_kernel(group, info_ref, taps_ref, mid_a, mid_b, mid_c, mid_d, out_a, out_b, fwd_ref, back_ref, mid_ref, out_ref):
    chans = taps_ref.shape[2]
    same = (
        lax.broadcasted_iota(jnp.int32, (chans, chans), 0) // group
        == lax.broadcasted_iota(jnp.int32, (chans, chans), 1) // group
    )
    for i in range(3):
        for j in range(3):
            wide = jnp.concatenate([taps_ref[3 * i + j].astype(F32)] * (chans // group), 0)
            wide = jnp.where(same, wide, 0.0)
            fwd_ref[i, j * chans : (j + 1) * chans, :] = wide.astype(BF16)
            back_ref[2 - i, (2 - j) * chans : (3 - j) * chans, :] = wide.T.astype(BF16)
    for row, ref in enumerate((mid_a, mid_b, mid_c, mid_d)):
        mid_ref[row : row + 1, :] = ref[...].astype(F32)
    for row, ref in enumerate((out_a, out_b)):
        out_ref[row : row + 1, :] = ref[...].astype(F32)


def prepare(info, kernel, mid_vectors, out_vectors):
    group, chans = kernel.shape[2], kernel.shape[3]
    wide = (3, 3 * chans, chans)
    rows = [v.reshape(1, -1) for v in list(mid_vectors) + list(out_vectors)]
    return kernel_call(
        functools.partial(prepare_kernel, group), "prepare", [info, kernel.reshape(9, group, chans)] + rows,
        [(wide, BF16), (wide, BF16), ((4, chans), F32), ((2, rows[-1].shape[1]), F32)],
    )


def cut_images(shares):
    return [(sum(shares[:i]), share) for i, share in enumerate(shares)]


def reduce_kernel(first, plan, count, info_ref, *refs):
    pixels, cols = plan
    pieces, w_ref, before_ref = refs[:count], refs[count], None if len(refs) == count + 4 else refs[count + 1]
    red_ref, edge_ref, sums_ref = refs[-3:]
    me = info_ref[CHAN_AT]
    part, images = pieces[0].shape[1], red_ref.shape[0]
    one, two = before_sums(before_ref, w_ref.shape[1])
    step = min(4, images)
    for start in range(0, images, step):
        total = None
        for k in range(count):
            rows = w_ref[pl.ds(pl.multiple_of((me ^ k) * part, part), part), :]
            term = dot(pieces[k][start * pixels : (start + step) * pixels, :], rows, 1, 0)
            total = term if total is None else total + term
        for i in range(start, start + step):
            value = total[(i - start) * pixels : (i - start + 1) * pixels]
            red_ref[i] = value
            edge_ref[i] = edge_rows(info_ref, red_ref, i, cols).astype(BF16)
            value = value * (first + i < info_ref[OWN_COUNT]).astype(F32)
            one, two = one + fold(value), two + fold(value * value)
    put_sums(sums_ref, one, two)


def reduce_chunk(info, pieces, chunk, w_reduce, before, images, plan, staged):
    pixels, cols = plan
    first, share = chunk
    count, mid = len(pieces), w_reduce.shape[1]
    ins = [info] + list(pieces) + [w_reduce] + ([] if before is None else [before])
    return kernel_call(
        functools.partial(reduce_kernel, first, plan, count), "reduce", ins,
        [((share, pixels, mid), F32), ((share, cols, mid), BF16), sums_out(first + share == images and not staged, mid)],
        flops=2 * pieces[0].size * count * mid,
    )


def each_image(chunks, body, carry, step=1):
    first = 0
    for refs in chunks:
        count = refs[0].shape[0]
        start = first
        carry = lax.fori_loop(
            0, count // step, lambda i, c, refs=refs, start=start: body(refs, i * step, start + i * step, c), carry
        )
        first += count
    return carry


def fill_windows(window_ref, slot, value, cols):
    rows, chans = value.shape
    place = lax.broadcasted_iota(jnp.int32, value.shape, 0) % cols
    left = jnp.where(place == 0, 0.0, pltpu.roll(value, 1, 0))
    right = jnp.where(place == cols - 1, 0.0, pltpu.roll(value, rows - 1, 0))
    window_ref[slot, :, 0:chans] = left.astype(BF16)
    window_ref[slot, :, chans : 2 * chans] = value.astype(BF16)
    window_ref[slot, :, 2 * chans : 3 * chans] = right.astype(BF16)


def with_edges(info_ref, own, edge):
    low = (info_ref[HEIGHT_AT] > 0).astype(F32)
    return jnp.concatenate([edge * low, own, edge * (1.0 - low)], 0)


def conv_forward_kernel(
    per_image, group_images, count, info_ref, *refs
):
    fields = list(zip(refs[:count], refs[count : 2 * count]))
    sums_one_ref, par_ref, mat_ref, act_ref, out_ref, out_edge_ref, sums_ref, window_ref = refs[2 * count :]
    images, pixels, chans = act_ref.shape
    cols = out_edge_ref.shape[1]
    average, inv_std = norm_of(sums_one_ref, pixel_count(info_ref, per_image))
    scale, bias = inv_std * par_ref[0:1, :], par_ref[1:2, :]

    def activate(v, keep):
        pre = (v - average) * scale + bias
        return pre * sigmoid(pre) * keep

    def fill(image):
        keep = (image < info_ref[OWN_COUNT]).astype(F32)
        own = activate(at_image([f[0] for f in fields], image), keep)
        edge = activate(at_image([f[1] for f in fields], image).astype(F32), keep)
        act_ref[image] = own.astype(BF16)
        fill_windows(window_ref, image, with_edges(info_ref, own, edge), cols)

    def convolve(first):
        total = None
        for i in range(3):
            piece = window_ref[first : first + group_images, i * cols : i * cols + pixels, :]
            term = dot(piece.reshape(group_images * pixels, 3 * chans), mat_ref[i], 1, 0)
            total = term if total is None else total + term
        out_ref[first : first + group_images] = total.reshape(group_images, pixels, chans)
        return fold(total), fold(total * total)

    one = two = jnp.zeros((8, chans), F32)
    for first in range(0, images + group_images, group_images):
        for image in range(first, min(first + group_images, images)):
            fill(image)
        if first:
            more = convolve(first - group_images)
            one, two = one + more[0], two + more[1]
    for image in range(images):
        out_edge_ref[image] = edge_rows(info_ref, out_ref, image, cols).astype(BF16)
    put_sums(sums_ref, one, two)


def conv_forward(info, reduced, edges, sums_one, params, matrices, per_image):
    images = sum(v.shape[0] for v in reduced)
    pixels, chans = reduced[0].shape[1:]
    cols = edges[0].shape[1]
    shape = (images, pixels, chans)
    return kernel_call(
        functools.partial(conv_forward_kernel, per_image, 4, len(reduced)), "conv_forward",
        [info, *reduced, *edges, sums_one, params, matrices],
        [(shape, BF16), (shape, F32), ((images, cols, chans), BF16), sums_out(True, chans)],
        [pltpu.VMEM((images, pixels + 2 * cols, 3 * chans), BF16)],
    )


def act_two_kernel(chunk, plan, per_image, info_ref, grp_ref, sums_ref, par_ref, out_ref):
    pixels, cols = plan
    first, images = chunk
    average, inv_std = norm_of(sums_ref, pixel_count(info_ref, per_image))
    scale, bias = inv_std * par_ref[2:3, :], par_ref[3:4, :]
    for i in range(images):
        image = first + i
        pre = (grp_ref[image] - average) * scale + bias
        act = pre * sigmoid(pre) * (image < info_ref[OWN_COUNT]).astype(F32)
        out_ref[i * pixels : (i + 1) * pixels] = act.astype(BF16)


def act_two_chunk(info, grouped, sums_two, params, chunk, plan, per_image):
    pixels, cols = plan
    shape = (chunk[1] * pixels, grouped.shape[2])
    return kernel_call(
        functools.partial(act_two_kernel, chunk, plan, per_image), "act_two",
        [info, grouped, sums_two, params], [(shape, BF16)],
    )[0]


def expand_kernel(first, plan, count, mid, info_ref, *refs):
    pixels, cols = plan
    acts, weights = refs[:count], refs[count : 2 * count]
    before_ref = None if len(refs) == 2 * count + 2 else refs[2 * count]
    out_ref, sums_ref = refs[-2:]
    images = out_ref.shape[0]
    one, two = before_sums(before_ref, out_ref.shape[2])
    step = min(4, images)
    for start in range(0, images, step):
        total = None
        for a_ref, w_ref in zip(acts, weights):
            term = dot(a_ref[start * pixels : (start + step) * pixels, :], w_ref[...], 1, 0)
            total = term if total is None else total + term
        out_ref[start : start + step] = total.reshape(step, pixels, total.shape[1])
        for i in range(step):
            keep = (first + start + i < info_ref[OWN_COUNT]).astype(F32)
            value = total[i * pixels : (i + 1) * pixels] * keep
            one, two = one + fold(value), two + fold(value * value)
    put_sums(sums_ref, one, two)


def expand_chunk(info, acts, weights, chunk, before, images, plan):
    pixels, cols = plan
    first, share = chunk
    count, mid, out = len(acts), acts[0].shape[1], weights[0].shape[1]
    ins = [info] + list(acts) + list(weights) + ([] if before is None else [before])
    return kernel_call(
        functools.partial(expand_kernel, first, plan, count, mid), "expand", ins,
        [((share, pixels, out), F32), sums_out(first + share == images, out)],
    )


def output_kernel(per_image, count, info_ref, *refs):
    expanded = [[v] for v in refs[:count]]
    in_ref, go_ref, sums_three_ref, par_ref, far_ref, grad_ref, sums_ref, out_ref, done_ref = refs[count:]
    average, inv_std = norm_of(sums_three_ref, pixel_count(info_ref, per_image))
    gain, bias = par_ref[0:1, :], par_ref[1:2, :]
    chans = out_ref.shape[2]

    def body(refs, at, image, sums):
        keep = (image < info_ref[OWN_COUNT]).astype(F32)
        normalized = (refs[0][at] - average) * inv_std
        summed = normalized * gain + bias + in_ref[image].astype(F32)
        logistic = sigmoid(summed)
        out_ref[image] = (summed * logistic * keep).astype(BF16)
        slope = logistic * (1.0 + summed * (1.0 - logistic))
        grad = go_ref[image].astype(F32) * (slope * keep)
        grad_ref[image] = grad
        pltpu.make_async_copy(out_ref.at[image], far_ref.at[image], done_ref.at[image]).start()
        return sums[0] + fold(grad), sums[1] + fold(grad * normalized)

    zero = jnp.zeros((8, chans), F32)
    put_sums(sums_ref, *each_image(expanded, body, (zero, zero)))
    for image in range(out_ref.shape[0]):
        pltpu.make_async_copy(out_ref.at[image], far_ref.at[image], done_ref.at[image]).wait()


def output_pass(info, expanded, field, grad_output, sums_three, params, per_image):
    return kernel_call(
        functools.partial(output_kernel, per_image, len(expanded)), "output",
        [info, *expanded, field, grad_output, sums_three, params],
        [(field.shape, BF16), (field.shape, F32), sums_out(True, field.shape[2])],
        [pltpu.VMEM(field.shape, BF16), pltpu.SemaphoreType.DMA((field.shape[0],))], far_outs=1,
    )


def at_image(refs, image):
    for ref in refs:
        if image < ref.shape[0]:
            return ref[image]
        image -= ref.shape[0]


def back_expand_kernel(first, plan, count, mid, fields, per_image, info_ref, *refs):
    pixels, cols = plan
    expanded, refs = refs[:fields], refs[fields:]
    grad_ref, sums_three_ref, grads_ref, par_ref = refs[:4]
    weights = refs[4 : 4 + count]
    out_ref, near_ref, far_ref = refs[-3:]
    total = pixel_count(info_ref, per_image)
    average, inv_std = norm_of(sums_three_ref, total)
    grads = jnp.sum(grads_ref[...], 0)
    scale = inv_std * par_ref[0:1, :]
    bias_part, gain_part = grads[0:1] / total, grads[1:2] / total * inv_std
    for i in range(out_ref.shape[0] // pixels):
        image = first + i
        value = grad_ref[image] - (bias_part + (at_image(expanded, image) - average) * gain_part)
        value = value * (scale * (image < info_ref[OWN_COUNT]).astype(F32))
        out_ref[i * pixels : (i + 1) * pixels, :] = value.astype(BF16)
    for k in range(count):
        term = dot(out_ref[...], weights[k][...], 1, 1)
        to = slice((k // 2) * mid, (k // 2 + 1) * mid)
        if k % 2 == 0:
            near_ref[:, to] = term
        else:
            far_ref[:, to] = term.astype(BF16)


def back_expand_chunk(info, grad_summed, expanded, sums_three, grads_three, params, weights, chunk, mid, plan, per_image):
    pixels, cols = plan
    count, out = len(weights), grad_summed.shape[2]
    block, half = chunk[1] * pixels, count // 2 * mid
    return kernel_call(
        functools.partial(back_expand_kernel, chunk[0], plan, count, mid, len(expanded), per_image), "back_expand",
        [info, *expanded, grad_summed, sums_three, grads_three, params, *weights],
        [((block, out), BF16), ((block, half), F32), ((block, half), BF16)],
        flops=2 * block * mid * count * out,
    )


def pair_sum_kernel(info_ref, near_ref, far_ref, own_ref, *send_refs):
    mid = own_ref.shape[1]
    for k, ref in enumerate((own_ref,) + send_refs):
        at = slice(k * mid, (k + 1) * mid)
        ref[...] = (near_ref[:, at] + far_ref[:, at].astype(F32)).astype(ref.dtype)


def pair_sum(info, near, far, mid):
    rows, half = near.shape
    return kernel_call(
        pair_sum_kernel, "pair_sum", [info, near, far],
        [((rows, mid), F32 if k == 0 else BF16) for k in range(half // mid)],
    )


def slope_two_kernel(first, plan, count, per_image, info_ref, own_ref, *refs):
    pixels, cols = plan
    arrived, refs = refs[:count], refs[count:]
    grp_ref, sums_two_ref, par_ref = refs[:3]
    before_ref = None if len(refs) == 6 else refs[3]
    out_ref, edge_ref, sums_ref = refs[-3:]
    average, inv_std = norm_of(sums_two_ref, pixel_count(info_ref, per_image))
    gain, bias = par_ref[2:3, :], par_ref[3:4, :]
    one, two = before_sums(before_ref, grp_ref.shape[2])
    for i in range(out_ref.shape[0]):
        image = first + i
        at = slice(i * pixels, (i + 1) * pixels)
        grad = own_ref[at, :]
        for ref in arrived:
            grad = grad + ref[at, :].astype(F32)
        normalized = (grp_ref[image] - average) * inv_std
        keep = (image < info_ref[OWN_COUNT]).astype(F32)
        grad = grad * (silu_slope(normalized * gain + bias) * keep)
        out_ref[i] = grad
        edge_ref[i] = edge_rows(info_ref, out_ref, i, cols).astype(BF16)
        one, two = one + fold(grad), two + fold(grad * normalized)
    put_sums(sums_ref, one, two)


def slope_two_chunk(info, own, arrived, grouped, sums_two, params, chunk, before, plan, per_image, staged):
    pixels, cols = plan
    first, share = chunk
    images, mid = grouped.shape[0], grouped.shape[2]
    ins = [info, own] + list(arrived) + [grouped, sums_two, params] + ([] if before is None else [before])
    return kernel_call(
        functools.partial(slope_two_kernel, first, plan, len(arrived), per_image), "slope_two", ins,
        [((share, pixels, mid), F32), ((share, cols, mid), BF16), sums_out(first + share == images and not staged, mid)],
    )


def conv_backward_kernel(
    per_image, group_images, d_count, red_count, info_ref, *refs
):
    d_fields, refs = list(zip(refs[:d_count], refs[d_count : 2 * d_count])), refs[2 * d_count :]
    reduced, refs = refs[:red_count], refs[red_count:]
    grp_ref, g_edge_ref, sums_two_ref, grads_two_ref, sums_one_ref, par_ref, mat_ref = refs[:7]
    out_ref, sums_ref, window_ref = refs[7:]
    images, pixels, chans = grp_ref.shape
    cols = g_edge_ref.shape[1]
    total_pixels = pixel_count(info_ref, per_image)
    avg_two, inv_two = norm_of(sums_two_ref, total_pixels)
    grads = jnp.sum(grads_two_ref[...], 0)
    bias_part, gain_part = grads[0:1] / total_pixels, grads[1:2] / total_pixels * inv_two
    scale_two = inv_two * par_ref[2:3, :]
    avg_one, inv_one = norm_of(sums_one_ref, total_pixels)
    gain_one, bias_one = par_ref[0:1, :], par_ref[1:2, :]

    def input_grad(d, grouped, keep):
        return (d - (bias_part + (grouped - avg_two) * gain_part)) * (scale_two * keep)

    def fill(image):
        keep = (image < info_ref[OWN_COUNT]).astype(F32)
        own = input_grad(at_image([f[0] for f in d_fields], image), grp_ref[image], keep)
        edge = at_image([f[1] for f in d_fields], image).astype(F32)
        edge = input_grad(edge, g_edge_ref[image].astype(F32), keep)
        fill_windows(window_ref, image, with_edges(info_ref, own, edge), cols)

    def convolve(first, one, two):
        grad = None
        for i in range(3):
            piece = window_ref[first : first + group_images, i * cols : i * cols + pixels, :]
            term = dot(piece.reshape(group_images * pixels, 3 * chans), mat_ref[i], 1, 0)
            grad = term if grad is None else grad + term
        for i in range(group_images):
            image = first + i
            keep = (image < info_ref[OWN_COUNT]).astype(F32)
            normalized = (at_image(reduced, image) - avg_one) * inv_one
            slope = silu_slope(normalized * gain_one + bias_one)
            d_one = grad[i * pixels : (i + 1) * pixels] * (slope * keep)
            out_ref[image] = d_one
            one, two = one + fold(d_one), two + fold(d_one * normalized)
        return one, two

    one = two = jnp.zeros((8, chans), F32)
    for first in range(0, images + group_images, group_images):
        for image in range(first, min(first + group_images, images)):
            fill(image)
        if first:
            one, two = convolve(first - group_images, one, two)
    put_sums(sums_ref, one, two)


def tap_grads_kernel(group, cols, step, info_ref, act_ref, window_ref, out_ref, turned_ref):
    images, pixels, chans = act_ref.shape
    for image in range(images):
        turned_ref[:, image * pixels : (image + 1) * pixels] = act_ref[image].T
    same = (
        lax.broadcasted_iota(jnp.int32, (chans, 3 * chans), 0) // group
        == lax.broadcasted_iota(jnp.int32, (chans, 3 * chans), 1) % chans // group
    )
    for i in range(3):
        total = None
        for first in range(0, images, step):
            piece = window_ref[first : first + step, i * cols : i * cols + pixels, :]
            turned = turned_ref[:, first * pixels : (first + step) * pixels]
            term = dot(turned, piece.reshape(step * pixels, 3 * chans), 1, 0)
            total = term if total is None else total + term
        total = jnp.sum(jnp.where(same, total, 0.0).reshape(chans // group, group, 3 * chans), 0)
        for j in range(3):
            out_ref[3 * (2 - i) + 2 - j] = total[:, j * chans : (j + 1) * chans]


def tap_grads(info, acts, windows, group, cols):
    images, pixels, chans = acts.shape
    return kernel_call(
        functools.partial(tap_grads_kernel, group, cols, 4), "tap_grads", [info, acts, windows], [((9, group, chans), F32)],
        [pltpu.VMEM((chans, images * pixels), BF16)],
    )[0]


def conv_backward(info, d_two, d_edges, grouped, g_edge, reduced, sums_two, grads_two, sums_one, params, matrices, per_image):
    images, pixels, chans = grouped.shape
    cols = g_edge.shape[1]
    return kernel_call(
        functools.partial(conv_backward_kernel, per_image, 4, len(d_two), len(reduced)), "conv_backward",
        [info, *d_two, *d_edges, *reduced, grouped, g_edge, sums_two, grads_two, sums_one, params, matrices],
        [(grouped.shape, F32), sums_out(True, chans), ((images, pixels + 2 * cols, 3 * chans), BF16)],
    )


def grad_reduced_kernel(per_image, count, info_ref, *refs):
    reduced = [[v] for v in refs[:count]]
    d_ref, sums_one_ref, grads_ref, par_ref, out_ref = refs[count:]
    pixels = d_ref.shape[1]
    total = pixel_count(info_ref, per_image)
    average, inv_std = norm_of(sums_one_ref, total)
    grads = jnp.sum(grads_ref[...], 0)
    bias_part, gain_part = grads[0:1] / total, grads[1:2] / total * inv_std
    scale = inv_std * par_ref[0:1, :]

    def body(refs, at, image, nothing):
        value = d_ref[image] - (bias_part + (refs[0][at] - average) * gain_part)
        value = value * (scale * (image < info_ref[OWN_COUNT]).astype(F32))
        out_ref[pl.ds(pl.multiple_of(image * pixels, pixels), pixels), :] = value.astype(BF16)
        return nothing

    each_image(reduced, body, 0)


def grad_reduced(info, d_one, reduced, sums_one, grads_one, params, per_image):
    images, pixels, mid = d_one.shape
    return kernel_call(
        functools.partial(grad_reduced_kernel, per_image, len(reduced)), "grad_reduced",
        [info, *reduced, d_one, sums_one, grads_one, params], [((images * pixels, mid), BF16)],
    )[0]


def input_grad_kernel(count, info_ref, grad_ref, *refs):
    pieces, weights, out_ref = refs[:count], refs[count : 2 * count], refs[-1]
    rows = 512

    def body(step, nothing):
        at = pl.ds(pl.multiple_of(step * rows, rows), rows)
        total = grad_ref[at, :]
        for p_ref, w_ref in zip(pieces, weights):
            total = total + dot(p_ref[at, :], w_ref[...], 1, 1)
        out_ref[at, :] = total.astype(BF16)
        return nothing

    lax.fori_loop(0, grad_ref.shape[0] // rows, body, 0)


def input_grad(info, grad_summed, pieces, weights):
    return kernel_call(
        functools.partial(input_grad_kernel, len(pieces)), "input_grad", [info, grad_summed] + list(pieces) + list(weights),
        [(grad_summed.shape, BF16)],
    )[0]


def cut_columns_kernel(info_ref, in_ref, *refs):
    for k, ref in enumerate(refs):
        part = ref.shape[1]
        ref[...] = in_ref[:, pl.ds(pl.multiple_of((info_ref[CHAN_AT] ^ k) * part, part), part)]


def cut_columns(info, value, count):
    rows, part = value.shape[0], value.shape[1] // count
    return kernel_call(cut_columns_kernel, "cut_columns", [info, value], [((rows, part), BF16)] * count)


def cut_rows_kernel(info_ref, in_ref, *refs):
    for k, ref in enumerate(refs):
        part = ref.shape[0]
        ref[...] = in_ref[pl.ds(pl.multiple_of((info_ref[CHAN_AT] ^ k) * part, part), part), :]


def cut_rows(info, value, count):
    part, cols = value.shape[0] // count, value.shape[1]
    return kernel_call(cut_rows_kernel, "cut_rows", [info, value], [((part, cols), BF16)] * count)


def sum_vectors_kernel(*refs):
    half = len(refs) // 3
    for ref, out_one, out_two in zip(refs[:half], refs[half::2], refs[half + 1 :: 2]):
        sums = jnp.sum(ref[...], 0)
        out_one[...] = sums[0:1]
        out_two[...] = sums[1:2]


def sum_vectors(values):
    outs = [((1, v.shape[2]), F32) for v in values for _ in range(2)]
    return [v.reshape(-1) for v in kernel_call(sum_vectors_kernel, "sum_vectors", list(values), outs)]


REDUCE_STEPS = (("height", 1, HEIGHT_AT), ("batch", 1, NEAR_AT), ("batch", 2, FAR_AT))
EXPAND_STEPS = (("height", 1, HEIGHT_AT), ("batch", 1, NEAR_AT), ("batch", 2, FAR_AT))


def part_of(info_ref, steps):
    number = 0
    for _, _, field in steps:
        number = number * 2 + info_ref[field]
    return number


def send_half(pair, step):
    return pair[0], permute(pair[1], step[0], step[1])


def split(at, keep_ref, send_ref, all_ref, arrived_ref):
    half = keep_ref.shape[0]
    for to, ref in ((at, keep_ref), (1 - at, send_ref)):
        value = all_ref[pl.ds(to * half, half)]
        if arrived_ref is not None:
            value = value + arrived_ref[pl.ds(to * half, half)].astype(F32)
        ref[...] = value.astype(ref.dtype)


def split_first_kernel(make, field, info_ref, *refs):
    keep_ref, send_ref, all_ref = refs[-3:]
    make(refs[:-3], all_ref)
    split(info_ref[field], keep_ref, send_ref, all_ref, None)


def split_first(info, make, step, name, ins, shape):
    half = (shape[0] // 2,) + shape[1:]
    return kernel_call(
        functools.partial(split_first_kernel, make, step[2]), name, [info] + ins, [(half, F32), (half, BF16)],
        [pltpu.VMEM(shape, F32)],
    )


def split_next_kernel(field, info_ref, keep_ref, arrived_ref, out_ref, send_ref):
    split(info_ref[field], out_ref, send_ref, keep_ref, arrived_ref)


def split_next(info, pair, step):
    half = (pair[0].shape[0] // 2,) + pair[0].shape[1:]
    return kernel_call(
        functools.partial(split_next_kernel, step[2]), "split_next", [info, *pair], [(half, F32), (half, BF16)], flops=SPLIT_COST
    )


def add_kernel(info_ref, first_ref, second_ref, out_ref):
    out_ref[...] = (first_ref[...] + second_ref[...].astype(F32)).astype(BF16)


def add_last(info, pair):
    return kernel_call(add_kernel, "add_last", [info, *pair], [(pair[0].shape, BF16)], flops=ADD_COST)[0]


def join_kernel(info_ref, *refs):
    size = refs[0].shape[0]
    for k, ref in enumerate(refs[:-1]):
        refs[-1][k * size : (k + 1) * size] = ref[...]


def join(info, *values):
    shape = (values[0].shape[0] * len(values),) + values[0].shape[1:]
    return kernel_call(join_kernel, "join", [info, *values], [(shape, BF16)], flops=STAGE_COST)[0]


def send_back(value, step):
    return value, permute(value, step[0], step[1])


def reduce_grad_make(places, spans, extra, refs, all_ref):
    grad_ref = refs[places * len(spans)]
    parts = all_ref.shape[0]
    per = parts // places
    for k in range(places):
        total = None
        for c, (first, end) in enumerate(spans):
            term = dot(refs[k * len(spans) + c][...], grad_ref[first:end, :], 0, 0)
            total = term if total is None else total + term
        size = total.shape[0] // per
        all_ref[k * per : (k + 1) * per, 0:size, :] = total.reshape(per, size, total.shape[1])
    if extra:
        more = refs[-1][...]
        more = more.reshape(-1, more.shape[2])
        room = parts * extra - more.shape[0]
        more = jnp.concatenate([more, jnp.zeros((room, more.shape[1]), F32)], 0)
        all_ref[:, size : size + extra, :] = more.reshape(parts, extra, more.shape[1])


def reduce_grad(info, inputs, grad, parts, more):
    spans = spans_of(inputs[0])
    rows, mid = len(inputs) * inputs[0][0].shape[1], grad.shape[1]
    extra = 0 if more is None else -(-more.shape[0] * more.shape[1] // (8 * parts)) * 8
    ins = [v for piece in inputs for v in piece] + [grad] + ([] if more is None else [more])
    return split_first(
        info, functools.partial(reduce_grad_make, len(inputs), tuple(spans), extra), REDUCE_STEPS[0], "reduce_grad", ins,
        (parts, rows // parts + extra, mid),
    )


def spans_of(values):
    spans, at = [], 0
    for value in values:
        spans.append((at, at + value.shape[0]))
        at += value.shape[0]
    return spans


def expand_grad_make(count, chunks, refs, all_ref):
    acts, grads = refs[: count * chunks], refs[count * chunks :]
    parts, wide, out = all_ref.shape
    size = wide // count
    for k in range(count):
        total = None
        own = acts[k * chunks : (k + 1) * chunks]
        for a_ref, (a_first, a_end) in zip(own, spans_of(own)):
            for g_ref, (g_first, g_end) in zip(grads, spans_of(grads)):
                first, end = max(a_first, g_first), min(a_end, g_end)
                if first < end:
                    term = dot(a_ref[first - a_first : end - a_first, :], g_ref[first - g_first : end - g_first, :], 0, 0)
                    total = term if total is None else total + term
        all_ref[:, k * size : (k + 1) * size, :] = total.reshape(parts, size, out)


def expand_grad(info, acts, grads, parts):
    count, mid, out = len(acts), acts[0][0].shape[1], grads[0].shape[1]
    return split_first(
        info, functools.partial(expand_grad_make, count, len(acts[0])), EXPAND_STEPS[0], "expand_grad",
        [a for piece in acts for a in piece] + list(grads), (parts, count * mid // parts, out),
    )


def cut_places_kernel(info_ref, keep_ref, arrived_ref, *refs):
    size = refs[0].shape[0]
    total = (keep_ref[0] + arrived_ref[0].astype(F32)).astype(BF16)
    for k, ref in enumerate(refs):
        ref[...] = total[k * size : (k + 1) * size, :]


def cut_places(info, pair, count):
    rows, out = pair[0].shape[1:]
    return kernel_call(cut_places_kernel, "cut_places", [info, *pair], [((rows // count, out), BF16)] * count)


def place_reduce_kernel(count, info_ref, *refs):
    out_ref, group_ref, more_ref = refs[4:]
    me, number = info_ref[CHAN_AT], part_of(info_ref, REDUCE_STEPS)
    part = out_ref.shape[0] // count
    batches = refs[0].shape[0]
    size = refs[0].shape[1]
    extra = refs[2].shape[1] - size
    for half in range(2):
        for other in range(2):
            ref = refs[2 * half + other]
            for k in range(batches):
                at = number ^ (other * batches + k)
                row = at * size
                to = (me ^ (half * (count // 2) + row // part)) * part + row % part
                out_ref[pl.ds(pl.multiple_of(to, size), size), :] = ref[k, 0:size, :].astype(F32)
                if half == 1:
                    more_ref[pl.ds(pl.multiple_of(at * extra, 8), extra), :] = ref[k, size:, :].astype(F32)
    group_ref[...] = more_ref[0 : group_ref.shape[0], :]


def place_reduce(info, halves, count, part, group_rows):
    batches, rows, mid = halves[1][0].shape
    extra = rows - halves[0][0].shape[1]
    return kernel_call(
        functools.partial(place_reduce_kernel, count), "place_reduce", [info] + [v for pair in halves for v in pair],
        [((part * count, mid), F32), ((group_rows, mid), F32)], [pltpu.VMEM((2 * batches * extra, mid), F32)],
    )


def place_expand_kernel(count, info_ref, own_ref, arrived_ref, out_ref):
    me, number = info_ref[CHAN_AT], part_of(info_ref, EXPAND_STEPS)
    batches, rows, out = own_ref.shape
    size = rows // count
    for other, ref in enumerate((own_ref, arrived_ref)):
        for k in range(batches):
            row = (number ^ (other * batches + k)) * size
            for place in range(count):
                to = pl.ds(pl.multiple_of((me ^ place) * out, out), out)
                out_ref[pl.ds(pl.multiple_of(row, size), size), to] = ref[k, place * size : (place + 1) * size, :].astype(F32)


def place_expand(info, pair, count, mid):
    out = pair[0].shape[2]
    return kernel_call(
        functools.partial(place_expand_kernel, count), "place_expand", [info] + list(pair), [((mid, out * count), F32)]
    )[0]


def plain_weight_grads(inputs, grad, acts, grad_expanded, grad_group):
    count, me = len(inputs), lax.axis_index("chan")
    part, mid = inputs[0][0].shape[1], grad.shape[1]
    grad_reduce = jnp.zeros((part * count, mid), BF16)
    grad_expand = jnp.zeros((mid, part * count), BF16)
    for k in range(count):
        block = dot(jnp.concatenate(inputs[k], 0), grad, 0, 0).astype(BF16)
        grad_reduce = lax.dynamic_update_slice(grad_reduce, block, ((me ^ k) * part, 0))
        block = dot(jnp.concatenate(acts[k], 0), jnp.concatenate(grad_expanded, 0), 0, 0).astype(BF16)
        block = swap(block, k) if k else block
        grad_expand = lax.dynamic_update_slice(grad_expand, block, (0, (me ^ k) * part))
    return [lax.psum(v, REDUCE_AXES).astype(F32) for v in (grad_reduce, grad_expand, grad_group.astype(BF16))]


def shards(
    block_input, w_reduce, w_group, w_expand, gain_one, bias_one, gain_two, bias_two,
    gain_three, bias_three, image_counts, grad_output,
):
    chan_size = lax.axis_size("chan")
    me = lax.axis_index("chan")
    height_at = lax.axis_index("height")
    images, rows, cols, out_part = block_input.shape
    mid_part, group = w_group.shape[3], w_group.shape[2]
    pixels = rows * cols
    per_image = float(pixels * lax.axis_size("height"))
    plan = (pixels, cols)
    distances = range(2, chan_size, 2)
    own_count = jnp.sum(
        jnp.where(jnp.arange(image_counts.shape[0]) == lax.axis_index("batch"), image_counts, 0)
    )
    batch_at = lax.axis_index("batch")
    info = jnp.stack(
        [
            own_count, jnp.sum(image_counts), height_at, me, jnp.where(height_at == 0, pixels - cols, 0),
            batch_at & 1, (batch_at >> 1) & 1,
        ]
    ).astype(jnp.int32)
    parts = lax.axis_size(REDUCE_AXES)
    staged = (lax.axis_size("height"), lax.axis_size("batch")) == (2, 4)

    def edge_swap(edge):
        return permute(edge, "height", 1)

    def sums_of(sums, *waits):
        return staged_sums(sums, *waits) if staged else spread_sums(sums)

    def gather(value, *waits):
        pieces = [value, swap(value, 1)]
        for k in distances:
            pieces.append(swap(value, k))
            pieces.append(swap(after(pieces[k], *waits) if waits else pieces[k], 1))
        return pieces

    field = block_input.reshape(images * pixels, out_part)
    matrices, matrices_back, mid_params, out_params = prepare(
        info, w_group, (gain_one, bias_one, gain_two, bias_two), (gain_three, bias_three)
    )
    columns = cut_columns(info, w_expand, chan_size)
    rows_back = cut_rows(info, w_reduce, chan_size)
    weights = [columns[0], swap(columns[1], 1)]
    reduce_back = [rows_back[0], swap(rows_back[1], 1)]
    inputs = []
    for first, share in cut_images(REDUCE_CHUNKS):
        source = after(field, inputs[0][0], info) if first else field
        piece = lax.slice_in_dim(source, first * pixels, (first + share) * pixels)
        inputs.append(gather(piece, mid_params, weights[1], reduce_back[1]) if first else gather(piece))
    reduced, red_edges, sums = [], [], None
    for pieces, (first, share) in zip(inputs, cut_images(REDUCE_CHUNKS)):
        red, edge, sums = reduce_chunk(info, pieces, (first, share), w_reduce, sums, images, plan, False)
        reduced.append(red)
        red_edges.append(edge_swap(edge))
    inputs = [list(chunks) for chunks in zip(*inputs)]
    weights += [swap(after(columns[k], inputs[2][-1]), k) for k in range(2, chan_size)]
    late_back = [swap(after(rows_back[k], inputs[2][-1]), k) for k in range(3, chan_size)]
    sums_one = spread_sums(sums)

    acts_one, grouped, grp_edge, sums = conv_forward(
        info, reduced, red_edges, sums_one, mid_params, matrices, per_image
    )
    sums_two = spread_sums(after(sums, *weights[2:], *late_back))

    acts = []
    for chunk in cut_images(EXPAND_CHUNKS):
        acts.append(gather(act_two_chunk(info, grouped, sums_two, mid_params, chunk, plan, per_image)))
    expanded, sums = [], None
    for pieces, chunk in zip(acts, cut_images(EXPAND_CHUNKS)):
        out, sums = expand_chunk(info, pieces, weights, chunk, sums, images, plan)
        expanded.append(out)
    acts = [list(chunks) for chunks in zip(*acts)]
    sums_three = spread_sums(sums)
    output, grad_summed, sums = output_pass(
        info, expanded, field.reshape(images, pixels, out_part), grad_output.reshape(images, pixels, out_part), sums_three,
        out_params, per_image,
    )
    grads_three = spread_sums(sums)

    grad_expanded, halves = [], []
    for chunk in cut_images(BACK_CHUNKS):
        grad, near, far = back_expand_chunk(
            info, grad_summed, expanded, sums_three, grads_three, out_params, weights, chunk, mid_part, plan, per_image
        )
        grad_expanded.append(grad)
        halves.append((near, swap(far, 1)))
    own, sent = [], []
    for near, far in halves:
        summed = pair_sum(info, near, far, mid_part)
        own.append(summed[0])
        sent.append([swap(value, k) for value, k in zip(summed[1:], distances)])
    grp_edge = edge_swap(after(grp_edge, own[0]))
    if staged:
        expand_pair = send_half(expand_grad(info, acts, grad_expanded, parts), EXPAND_STEPS[0])
    d_two, d_edges, sums, turn = [], [], None, info
    for c, chunk in enumerate(cut_images(BACK_CHUNKS)):
        if staged and c == 1:
            pair = split_next(after(info, d_two[0]), expand_pair, EXPAND_STEPS[1])
            turn = after(info, pair[0])
            expand_pair = send_half(pair, EXPAND_STEPS[1])
        grad, edge, sums = slope_two_chunk(
            turn, own[c], sent[c], grouped, sums_two, mid_params, chunk, sums, plan, per_image, staged
        )
        d_two.append(grad)
        d_edges.append(edge_swap(edge))
    if staged:
        sums = after(sums, expand_pair[1], grp_edge, d_edges[0])
    grads_two = sums_of(sums, d_edges[-1])
    turn = info
    if staged:
        pair = split_next(after(info, grads_two), expand_pair, EXPAND_STEPS[2])
        turn = after(info, pair[0])
        expand_pair = send_half(pair, EXPAND_STEPS[2])

    d_one, sums, windows = conv_backward(
        turn, d_two, d_edges, grouped, grp_edge, reduced, sums_two, grads_two, sums_one, mid_params, matrices_back, per_image
    )
    if staged:
        reduce_back.append(swap(after(rows_back[2], grads_two), 2))
    grads_one = spread_sums(sums)

    grad = grad_reduced(info, d_one, reduced, sums_one, grads_one, mid_params, per_image)
    grad_field = grad_summed.reshape(images * pixels, out_part)
    if staged:
        half = chan_size // 2
        pairs, turn = [], after(info, grad)

        def in_turn(call, *args):
            nonlocal turn
            result = call(turn, *args)
            turn = after(info, result[0] if isinstance(result, (list, tuple)) else result)
            return result

        def first_half(i):
            own = inputs[i * half : (i + 1) * half]
            pairs.append(send_half(in_turn(reduce_grad, own, grad, parts, taps if i else None), REDUCE_STEPS[0]))

        def next_half(i, step):
            pairs[i] = send_half(in_turn(split_next, pairs[i], REDUCE_STEPS[step]), REDUCE_STEPS[step])

        def last_half(i):
            pairs[i] = send_back(in_turn(add_last, pairs[i]), REDUCE_STEPS[2])

        def back_half(i, step):
            pairs[i] = send_back(in_turn(join, *pairs[i]), REDUCE_STEPS[step])

        reduce_back += late_back
        for word in LAST_PHASE:
            kind, place = word[0], word[1:]
            if kind in "ab":
                i = "ab".index(kind)
                if place == "0":
                    first_half(i)
                elif place in ("1", "2"):
                    next_half(i, int(place))
                elif place == "3":
                    last_half(i)
                else:
                    back_half(i, 5 - int(place))
            elif word == "t":
                taps = in_turn(tap_grads, acts_one, windows, group, cols)
            elif word == "c":
                places = in_turn(cut_places, expand_pair, chan_size)
                places = [v if k == 0 else swap(v, k) for k, v in enumerate(places)]
            elif word == "e0":
                back = in_turn(join, *places)
                back = send_back(back.reshape((1,) + back.shape), EXPAND_STEPS[2])
            elif kind == "e":
                back = send_back(in_turn(join, *back), EXPAND_STEPS[2 - int(place)])
            elif word == "x":
                far_grads = [swap(after(grad, turn), k) for k in distances]
            elif word == "o":
                grads = [grad, swap(after(grad, turn), 1)]
            elif word == "d":
                for value in far_grads:
                    grads += [value, swap(after(value, turn), 1)]
            elif word == "p":
                grad_expand = in_turn(place_expand, back, chan_size, mid_part)
            elif word == "i":
                grad_input = in_turn(input_grad, grad_field, grads, reduce_back)
            elif word == "wo":
                turn = after(turn, grads[1])
            elif word == "wd":
                turn = after(turn, *grads[2:])
            elif word == "wz":
                turn = after(turn, expand_pair[1])
            elif word == "wr":
                turn = after(turn, *reduce_back[2:])
            elif word == "wa":
                turn = after(turn, pairs[0][1])
            elif word == "wb":
                turn = after(turn, pairs[1][1])
            elif word == "we":
                turn = after(turn, back[1])
        grad_reduce, grad_group = place_reduce(turn, pairs, chan_size, out_part, 9 * group)
    else:
        reduce_back += [swap(rows_back[2], 2)] + late_back
        grad_input = input_grad(info, grad_field, gather(grad), reduce_back)
        grad_group = tap_grads(info, acts_one, windows, group, cols)
        grad_reduce, grad_expand, grad_group = plain_weight_grads(inputs, grad, acts, grad_expanded, grad_group)
    vectors = sum_vectors([grads_one, grads_two, grads_three])
    return (
        output.reshape(block_input.shape), grad_input.reshape(block_input.shape), grad_reduce,
        grad_group.reshape(w_group.shape), grad_expand,
        vectors[1], vectors[0], vectors[3], vectors[2], vectors[5], vectors[4],
    )


def solution(mesh):
    split = P("batch", "height", None, "chan")
    vector = P("chan")
    return jax.shard_map(
        shards,
        mesh=mesh,
        in_specs=(
            split, P(None, "chan"), P(None, None, None, "chan"), P("chan", None),
            vector, vector, vector, vector, vector, vector, P(), split,
        ),
        out_specs=(
            split, split, P(None, "chan"), P(None, None, None, "chan"), P("chan", None),
            vector, vector, vector, vector, vector, vector,
        ),
        check_vma=False,
    )
```
